32 devices in a mesh: dp: 8 (over y, x, core), seq: 4 (over z).
Axes of the slice: x: 2, y: 2, z: 4, core: 2. Of those that a mesh axis runs over, the one named last changes fastest.
Arguments:
- layer_input: bfloat16 [8, 512, 768], P('dp', 'seq')
- w_qkv: bfloat16 [768, 2304], P('dp'), may hold values from -0.21875 to 0.21875
- w_out: bfloat16 [768, 768], P('dp'), may hold values from -0.875 to 0.875
- ln1_gain: bfloat16 [768], P('dp'), may hold values from 0.5 to 1.5
- ln1_bias: bfloat16 [768], P('dp'), may hold values from -1 to 1
- w_gate_up: bfloat16 [768, 6144], P('dp'), may hold values from -0.21875 to 0.21875
- w_down: bfloat16 [3072, 768], P('dp'), may hold values from -0.15625 to 0.15625
- ln2_gain: bfloat16 [768], P('dp'), may hold values from 0.5 to 1.5
- ln2_bias: bfloat16 [768], P('dp'), may hold values from -1 to 1
- doc_starts: int32 [8, 8], P('dp'), may hold values from 0 to 511, as said below
- cotangent: bfloat16 [8, 512, 768], P('dp', 'seq'), may hold values from -6 to 6
Outputs:
- output: bfloat16 [8, 512, 768], P('dp', 'seq')
- input_grad: bfloat16 [8, 512, 768], P('dp', 'seq')
- w_qkv_grad: float32 [768, 2304], P('dp')
- w_out_grad: float32 [768, 768], P('dp')
- ln1_gain_grad: float32 [768], P('dp')
- ln1_bias_grad: float32 [768], P('dp')
- w_gate_up_grad: float32 [768, 6144], P('dp')
- w_down_grad: float32 [3072, 768], P('dp')
- ln2_gain_grad: float32 [768], P('dp')
- ln2_bias_grad: float32 [768], P('dp')
- root_means: float32 [8, 4], P('dp')
The draws below stay inside these ranges and needn't reach their ends.
Inputs may be any that keep to these rules, and one draw needn't show every extreme that they name: `doc_starts`: row b holds the first positions of the 8 documents of window b: 0 first, strictly rising, each below 512; a document runs to the next start or to the window's end. In the last window the last document begins at 511.
All inputs are finite; a program needn't handle non-finite values.
Results may differ from the reference program's by a relative error of at most 0.015.
Values may be sent and summed in bfloat16 or wider, within the bound.
No kernel may reach another device: no remote copies, remote signals or barrier semaphores. Data moves between devices by JAX's collectives and lax.ppermute only.
A program may use at most 128 MiB of HBM per device.

```python
import math
import jax
import jax.numpy as jnp
from jax import lax

D = 768
HEADS = 12
HEAD_DIM = 64
FF = 3072
NDOC = 8
LEN = 512
BATCH = 8


def draw_layer_input(key, part):
    position = jnp.arange(LEN).astype(jnp.float32) / max(LEN - 1, 1)
    base = jnp.clip(jax.random.normal(key, (BATCH, LEN, D), jnp.float32), -6.0, 6.0)
    factor = 0.6 * 3.0 ** position
    return (base * factor[None, :, None]).astype(jnp.bfloat16)


def draw_doc_starts(key, part):
    row_keys = jax.random.split(key, BATCH)

    def one_row(row_key):
        picked = jax.random.permutation(row_key, LEN - 1)[:NDOC - 1].astype(jnp.int32) + 1
        return jnp.concatenate([jnp.zeros((1,), jnp.int32), jnp.sort(picked).astype(jnp.int32)])
    starts = jax.vmap(one_row)(row_keys)
    last_row = jnp.concatenate([jnp.zeros((1,), jnp.int32), jnp.arange(LEN - NDOC + 1, LEN).astype(jnp.int32)])
    return starts.at[BATCH - 1].set(last_row)


def steps_of(rng, extent, shards, smallest, largest):
    level = 1.0
    for dim, shards_of in shards:
        steps = jax.random.uniform(jax.random.fold_in(jax.random.fold_in(rng, 6), dim), (shards_of,), jnp.float32, smallest / len(shards), largest / len(shards))
        level = level * jnp.repeat(jnp.exp(steps), extent[dim] // shards_of).reshape((-1,) + (1,) * (len(extent) - 1 - dim))
    return level


def bell_draw(rng, dims, width, most, shards=(), dtype=jnp.bfloat16):
    array = jax.random.normal(rng, dims, jnp.float32) * width
    if len(shards) > 0:
        array = steps_of(rng, dims, shards, -0.22, 0.18) * array
    return jnp.clip(array, min=-most, max=most).astype(dtype)


def setup_inputs(seed: int = 0) -> dict:
    seeds = jax.random.split(jax.random.key(seed), 12)
    layer_input = draw_layer_input(jax.random.fold_in(seeds[11], 71), 0)
    w_qkv = bell_draw(seeds[1], (D, 3 * D), D ** -0.5, 0.21875, ((0, 8),))
    w_out = bell_draw(seeds[2], (D, D), (D // 16) ** -0.5, 0.875, ((0, 8),))
    ln1_gain = jnp.clip(1.0 + 0.1 * jax.random.normal(seeds[3], (D,), jnp.float32), 0.5, 1.5).astype(jnp.bfloat16)
    ln1_bias = bell_draw(seeds[4], (D,), 0.2, 1.0, ((0, 8),))
    w_gate_up = bell_draw(seeds[5], (D, 2 * FF), D ** -0.5, 0.21875, ((0, 8),))
    w_down = bell_draw(seeds[6], (FF, D), (FF // 2) ** -0.5, 0.15625, ((0, 8),))
    ln2_gain = jnp.clip(1.0 + 0.1 * jax.random.normal(seeds[7], (D,), jnp.float32), 0.5, 1.5).astype(jnp.bfloat16)
    ln2_bias = bell_draw(seeds[8], (D,), 0.2, 1.0, ((0, 8),))
    doc_starts = draw_doc_starts(jax.random.fold_in(seeds[11], 71), 0)
    cotangent = bell_draw(seeds[10], (BATCH, LEN, D), 1.0, 6.0, ((0, 8), (1, 4)))
    return dict(layer_input=layer_input, w_qkv=w_qkv, w_out=w_out, ln1_gain=ln1_gain, ln1_bias=ln1_bias, w_gate_up=w_gate_up, w_down=w_down, ln2_gain=ln2_gain, ln2_bias=ln2_bias, doc_starts=doc_starts, cotangent=cotangent)


NORM_EPSILON = 1e-05
HIGHEST = lax.Precision.HIGHEST

@jax.custom_vjp
def low(v):
    return lax.optimization_barrier(v.astype(jnp.bfloat16)).astype(jnp.float32)

@jax.custom_vjp
def low_back(v):
    return v

def low_keep(v):
    return (low(v), None)

def low_pass(kept, grad):
    return (grad,)

def back_keep(v):
    return (v, None)

def back_low(kept, grad):
    return (low(grad),)
low.defvjp(low_keep, low_pass)
low_back.defvjp(back_keep, back_low)

def matmul(left, right):
    return jnp.dot(left, right, precision=HIGHEST, preferred_element_type=jnp.float32)

def gelu_tanh(value):
    return 0.5 * value * (1.0 + jnp.tanh(0.7978845608028654 * (value + 0.044715 * value * value * value)))

def layer_norm(summed, gain, shift):
    row_mean = lax.optimization_barrier(jnp.mean(summed, axis=-1, keepdims=True))
    centered = summed - row_mean
    variance = lax.optimization_barrier(jnp.mean(centered * centered, axis=-1, keepdims=True))
    return centered * lax.rsqrt(variance + NORM_EPSILON) * gain + shift

def doc_ids_of(start_rows):
    positions = jnp.arange(LEN).astype(jnp.int32)
    return lax.optimization_barrier(jnp.sum((start_rows[..., None, :] <= positions[:, None]).astype(jnp.int32), axis=-1))

def attend(queries, key_heads, value_heads, doc_ids):
    block_rows = min(512, LEN)
    score_scale = 1.0 / math.sqrt(HEAD_DIM)
    slopes = 2.0 ** (-8.0 * (jnp.arange(HEADS).astype(jnp.float32) + 1.0) / HEADS)
    key_pos = jnp.arange(LEN).astype(jnp.int32)

    def one_block(row_start):
        query_block = lax.dynamic_slice_in_dim(queries, row_start, block_rows, 0)
        query_docs = lax.dynamic_slice_in_dim(doc_ids, row_start, block_rows, 0)
        query_pos = row_start + jnp.arange(block_rows).astype(jnp.int32)
        distance = jnp.abs(query_pos[:, None] - key_pos[None, :]).astype(jnp.float32)
        raw_scores = jnp.einsum('qhd,khd->hqk', query_block, key_heads, precision=HIGHEST) * score_scale
        raw_scores = low_back(raw_scores - slopes[:, None, None] * distance[None])
        same_doc = query_docs[:, None] == doc_ids[None, :]
        masked = jnp.where(same_doc[None], raw_scores, -1e+30)
        row_max = lax.optimization_barrier(jnp.max(masked, axis=-1, keepdims=True))
        expon_vals = jnp.exp(masked - row_max)
        probabilities = low(expon_vals / lax.optimization_barrier(jnp.sum(expon_vals, axis=-1, keepdims=True)))
        return jnp.einsum('hqk,khd->qhd', probabilities, value_heads, precision=HIGHEST)
    block_starts = (jnp.arange(LEN // block_rows) * block_rows).astype(jnp.int32)
    blocks = lax.map(jax.checkpoint(one_block), block_starts)
    return blocks.reshape(LEN, HEADS, HEAD_DIM)

def forward(inputs, w_qkv, w_out, gain1, shift1, w_gate_up, w_down, gain2, shift2, doc_ids):
    group = inputs.shape[0]
    token_rows = inputs.reshape(group * LEN, D)
    joint = low_back(low(matmul(token_rows, w_qkv))).reshape(group, LEN, 3, HEADS, HEAD_DIM)
    attn_heads = jax.vmap(attend)(joint[:, :, 0], joint[:, :, 1], joint[:, :, 2], doc_ids)
    attn_rows = low_back(low(attn_heads.reshape(group * LEN, D)))
    branch = low_back(matmul(attn_rows, w_out))
    first_sum = token_rows + branch
    normed = low(layer_norm(first_sum, gain1, shift1))
    gate_up = low_back(matmul(normed, w_gate_up))
    hidden = low(gelu_tanh(gate_up[:, :FF]) * gate_up[:, FF:])
    feed_out = low_back(matmul(hidden, w_down))
    second = normed + feed_out
    result = layer_norm(second, gain2, shift2)

    def root_mean(value):
        return jnp.sqrt(lax.optimization_barrier(jnp.mean((value * value).reshape(group, LEN * D), axis=1)))
    stats = jnp.stack([root_mean(branch), root_mean(first_sum), root_mean(feed_out), root_mean(second)], axis=1)
    return (result, stats)

def reference(layer_input, w_qkv, w_out, ln1_gain, ln1_bias, w_gate_up, w_down, ln2_gain, ln2_bias, doc_starts, cotangent):
    weights = tuple((weight.astype(jnp.float32) for weight in (w_qkv, w_out, ln1_gain, ln1_bias, w_gate_up, w_down, ln2_gain, ln2_bias)))
    group = math.gcd(BATCH, max(1, 4096 // LEN))
    group_count = BATCH // group
    inputs = layer_input.astype(jnp.float32).reshape(group_count, group, LEN, D)
    cotangents = cotangent.astype(jnp.float32).reshape(group_count, group * LEN, D)
    start_groups = doc_starts.reshape(group_count, group, NDOC)
    zero_grads = tuple((jnp.zeros_like(weight) for weight in weights))

    def group_step(running, sliced):
        input_group, cot_group, start_group = sliced
        doc_ids = doc_ids_of(start_group)

        def apply_layer(inputs_now, *weights_now):
            return forward(inputs_now, *weights_now, doc_ids)
        result, pull_back, stats = jax.vjp(apply_layer, input_group, *weights, has_aux=True)
        gradients = pull_back(cot_group)
        running = tuple((summed + grad_now for summed, grad_now in zip(running, gradients[1:])))
        return (running, (result.astype(jnp.bfloat16), gradients[0].astype(jnp.bfloat16), stats))
    sums, (results, input_grads, stats) = lax.scan(group_step, zero_grads, (inputs, cotangents, start_groups))
    output = results.reshape(BATCH, LEN, D)
    input_grad = input_grads.reshape(BATCH, LEN, D)
    root_means = stats.reshape(BATCH, 4)
    return (output, input_grad, sums[0], sums[1], sums[2], sums[3], sums[4], sums[5], sums[6], sums[7], root_means)
```

```python
import functools
import math

import jax
import jax.numpy as jnp
import numpy as np
from jax import lax
from jax.experimental import pallas as pl
from jax.experimental.pallas import tpu as pltpu
from jax.sharding import PartitionSpec as P

HEADS = 12
HEAD_DIM = 64
NORM_EPSILON = 1e-05
GELU_C = 0.7978845608028654
GELU_A = 0.044715
INNER = 8
CHIPS = 4
SEQ = 4
PAD = 16

F32 = jnp.float32
BF16 = jnp.bfloat16
SLOPES = (2.0 ** (-8.0 * (np.arange(HEADS) + 1.0) / HEADS)).astype(np.float32)


def dot(left, right):
    return jnp.dot(left, right, preferred_element_type=F32)


def dot_nt(left, right):
    return lax.dot_general(left, right, (((1,), (1,)), ((), ())), preferred_element_type=F32)


def dot_tn(left, right):
    return lax.dot_general(left, right, (((0,), (0,)), ((), ())), preferred_element_type=F32)


def gelu_parts(value):
    square = value * value
    tanh = jnp.tanh(GELU_C * (value + GELU_A * square * value))
    half = 0.5 * (1.0 + tanh)
    slope = half + 0.5 * value * (1.0 - tanh * tanh) * (GELU_C * (1.0 + 3.0 * GELU_A * square))
    return value * half, slope


def gelu(value):
    return 0.5 * value * (1.0 + jnp.tanh(GELU_C * (value + GELU_A * value * value * value)))


def norm_parts(summed):
    centered = summed - jnp.mean(summed, axis=-1, keepdims=True)
    variance = jnp.mean(centered * centered, axis=-1, keepdims=True)
    inv_std = lax.rsqrt(variance + NORM_EPSILON)
    return centered * inv_std, inv_std


def norm_back(grad_in, normalized, inv_std, gain):
    scaled = grad_in * gain
    return inv_std * (
        scaled
        - jnp.mean(scaled, axis=-1, keepdims=True)
        - normalized * jnp.mean(scaled * normalized, axis=-1, keepdims=True)
    )


def column_sum(value):
    return jnp.sum(value, axis=0, keepdims=True)


def total(value):
    return jnp.sum(jnp.sum(value, axis=1, keepdims=True), axis=0, keepdims=True)


def at(start, size, step):
    return pl.ds(pl.multiple_of(start, step), size)


def call(kernel, outs, smem, *vmem, scratch=(), flops=0):
    specs = [pl.BlockSpec(memory_space=pltpu.SMEM) for _ in smem]
    specs += [pl.BlockSpec(memory_space=pltpu.VMEM) for _ in vmem]
    out_shape = [jax.ShapeDtypeStruct(shape, dtype) for shape, dtype in outs]
    moved = sum(math.prod(a.shape) * a.dtype.itemsize for a in list(vmem) + out_shape)
    return pl.pallas_call(
        kernel,
        out_shape=out_shape,
        in_specs=specs,
        out_specs=[pl.BlockSpec(memory_space=pltpu.VMEM) for _ in outs],
        scratch_shapes=[pltpu.VMEM(shape, dtype) for shape, dtype in scratch],
        cost_estimate=pl.CostEstimate(flops=flops, transcendentals=0, bytes_accessed=moved),
        name=kernel.__name__,
    )(*smem, *vmem)


def gather_weights(ids, *refs):
    blocks, params, downs = refs[0:8], refs[8:16], refs[16:18]
    gate_up, w_out, down, vectors = refs[18:22]
    rows = blocks[0].shape[1]
    model = w_out.shape[0]
    gathered = jnp.zeros((16, model), F32)
    for s in range(INNER):
        start = ids[s] * rows
        place = at(start, rows, 32)
        gate_up[0, place, :] = blocks[s][0]
        gate_up[1, place, :] = blocks[s][1]
        w_out[place, :] = blocks[s][2]
        piece = params[s][0, rows : rows + PAD, :].astype(F32)
        lanes = lax.broadcasted_iota(jnp.int32, piece.shape, 1)
        piece = jnp.where(lanes < rows, piece, 0.0)
        wide = jnp.concatenate([piece[:, :128], jnp.zeros((16, model - 128), F32)], axis=1)
        gathered = gathered + pltpu.roll(wide, start, 1)
    vectors[...] = gathered[0:8]
    down_rows = downs[0].shape[0]
    for s in range(2):
        down[at((ids[s] % 2) * down_rows, down_rows, 32), :] = downs[s][...]


def attention_forward(ids, starts, slopes, *refs):
    x_blocks, w_blocks = refs[0:4], refs[4:12]
    outs = refs[12:16]
    q_out, k_out, v_out, probs_out, w_qkv = refs[16:21]
    xs = refs[21]
    rows = x_blocks[0].shape[0]
    length = SEQ * rows
    shard = w_blocks[0].shape[1] - PAD
    for s in range(INNER):
        w_qkv[:, at(ids[s] * shard, shard, 32), :] = w_blocks[s][:, 0:shard, :]
    for s in range(SEQ):
        xs[s * rows : (s + 1) * rows, :] = x_blocks[s][...]
    joint = xs[...]
    q_out[...] = dot(joint, w_qkv[0]).astype(BF16)
    k_out[...] = dot(joint, w_qkv[1]).astype(BF16)
    v_out[...] = dot(joint, w_qkv[2]).astype(BF16)
    keys = k_out[...]
    values = v_out[...]
    width = keys.shape[1]
    heads = width // HEAD_DIM
    z = ids[8]

    def doc_of(position):
        count = jnp.zeros(position.shape, jnp.int32)
        for n in range(starts.shape[1]):
            count = count + (starts[0, n] <= position).astype(jnp.int32)
        return count

    lane = lax.broadcasted_iota(jnp.int32, (1, length), 1)
    key_pos = (jnp.bitwise_xor(lane // rows, z)) * rows + lane % rows
    key_docs = doc_of(key_pos)
    head_of = lax.broadcasted_iota(jnp.int32, (1, width), 1) // HEAD_DIM
    head_values = [jnp.where(head_of == h, values, jnp.zeros_like(values)) for h in range(heads)]
    for s in range(SEQ):
        query_pos = ids[8 + s] * rows + lax.broadcasted_iota(jnp.int32, (rows, 1), 0)
        distance = jnp.abs(query_pos - key_pos).astype(F32)
        same_doc = doc_of(query_pos) == key_docs
        block = q_out[s * rows : (s + 1) * rows, :] * BF16(1.0 / math.sqrt(HEAD_DIM))
        total_out = jnp.zeros((rows, width), F32)
        for h in range(heads):
            query = jnp.where(head_of == h, block, jnp.zeros_like(block))
            scores = dot_nt(query, keys) - slopes[z * heads + h] * distance
            scores = jnp.where(same_doc, scores, -1e30)
            expon = jnp.exp(scores - jnp.max(scores, axis=-1, keepdims=True))
            probs = (expon / jnp.sum(expon, axis=-1, keepdims=True)).astype(BF16)
            probs_out[h, s * rows : (s + 1) * rows, :] = probs
            total_out = total_out + dot(probs, head_values[h])
        outs[s][...] = total_out.astype(BF16)


def project_forward(ids, *refs):
    attn_blocks = refs[0:4]
    x_ref, w_out, vectors = refs[4:7]
    first_ref, normed_ref, stats_ref = refs[7:10]
    width = attn_blocks[0].shape[1]
    branch = jnp.zeros(x_ref.shape, F32)
    for s in range(SEQ):
        branch = branch + dot(attn_blocks[s][...], w_out[at(ids[8 + s] * width, width, 64), :])
    first_sum = x_ref[...].astype(F32) + branch
    normalized, _ = norm_parts(first_sum)
    first_ref[...] = first_sum
    normed_ref[...] = (normalized * vectors[0:1, :] + vectors[1:2, :]).astype(BF16)
    lane = lax.broadcasted_iota(jnp.int32, stats_ref.shape, 1)
    stats_ref[...] = jnp.where(lane == 0, total(branch * branch), 0.0) + jnp.where(
        lane == 1, total(first_sum * first_sum), 0.0
    )


def feed_forward(*refs):
    blocks, gate_up, down = refs[0:4], refs[4], refs[5]
    outs = refs[6:10]
    tokens, acc = refs[10:12]
    rows = blocks[0].shape[0]
    for s in range(CHIPS):
        tokens[s * rows : (s + 1) * rows, :] = blocks[s][...]
    normed = tokens[...]
    step = 256
    for start in range(0, down.shape[0], step):
        cols = slice(start, start + step)
        gate = dot(normed, gate_up[0, :, cols])
        up = dot(normed, gate_up[1, :, cols])
        hidden = (gelu(gate) * up).astype(BF16)
        part = dot(hidden, down[cols, :])
        if start == 0:
            acc[...] = part
        else:
            acc[...] += part
    for s in range(CHIPS):
        outs[s][...] = acc[s * rows : (s + 1) * rows, :].astype(outs[s].dtype)


def final_norm(*refs):
    parts = refs[0:4]
    normed_ref, cot_ref, vectors, stats_in = refs[4:8]
    out_ref, grad_feed_ref, grad_second_ref, sums_ref, stats_ref = refs[8:13]
    feed_out = parts[0][...]
    for s in range(1, CHIPS):
        feed_out = feed_out + parts[s][...].astype(F32)
    second = normed_ref[...].astype(F32) + feed_out
    normalized, inv_std = norm_parts(second)
    gain = vectors[2:3, :]
    out_ref[...] = (normalized * gain + vectors[3:4, :]).astype(BF16)
    grad = cot_ref[...].astype(F32)
    grad_second = norm_back(grad, normalized, inv_std, gain)
    grad_second_ref[...] = grad_second
    grad_feed_ref[...] = grad_second.astype(BF16)
    sums_ref[0:1, :] = column_sum(grad * normalized)
    sums_ref[1:2, :] = column_sum(grad)
    sums_ref[2:8, :] = jnp.zeros((6, gain.shape[1]), F32)
    lane = lax.broadcasted_iota(jnp.int32, stats_ref.shape, 1)
    stats_ref[...] = (
        stats_in[...]
        + jnp.where(lane == 2, total(feed_out * feed_out), 0.0)
        + jnp.where(lane == 3, total(second * second), 0.0)
    )


def feed_back(*refs):
    normed_blocks, grad_blocks = refs[0:4], refs[4:8]
    gate_up, down = refs[8:10]
    outs = refs[10:14]
    hidden_ref, dgate_ref, dup_ref = refs[14:17]
    tokens, grads, acc = refs[17:20]
    rows = normed_blocks[0].shape[0]
    for s in range(CHIPS):
        place = slice(s * rows, (s + 1) * rows)
        tokens[place, :] = normed_blocks[s][...]
        grads[place, :] = grad_blocks[s][...]
    normed = tokens[...]
    grad_feed = grads[...]
    step = 256
    for start in range(0, down.shape[0], step):
        cols = slice(start, start + step)
        gate = dot(normed, gate_up[0, :, cols])
        up = dot(normed, gate_up[1, :, cols])
        grad_hidden = dot_nt(grad_feed, down[cols, :])
        act, slope = gelu_parts(gate)
        hidden_ref[:, cols] = (act * up).astype(BF16)
        dgate = (grad_hidden * up * slope).astype(BF16)
        dup = (grad_hidden * act).astype(BF16)
        dgate_ref[:, cols] = dgate
        dup_ref[:, cols] = dup
        part = dot_nt(dgate, gate_up[0, :, cols]) + dot_nt(dup, gate_up[1, :, cols])
        if start == 0:
            acc[...] = part
        else:
            acc[...] += part
    for s in range(CHIPS):
        outs[s][...] = acc[s * rows : (s + 1) * rows, :].astype(outs[s].dtype)


def feed_weight_grads(ids, *refs):
    hidden_ref, dgate_ref, dup_ref = refs[0:3]
    normed_blocks, grad_blocks = refs[3:7], refs[7:11]
    normed_far, grad_far = refs[11:15], refs[15:19]
    gate_up, down = refs[19:21]
    down_keep, down_send, keep, send = refs[21:25]
    tokens, grads, down_acc, gate_acc = refs[25:29]
    rows = normed_blocks[0].shape[0]
    far = normed_far[0].shape[0]
    near = CHIPS * rows
    for s in range(CHIPS):
        place = slice(s * rows, (s + 1) * rows)
        tokens[place, :] = normed_blocks[s][...]
        grads[place, :] = grad_blocks[s][...]
        place = slice(near + s * far, near + (s + 1) * far)
        tokens[place, :] = normed_far[s][...]
        grads[place, :] = grad_far[s][...]
    step = 256
    for start in range(0, down.shape[0], step):
        cols = slice(start, start + step)
        for chunk in range(SEQ):
            place = slice(chunk * near, (chunk + 1) * near)
            normed = tokens[place, :]
            grad_feed = grads[place, :]
            if chunk == 0:
                hidden = hidden_ref[:, cols]
                dgate = dgate_ref[:, cols]
                dup = dup_ref[:, cols]
            else:
                gate = dot(normed, gate_up[0, :, cols])
                up = dot(normed, gate_up[1, :, cols])
                grad_hidden = dot_nt(grad_feed, down[cols, :])
                act, slope = gelu_parts(gate)
                hidden = (act * up).astype(BF16)
                dgate = (grad_hidden * up * slope).astype(BF16)
                dup = (grad_hidden * act).astype(BF16)
            parts = (dot_tn(hidden, grad_feed), dot_tn(normed, dgate), dot_tn(normed, dup))
            if chunk == 0:
                down_acc[cols, :] = parts[0]
                gate_acc[0, :, cols] = parts[1]
                gate_acc[1, :, cols] = parts[2]
            else:
                down_acc[cols, :] += parts[0]
                gate_acc[0, :, cols] += parts[1]
                gate_acc[1, :, cols] += parts[2]
    half = down_keep.shape[0]
    down_keep[...] = down_acc[at((ids[0] % 2) * half, half, 32), :]
    down_send[...] = down_acc[at((ids[1] % 2) * half, half, 32), :].astype(BF16)
    shard = keep.shape[2]
    for t in range(CHIPS):
        keep[t] = gate_acc[:, at(ids[2 * t] * shard, shard, 32), :]
        send[t] = gate_acc[:, at(ids[2 * t + 1] * shard, shard, 32), :].astype(BF16)


def pair_sum(*refs):
    keep, received = refs[0:2]
    for t in range(CHIPS):
        refs[2 + t][...] = (keep[t] + received[t].astype(F32)).astype(refs[2 + t].dtype)


def feed_weight_final(ids, *refs):
    blocks, down_keep, down_received = refs[0:4], refs[4], refs[5]
    out, down_out = refs[6:8]
    width = blocks[0].shape[2]
    for t in range(CHIPS):
        column = (ids[2 * t] // 2) * width
        for half in range(2):
            out[:, at(column + half * CHIPS * width, width, 128)] = blocks[t][half].astype(F32)
    down_out[...] = down_keep[...] + down_received[...].astype(F32)


def project_back(ids, *refs):
    parts = refs[0:4]
    grad_second, first_ref, vectors, w_out = refs[4:8]
    attn_blocks = refs[8:12]
    sums_in, stats_ref = refs[12:14]
    grad_first_ref = refs[14]
    grad_outs = refs[15:19]
    keep, send = refs[19:21]
    acc = refs[21]
    grad = grad_second[...] + parts[0][...]
    for s in range(1, CHIPS):
        grad = grad + parts[s][...].astype(F32)
    normalized, inv_std = norm_parts(first_ref[...])
    grad_first = norm_back(grad, normalized, inv_std, vectors[0:1, :])
    grad_first_ref[...] = grad_first
    grad_branch = grad_first.astype(BF16)
    rows = grad_branch.shape[0]
    width = attn_blocks[0].shape[1]
    high = stats_ref[...].astype(BF16)
    low = (stats_ref[...] - high.astype(F32)).astype(BF16)
    stats_rows = jnp.concatenate([high, low], axis=0)
    stats_rows = jnp.concatenate([stats_rows, jnp.zeros((PAD, width - 128), BF16)], axis=1)
    for s in range(SEQ):
        place = at(ids[8 + s] * width, width, 64)
        grad_outs[s][0:rows, :] = dot_nt(grad_branch, w_out[place, :]).astype(BF16)
        grad_outs[s][rows : rows + PAD, :] = stats_rows
        acc[place, :] = dot_tn(attn_blocks[s][...], grad_branch)
    sums = jnp.concatenate(
        [column_sum(grad * normalized), column_sum(grad), sums_in[0:2, :], sums_in[2:6, :]],
        axis=0,
    )
    sums = jnp.concatenate([sums, jnp.zeros((PAD - 8, sums.shape[1]), F32)], axis=0)
    shard = keep.shape[1] - PAD
    for t in range(CHIPS):
        keep[t, 0:shard, :] = acc[at(ids[2 * t] * shard, shard, 32), :]
        keep[t, shard : shard + PAD, :] = sums
        send[t, 0:shard, :] = acc[at(ids[2 * t + 1] * shard, shard, 32), :].astype(BF16)
        send[t, shard : shard + PAD, :] = sums.astype(BF16)


def plane_sum(*refs):
    out = refs[-1]
    acc = refs[0][...].astype(F32)
    for ref in refs[1:-1]:
        acc = acc + ref[...].astype(F32)
    out[...] = acc.astype(out.dtype)


def project_final(ids, *refs):
    blocks, out, vectors = refs[0:4], refs[4], refs[5]
    acc = blocks[0][...].astype(F32)
    for s in range(1, SEQ):
        acc = acc + blocks[s][...].astype(F32)
    shard = out.shape[0]
    out[...] = acc[0:shard, :]
    sums = acc[shard : shard + 8, :]
    shift = sums.shape[1] - ids[0] * shard
    vectors[...] = pltpu.roll(sums, lax.rem(shift, sums.shape[1]), 1)[:, 0:128]


def attention_back(ids, *refs):
    grad_blocks = refs[0:4]
    q_ref, k_ref, v_ref, probs_ref, w_qkv = refs[4:9]
    x_blocks = refs[9:13]
    outs = refs[13:17]
    keep, send = refs[17:19]
    xs, grads, grad_q, grad_k, grad_v, w_acc = refs[19:25]
    rows = x_blocks[0].shape[0]
    for s in range(SEQ):
        place = slice(s * rows, (s + 1) * rows)
        xs[place, :] = x_blocks[s][...]
        grads[place, :] = grad_blocks[s][0:rows, :]
    queries, keys, values = q_ref[...], k_ref[...], v_ref[...]
    width = keys.shape[1]
    heads = width // HEAD_DIM
    head_of = lax.broadcasted_iota(jnp.int32, (1, width), 1) // HEAD_DIM
    scale = 1.0 / math.sqrt(HEAD_DIM)
    for h in range(heads):
        mine = head_of == h
        head_keys = jnp.where(mine, keys, jnp.zeros_like(keys))
        for s in range(SEQ):
            place = slice(s * rows, (s + 1) * rows)
            grad_out = jnp.where(mine, grads[place, :], jnp.zeros((rows, width), BF16))
            query = jnp.where(mine, queries[place, :], jnp.zeros((rows, width), BF16))
            probs_low = probs_ref[h, place, :]
            probs = probs_low.astype(F32)
            grad_probs = dot_nt(grad_out, values)
            delta = jnp.sum(probs * grad_probs, axis=-1, keepdims=True)
            grad_scores = (probs * (grad_probs - delta)).astype(BF16)
            dq = dot(grad_scores, head_keys)
            dk = dot_tn(grad_scores, query)
            dv = dot_tn(probs_low, grad_out)
            if h == 0:
                grad_q[place, :] = dq
            else:
                grad_q[place, :] += dq
            if h == 0 and s == 0:
                grad_k[...] = dk
                grad_v[...] = dv
            else:
                grad_k[...] += dk
                grad_v[...] += dv
    low = (
        (grad_q[...] * scale).astype(BF16),
        (grad_k[...] * scale).astype(BF16),
        grad_v[...].astype(BF16),
    )
    grad_input = dot_nt(low[0], w_qkv[0]) + dot_nt(low[1], w_qkv[1]) + dot_nt(low[2], w_qkv[2])
    for s in range(SEQ):
        outs[s][...] = grad_input[s * rows : (s + 1) * rows, :].astype(outs[s].dtype)
    joint = xs[...]
    for part in range(3):
        w_acc[part] = dot_tn(joint, low[part])
    shard = keep.shape[2]
    for t in range(CHIPS):
        keep[t] = w_acc[:, at(ids[2 * t] * shard, shard, 32), :]
        send[t] = w_acc[:, at(ids[2 * t + 1] * shard, shard, 32), :].astype(BF16)


def input_final(*refs):
    grad_first, parts, stats_in, grad_blocks = refs[0], refs[1:5], refs[5], refs[6:9]
    out, means = refs[9:11]
    acc = grad_first[...] + parts[0][...]
    for s in range(1, SEQ):
        acc = acc + parts[s][...].astype(F32)
    out[...] = acc.astype(BF16)
    rows, model = out.shape
    stats = stats_in[...]
    for ref in grad_blocks:
        extra = ref[rows : rows + PAD, 0:128].astype(F32)
        stats = stats + (extra[0:8] + extra[8:16])
    means[...] = jnp.sqrt(stats * (1.0 / (SEQ * rows * model)))


def qkv_weight_final(ids, *refs):
    blocks, out, stage = refs[0:4], refs[4], refs[5]
    for s in range(SEQ):
        stage[ids[8 + s]] = blocks[s][...].astype(F32)
    width = blocks[0].shape[2]
    for part in range(3):
        for pos in range(SEQ):
            start = (part * SEQ + pos) * width
            out[:, start : start + width] = stage[pos, part]


def body(
    layer_input,
    w_qkv,
    w_out,
    ln1_gain,
    ln1_bias,
    w_gate_up,
    w_down,
    ln2_gain,
    ln2_bias,
    doc_starts,
    cotangent,
):
    dp = lax.axis_size("dp")
    stride = dp // INNER
    rows, model = layer_input.shape[1:]
    columns = tuple(tuple(range(g * stride, (g + 1) * stride)) for g in range(INNER))

    def gather_outer(value):
        if stride == 1:
            return value
        return lax.all_gather(value, "dp", axis=0, tiled=True, axis_index_groups=columns)

    def scatter_outer(value):
        if stride == 1:
            return value
        return lax.psum_scatter(
            value, "dp", scatter_dimension=0, tiled=True, axis_index_groups=columns
        )

    def swap(value, s):
        return lax.ppermute(value, "dp", [(i, i ^ (s * stride)) for i in range(dp)])

    def pass_seq(value, s):
        return lax.ppermute(value, "seq", [(i, i ^ s) for i in range(SEQ)])

    j = lax.axis_index("dp") // stride
    z = lax.axis_index("seq")
    chip = j // 2
    ids = jnp.concatenate(
        [
            jnp.bitwise_xor(j, jnp.arange(INNER, dtype=jnp.int32)),
            jnp.bitwise_xor(z, jnp.arange(SEQ, dtype=jnp.int32)),
        ]
    )
    slopes = jnp.asarray(SLOPES)

    w_qkv, w_out, w_gate_up, w_down = map(gather_outer, (w_qkv, w_out, w_gate_up, w_down))
    vectors = [gather_outer(v) for v in (ln1_gain, ln1_bias, ln2_gain, ln2_bias)]
    shard = w_out.shape[0]
    head_width = HEADS // SEQ * HEAD_DIM
    hidden_units = w_gate_up.shape[1] // 2
    slice_units = hidden_units // CHIPS

    x_own = layer_input[0]
    x_blocks = [x_own] + [pass_seq(x_own, s) for s in range(1, SEQ)]

    params = jnp.stack(vectors, axis=0)
    params = jnp.pad(params, ((0, PAD - 4), (0, head_width - shard)))
    heads_part = [
        lax.dynamic_slice(w_qkv, (0, part * model + z * head_width), (shard, head_width))
        for part in range(3)
    ]
    own_qkv = jnp.stack([jnp.concatenate([block, params], axis=0) for block in heads_part], axis=0)
    qkv_even = [own_qkv] + [swap(own_qkv, s) for s in (2, 4, 6)]
    qkv_odd = [swap(block, 1) for block in qkv_even]
    qkv_pieces = [block for pair in zip(qkv_even, qkv_odd) for block in pair]

    def quarter(s):
        target = jnp.bitwise_xor(chip, s // 2) * slice_units
        gate = lax.dynamic_slice(w_gate_up, (0, target), (shard, slice_units))
        up = lax.dynamic_slice(w_gate_up, (0, hidden_units + target), (shard, slice_units))
        return jnp.stack([gate, up, w_out], axis=0)

    feed_even = [quarter(0)] + [swap(quarter(s), s) for s in (2, 4, 6)]
    feed_odd = [swap(block, 1) for block in feed_even]
    feed_pieces = [block for pair in zip(feed_even, feed_odd) for block in pair]
    down_pieces = [w_down, swap(w_down, 1)]

    gate_up_full, out_full, down_full, norm_vectors = call(
        gather_weights,
        [
            ((2, model, slice_units), BF16),
            ((model, model), BF16),
            ((slice_units, model), BF16),
            ((8, model), F32),
        ],
        [ids],
        *feed_pieces,
        *qkv_pieces,
        *down_pieces,
    )

    length = SEQ * rows
    attended = call(
        attention_forward,
        [((rows, head_width), BF16)] * SEQ
        + [((length, head_width), BF16)] * 3
        + [((HEADS // SEQ, length, length), BF16), ((3, model, head_width), BF16)],
        [ids, doc_starts, slopes],
        *x_blocks,
        *qkv_pieces,
        scratch=[((length, model), BF16)],
    )
    attn_out, (queries, keys, values, probs, qkv_full) = attended[:SEQ], attended[SEQ:]
    attn_blocks = [attn_out[0]] + [pass_seq(attn_out[s], s) for s in range(1, SEQ)]

    first_sum, normed, stats1 = call(
        project_forward,
        [((rows, model), F32), ((rows, model), BF16), ((8, 128), F32)],
        [ids],
        *attn_blocks,
        x_own,
        out_full,
        norm_vectors,
    )

    def plane(value):
        return [value] + [swap(value, s) for s in (2, 4, 6)]

    def far(value):
        others = jnp.concatenate([pass_seq(value, s) for s in range(1, SEQ)], axis=0)
        return plane(others)

    normed_blocks = plane(normed)
    shares = [((rows, model), F32)] + [((rows, model), BF16)] * 3
    feed_parts = call(
        feed_forward,
        shares,
        [],
        *normed_blocks,
        gate_up_full,
        down_full,
        scratch=[((CHIPS * rows, model), BF16), ((CHIPS * rows, model), F32)],
    )
    feed_parts = [feed_parts[0]] + [swap(feed_parts[t], 2 * t) for t in range(1, CHIPS)]

    output, grad_feed, grad_second, sums2, stats2 = call(
        final_norm,
        [
            ((rows, model), BF16),
            ((rows, model), BF16),
            ((rows, model), F32),
            ((8, model), F32),
            ((8, 128), F32),
        ],
        [],
        *feed_parts,
        normed,
        cotangent[0],
        norm_vectors,
        stats1,
    )

    grad_blocks = plane(grad_feed)
    back = call(
        feed_back,
        shares + [((CHIPS * rows, slice_units), BF16)] * 3,
        [],
        *normed_blocks,
        *grad_blocks,
        gate_up_full,
        down_full,
        scratch=[((CHIPS * rows, model), BF16)] * 2 + [((CHIPS * rows, model), F32)],
    )
    back_parts, saved = back[:CHIPS], back[CHIPS:]
    back_parts = [back_parts[0]] + [swap(back_parts[t], 2 * t) for t in range(1, CHIPS)]

    projected = call(
        project_back,
        [((rows, model), F32)]
        + [((rows + PAD, head_width), BF16)] * SEQ
        + [((CHIPS, shard + PAD, model), F32), ((CHIPS, shard + PAD, model), BF16)],
        [ids],
        *back_parts,
        grad_second,
        first_sum,
        norm_vectors,
        out_full,
        *attn_blocks,
        sums2,
        stats2,
        scratch=[((model, model), F32)],
    )
    grad_first, grad_attn, (out_keep, out_send) = projected[0], projected[1:5], projected[5:7]
    grad_attn = [grad_attn[0]] + [pass_seq(grad_attn[s], s) for s in range(1, SEQ)]

    attended_back = call(
        attention_back,
        shares
        + [
            ((CHIPS, 3, shard, head_width), F32),
            ((CHIPS, 3, shard, head_width), BF16),
        ],
        [ids],
        *grad_attn,
        queries,
        keys,
        values,
        probs,
        qkv_full,
        *x_blocks,
        scratch=[((length, model), BF16), ((length, head_width), BF16)]
        + [((length, head_width), F32)] * 3
        + [((3, model, head_width), F32)],
    )
    input_parts, (qkv_keep, qkv_send) = attended_back[:4], attended_back[4:6]
    input_parts = [input_parts[0]] + [pass_seq(input_parts[s], s) for s in range(1, SEQ)]

    def reduce_plane(keep, send):
        shape = keep.shape[1:]
        pieces = call(
            pair_sum, [(shape, F32)] + [(shape, BF16)] * 3, [], keep, swap(send, 1)
        )
        return [pieces[0]] + [swap(pieces[t], 2 * t) for t in range(1, CHIPS)]

    normed_far = far(normed)
    grad_far = far(grad_feed)
    down_keep, down_send, gate_keep, gate_send = call(
        feed_weight_grads,
        [
            ((slice_units // 2, model), F32),
            ((slice_units // 2, model), BF16),
            ((CHIPS, 2, shard, slice_units), F32),
            ((CHIPS, 2, shard, slice_units), BF16),
        ],
        [ids],
        *saved,
        *normed_blocks,
        *grad_blocks,
        *normed_far,
        *grad_far,
        gate_up_full,
        down_full,
        scratch=[((length * CHIPS, model), BF16)] * 2
        + [((slice_units, model), F32), ((2, model, slice_units), F32)],
    )
    grad_gate_up_w, grad_down_w = call(
        feed_weight_final,
        [((shard, 2 * hidden_units), F32), ((slice_units // 2, model), F32)],
        [ids],
        *reduce_plane(gate_keep, gate_send),
        down_keep,
        swap(down_send, 1),
    )

    (out_share,) = call(
        plane_sum, [((shard + PAD, model), BF16)], [], *reduce_plane(out_keep, out_send)
    )
    grad_out_w, vector_grads = call(
        project_final,
        [((shard, model), F32), ((8, 128), F32)],
        [ids],
        out_share,
        *[pass_seq(out_share, s) for s in range(1, SEQ)],
    )

    (qkv_share,) = call(
        plane_sum, [((3, shard, head_width), BF16)], [], *reduce_plane(qkv_keep, qkv_send)
    )
    (grad_qkv_w,) = call(
        qkv_weight_final,
        [((shard, 3 * model), F32)],
        [ids],
        qkv_share,
        *[pass_seq(qkv_share, s) for s in range(1, SEQ)],
        scratch=[((SEQ, 3, shard, head_width), F32)],
    )

    input_grad, means = call(
        input_final,
        [((rows, model), BF16), ((8, 128), F32)],
        [],
        grad_first,
        *input_parts,
        stats2,
        *grad_attn[1:],
    )
    vector_grads = [scatter_outer(vector_grads[n, :shard]) for n in range(4)]
    return (
        output[None],
        input_grad[None],
        scatter_outer(grad_qkv_w),
        scatter_outer(grad_out_w),
        vector_grads[0],
        vector_grads[1],
        scatter_outer(grad_gate_up_w),
        scatter_outer(grad_down_w),
        vector_grads[2],
        vector_grads[3],
        means[0:1, 0:4],
    )


def solution(mesh):
    return jax.shard_map(
        body,
        mesh=mesh,
        in_specs=(
            P("dp", "seq", None),
            P("dp", None),
            P("dp", None),
            P("dp"),
            P("dp"),
            P("dp", None),
            P("dp", None),
            P("dp"),
            P("dp"),
            P("dp", None),
            P("dp", "seq", None),
        ),
        out_specs=(
            P("dp", "seq", None),
            P("dp", "seq", None),
            P("dp", None),
            P("dp", None),
            P("dp"),
            P("dp"),
            P("dp", None),
            P("dp", None),
            P("dp"),
            P("dp"),
            P("dp", None),
        ),
        check_vma=False,
    )
```

```python
import functools
import math

import jax
import jax.numpy as jnp
import numpy as np
from jax import lax
from jax.experimental import pallas as pl
from jax.experimental.pallas import tpu as pltpu
from jax.sharding import PartitionSpec as P

HEADS = 12
HEAD_DIM = 64
NORM_EPSILON = 1e-05
GELU_C = 0.7978845608028654
GELU_A = 0.044715
INNER = 8
CHIPS = 4
SEQ = 4
PAD = 16

F32 = jnp.float32
BF16 = jnp.bfloat16
SLOPES = (2.0 ** (-8.0 * (np.arange(HEADS) + 1.0) / HEADS)).astype(np.float32)


def dot(left, right):
    return jnp.dot(left, right, preferred_element_type=F32)


def dot_nt(left, right):
    return lax.dot_general(left, right, (((1,), (1,)), ((), ())), preferred_element_type=F32)


def dot_tn(left, right):
    return lax.dot_general(left, right, (((0,), (0,)), ((), ())), preferred_element_type=F32)


def gelu_parts(value):
    square = value * value
    tanh = jnp.tanh(GELU_C * (value + GELU_A * square * value))
    half = 0.5 * (1.0 + tanh)
    slope = half + 0.5 * value * (1.0 - tanh * tanh) * (GELU_C * (1.0 + 3.0 * GELU_A * square))
    return value * half, slope


def gelu(value):
    return 0.5 * value * (1.0 + jnp.tanh(GELU_C * (value + GELU_A * value * value * value)))


def norm_parts(summed):
    centered = summed - jnp.mean(summed, axis=-1, keepdims=True)
    variance = jnp.mean(centered * centered, axis=-1, keepdims=True)
    inv_std = lax.rsqrt(variance + NORM_EPSILON)
    return centered * inv_std, inv_std


def norm_back(grad_in, normalized, inv_std, gain):
    scaled = grad_in * gain
    return inv_std * (
        scaled
        - jnp.mean(scaled, axis=-1, keepdims=True)
        - normalized * jnp.mean(scaled * normalized, axis=-1, keepdims=True)
    )


def column_sum(value):
    return jnp.sum(value, axis=0, keepdims=True)


def total(value):
    return jnp.sum(jnp.sum(value, axis=1, keepdims=True), axis=0, keepdims=True)


def at(start, size, step):
    return pl.ds(pl.multiple_of(start, step), size)


def call(kernel, outs, smem, *vmem, scratch=(), flops=0, mib=8, aliases=None):
    specs = [pl.BlockSpec(memory_space=pltpu.SMEM) for _ in smem]
    specs += [pl.BlockSpec(memory_space=pltpu.VMEM) for _ in vmem]
    out_shape = [jax.ShapeDtypeStruct(shape, dtype) for shape, dtype in outs]
    moved = sum(math.prod(a.shape) * a.dtype.itemsize for a in list(vmem) + out_shape)
    return pl.pallas_call(
        kernel,
        out_shape=out_shape,
        in_specs=specs,
        out_specs=[pl.BlockSpec(memory_space=pltpu.VMEM) for _ in outs],
        scratch_shapes=[pltpu.VMEM(shape, dtype) for shape, dtype in scratch],
        input_output_aliases=aliases or {},
        cost_estimate=pl.CostEstimate(flops=flops, transcendentals=0, bytes_accessed=moved),
        name=getattr(kernel, "func", kernel).__name__,
        compiler_params=pltpu.CompilerParams(vmem_limit_bytes=mib << 20),
    )(*smem, *vmem)


def gather_out(ids, *refs):
    blocks, odd = refs[0:4], refs[4]
    w_out, vectors = refs[5:7]
    model = w_out.shape[0]
    rows = model // INNER
    size = blocks[0].shape[0]
    gathered = jnp.zeros((8, model), F32)
    for t in range(CHIPS):
        for s in range(2):
            start = ids[2 * t + s] * rows
            block = blocks[t] if s == 0 else odd.at[t * size : (t + 1) * size]
            w_out[at(start, rows, 32), :] = block[2 * rows : 3 * rows, :]
            piece = block[3 * rows : 3 * rows + PAD, :].astype(F32)
            gathered = gathered + pltpu.roll(piece, start, 1)[0:8]
    vectors[...] = gathered


def gather_feed(ids, *refs):
    blocks, odd, own_down = refs[0:4], refs[4], refs[5]
    gate_up, down = refs[6:8]
    rows = gate_up.shape[1] // INNER
    size = blocks[0].shape[0]
    for t in range(CHIPS):
        for s in range(2):
            place = at(ids[2 * t + s] * rows, rows, 32)
            block = blocks[t] if s == 0 else odd.at[t * size : (t + 1) * size]
            gate_up[0, place, :] = block[0:rows, :]
            gate_up[1, place, :] = block[rows : 2 * rows, :]
    down_rows = own_down.shape[0]
    down[at((ids[0] % 2) * down_rows, down_rows, 32), :] = own_down[...]
    down[at((ids[1] % 2) * down_rows, down_rows, 32), :] = odd[CHIPS * size :, :]


def attention_forward(ids, starts, slopes, *refs):
    x_blocks, w_blocks = refs[0:4], refs[4:12]
    outs = refs[12:16]
    q_out, k_out, v_out, probs_out, w_qkv = refs[16:21]
    xs, attended = refs[21:23]
    rows = x_blocks[0].shape[0]
    length = SEQ * rows
    model = w_qkv.shape[1]
    width = w_qkv.shape[2]
    shard = model // INNER
    for s in range(INNER):
        place = at(ids[s] * shard, shard, 32)
        for part in range(3):
            w_qkv[part, place, :] = w_blocks[s][:, part * width : (part + 1) * width]
    for s in range(SEQ):
        xs[s * rows : (s + 1) * rows, :] = x_blocks[s][...]
    joint = xs[...]
    q_out[...] = dot(joint, w_qkv[0]).astype(BF16)
    k_out[...] = dot(joint, w_qkv[1]).astype(BF16)
    v_out[...] = dot(joint, w_qkv[2]).astype(BF16)
    keys = k_out[...]
    values = v_out[...]
    heads = width // HEAD_DIM
    z = ids[8]

    def doc_of(position):
        count = jnp.zeros(position.shape, jnp.int32)
        for n in range(starts.shape[1]):
            count = count + (starts[0, n] <= position).astype(jnp.int32)
        return count

    lane = lax.broadcasted_iota(jnp.int32, (1, length), 1)
    key_pos = (jnp.bitwise_xor(lane // rows, z)) * rows + lane % rows
    key_docs = doc_of(key_pos)
    head_of = lax.broadcasted_iota(jnp.int32, (1, width), 1) // HEAD_DIM
    head_values = [jnp.where(head_of == h, values, jnp.zeros_like(values)) for h in range(heads)]

    def one_block(s, carry):
        place = at(s * rows, rows, 128)
        query_pos = ids[8 + s] * rows + lax.broadcasted_iota(jnp.int32, (rows, 1), 0)
        distance = jnp.abs(query_pos - key_pos).astype(F32)
        same_doc = doc_of(query_pos) == key_docs
        block = q_out[place, :] * BF16(1.0 / math.sqrt(HEAD_DIM))
        total_out = jnp.zeros((rows, width), F32)
        for h in range(heads):
            query = jnp.where(head_of == h, block, jnp.zeros_like(block))
            scores = dot_nt(query, keys) - slopes[z * heads + h] * distance
            scores = jnp.where(same_doc, scores, -1e30)
            expon = jnp.exp(scores - jnp.max(scores, axis=-1, keepdims=True))
            probs = (expon / jnp.sum(expon, axis=-1, keepdims=True)).astype(BF16)
            probs_out[h, place, :] = probs
            total_out = total_out + dot(probs, head_values[h])
        attended[place, :] = total_out.astype(BF16)
        return carry

    lax.fori_loop(0, SEQ, one_block, 0)
    for s in range(SEQ):
        outs[s][...] = attended[s * rows : (s + 1) * rows, :]


def project_forward(ids, *refs):
    attn_blocks = refs[0:4]
    x_ref, w_out, vectors = refs[4:7]
    first_ref, normed_ref, stats_ref = refs[7:10]
    width = attn_blocks[0].shape[1]
    branch = jnp.zeros(x_ref.shape, F32)
    for s in range(SEQ):
        branch = branch + dot(attn_blocks[s][...], w_out[at(ids[8 + s] * width, width, 64), :])
    first_sum = x_ref[...].astype(F32) + branch
    normalized, _ = norm_parts(first_sum)
    first_ref[...] = first_sum
    normed_ref[...] = (normalized * vectors[0:1, :] + vectors[1:2, :]).astype(BF16)
    lane = lax.broadcasted_iota(jnp.int32, stats_ref.shape, 1)
    stats_ref[...] = jnp.where(lane == 0, total(branch * branch), 0.0) + jnp.where(
        lane == 1, total(first_sum * first_sum), 0.0
    )


def pack_halves(pack, blocks):
    half = pack.shape[0] // 2
    pack[0:half, :] = blocks[1][0:half, :]
    pack[half:, :] = blocks[2][half:, :]


def feed_forward(*refs):
    blocks, gate_up, down = refs[0:4], refs[4], refs[5]
    outs, pack = refs[6:10], refs[10]
    tokens, acc = refs[11:13]
    rows = blocks[0].shape[0]
    pack_halves(pack, blocks)
    for s in range(CHIPS):
        tokens[s * rows : (s + 1) * rows, :] = blocks[s][...]
    normed = tokens[...]
    step = 256
    for start in range(0, down.shape[0], step):
        cols = slice(start, start + step)
        gate = dot(normed, gate_up[0, :, cols])
        up = dot(normed, gate_up[1, :, cols])
        hidden = (gelu(gate) * up).astype(BF16)
        part = dot(hidden, down[cols, :])
        if start == 0:
            acc[...] = part
        else:
            acc[...] += part
    for s in range(CHIPS):
        outs[s][...] = acc[s * rows : (s + 1) * rows, :].astype(outs[s].dtype)


def final_norm(*refs):
    parts = refs[0:4]
    normed_ref, cot_ref, vectors, stats_in = refs[4:8]
    out_ref, grad_feed_ref, grad_second_ref, sums_ref, stats_ref = refs[8:13]
    feed_out = parts[0][...]
    for s in range(1, CHIPS):
        feed_out = feed_out + parts[s][...].astype(F32)
    second = normed_ref[...].astype(F32) + feed_out
    normalized, inv_std = norm_parts(second)
    gain = vectors[2:3, :]
    out_ref[...] = (normalized * gain + vectors[3:4, :]).astype(BF16)
    grad = cot_ref[...].astype(F32)
    grad_second = norm_back(grad, normalized, inv_std, gain)
    grad_second_ref[...] = grad_second
    grad_feed_ref[...] = grad_second.astype(BF16)
    sums_ref[0:1, :] = column_sum(grad * normalized)
    sums_ref[1:2, :] = column_sum(grad)
    sums_ref[2:8, :] = jnp.zeros((6, gain.shape[1]), F32)
    lane = lax.broadcasted_iota(jnp.int32, stats_ref.shape, 1)
    stats_ref[...] = (
        stats_in[...]
        + jnp.where(lane == 2, total(feed_out * feed_out), 0.0)
        + jnp.where(lane == 3, total(second * second), 0.0)
    )


def feed_back(*refs):
    normed_blocks, grad_blocks = refs[0:4], refs[4:8]
    gate_up, down = refs[8:10]
    outs = refs[10:14]
    hidden_ref, dgate_ref, dup_ref, pack = refs[14:18]
    tokens, grads, acc = refs[18:21]
    rows = normed_blocks[0].shape[0]
    pack_halves(pack, grad_blocks)
    for s in range(CHIPS):
        place = slice(s * rows, (s + 1) * rows)
        tokens[place, :] = normed_blocks[s][...]
        grads[place, :] = grad_blocks[s][...]
    normed = tokens[...]
    grad_feed = grads[...]
    step = 256
    for start in range(0, down.shape[0], step):
        cols = slice(start, start + step)
        gate = dot(normed, gate_up[0, :, cols])
        up = dot(normed, gate_up[1, :, cols])
        grad_hidden = dot_nt(grad_feed, down[cols, :])
        act, slope = gelu_parts(gate)
        hidden_ref[:, cols] = (act * up).astype(BF16)
        dgate = (grad_hidden * up * slope).astype(BF16)
        dup = (grad_hidden * act).astype(BF16)
        dgate_ref[:, cols] = dgate
        dup_ref[:, cols] = dup
        part = dot_nt(dgate, gate_up[0, :, cols]) + dot_nt(dup, gate_up[1, :, cols])
        if start == 0:
            acc[...] = part
        else:
            acc[...] += part
    for s in range(CHIPS):
        outs[s][...] = acc[s * rows : (s + 1) * rows, :].astype(outs[s].dtype)


def add_tokens(normed, grad_feed, gate_up, down, cols, accs):
    gate = dot(normed, gate_up[0, :, cols])
    up = dot(normed, gate_up[1, :, cols])
    grad_hidden = dot_nt(grad_feed, down[cols, :])
    act, slope = gelu_parts(gate)
    hidden = (act * up).astype(BF16)
    dgate = (grad_hidden * up * slope).astype(BF16)
    dup = (grad_hidden * act).astype(BF16)
    down_acc, gate_acc = accs
    down_acc[...] += dot_tn(hidden, grad_feed)
    gate_acc[0] += dot_tn(normed, dgate)
    gate_acc[1] += dot_tn(normed, dup)


def weight_grads_near(*refs):
    hidden_ref, dgate_ref, dup_ref = refs[0:3]
    normed_blocks, grad_blocks = refs[3:7], refs[7:11]
    accs = (refs[11:13], refs[13:15])
    tokens, grads = refs[15:17]
    rows = normed_blocks[0].shape[0]
    for s in range(CHIPS):
        place = slice(s * rows, (s + 1) * rows)
        tokens[place, :] = normed_blocks[s][...]
        grads[place, :] = grad_blocks[s][...]
    units = hidden_ref.shape[1] // 2
    for half in range(2):
        cols = slice(half * units, (half + 1) * units)
        down_acc, gate_acc = accs[half]
        down_acc[...] = dot_tn(hidden_ref[:, cols], grads[...])
        gate_acc[0] = dot_tn(tokens[...], dgate_ref[:, cols])
        gate_acc[1] = dot_tn(tokens[...], dup_ref[:, cols])


def weight_grads_far(*refs):
    normed_blocks, grad_blocks = refs[0:3], refs[3:6]
    gate_up, down = refs[6:8]
    accs_in = (refs[8:10], refs[10:12])
    accs = (refs[12:14], refs[14:16])
    tokens, grads = refs[16:18]
    rows = normed_blocks[0].shape[0]
    for s in range(3):
        place = slice(s * rows, (s + 1) * rows)
        tokens[place, :] = normed_blocks[s][...]
        grads[place, :] = grad_blocks[s][...]
    units = down.shape[0] // 2
    for half in range(2):
        accs[half][0][...] = accs_in[half][0][...]
        accs[half][1][...] = accs_in[half][1][...]
        cols = slice(half * units, (half + 1) * units)
        add_tokens(tokens[...], grads[...], gate_up, down, cols, accs[half])


def weight_grads_last(half, ids, *refs):
    normed_blocks, grad_blocks = refs[0:2], refs[2:4]
    gate_up, down = refs[4:6]
    accs_in = refs[6:8]
    down_out, keep, send = refs[8:11]
    accs = refs[11:13]
    units = down.shape[0] // 2
    cols = slice(half * units, (half + 1) * units)
    accs[0][...] = accs_in[0][...]
    accs[1][...] = accs_in[1][...]
    for normed_ref, grad_ref in zip(normed_blocks, grad_blocks):
        add_tokens(normed_ref[...], grad_ref[...], gate_up, down, cols, accs)
    down_out[...] = accs[0][...]
    shard = keep.shape[2]
    for t in range(CHIPS):
        keep[t] = accs[1][:, at(ids[2 * t] * shard, shard, 32), :]
        send[t] = accs[1][:, at(ids[2 * t + 1] * shard, shard, 32), :].astype(BF16)


weight_grads_first_half = functools.partial(weight_grads_last, 0)
weight_grads_second_half = functools.partial(weight_grads_last, 1)


def pair_sum(*refs):
    keep, received = refs[0:2]
    for t in range(CHIPS):
        refs[2 + t][...] = (keep[t] + received[t].astype(F32)).astype(refs[2 + t].dtype)


def feed_weight_final(ids, *refs):
    blocks, down_keep, down_received = (refs[0:4], refs[4:8]), refs[8], refs[9]
    out, down_out = refs[10:12]
    units = blocks[0][0].shape[2]
    for side in range(2):
        for t in range(CHIPS):
            column = (2 * (ids[2 * t] // 2) + side) * units
            for half in range(2):
                place = at(column + half * INNER * units, units, 128)
                out[:, place] = blocks[side][t][half].astype(F32)
    down_out[...] = down_keep[...] + down_received[...].astype(F32)


def project_back(ids, *refs):
    parts = refs[0:4]
    grad_second, first_ref, vectors, w_out = refs[4:8]
    attn_blocks = refs[8:12]
    sums_in, stats_ref = refs[12:14]
    grad_first_ref = refs[14]
    grad_outs = refs[15:19]
    keep, send = refs[19:21]
    acc = refs[21]
    grad = grad_second[...] + parts[0][...]
    for s in range(1, CHIPS):
        grad = grad + parts[s][...].astype(F32)
    normalized, inv_std = norm_parts(first_ref[...])
    grad_first = norm_back(grad, normalized, inv_std, vectors[0:1, :])
    grad_first_ref[...] = grad_first
    grad_branch = grad_first.astype(BF16)
    rows = grad_branch.shape[0]
    width = attn_blocks[0].shape[1]
    high = stats_ref[...].astype(BF16)
    low = (stats_ref[...] - high.astype(F32)).astype(BF16)
    stats_rows = jnp.concatenate([high, low], axis=0)
    stats_rows = jnp.concatenate([stats_rows, jnp.zeros((PAD, width - 128), BF16)], axis=1)
    for s in range(SEQ):
        place = at(ids[8 + s] * width, width, 64)
        grad_outs[s][0:rows, :] = dot_nt(grad_branch, w_out[place, :]).astype(BF16)
        grad_outs[s][rows : rows + PAD, :] = stats_rows
        acc[place, :] = dot_tn(attn_blocks[s][...], grad_branch)
    sums = jnp.concatenate(
        [column_sum(grad * normalized), column_sum(grad), sums_in[0:2, :], sums_in[2:6, :]],
        axis=0,
    )
    sums = jnp.concatenate([sums, jnp.zeros((PAD - 8, sums.shape[1]), F32)], axis=0)
    shard = keep.shape[1] - PAD
    for t in range(CHIPS):
        keep[t, 0:shard, :] = acc[at(ids[2 * t] * shard, shard, 32), :]
        keep[t, shard : shard + PAD, :] = sums
        send[t, 0:shard, :] = acc[at(ids[2 * t + 1] * shard, shard, 32), :].astype(BF16)
        send[t, shard : shard + PAD, :] = sums.astype(BF16)


def plane_sum(*refs):
    out = refs[-1]
    acc = refs[0][...].astype(F32)
    for ref in refs[1:-1]:
        acc = acc + ref[...].astype(F32)
    out[...] = acc.astype(out.dtype)


def project_final(ids, *refs):
    blocks, out, vectors = refs[0:4], refs[4], refs[5]
    acc = blocks[0][...].astype(F32)
    for s in range(1, SEQ):
        acc = acc + blocks[s][...].astype(F32)
    shard = out.shape[0]
    out[...] = acc[0:shard, :]
    sums = acc[shard : shard + 8, :]
    shift = sums.shape[1] - ids[0] * shard
    vectors[...] = pltpu.roll(sums, lax.rem(shift, sums.shape[1]), 1)[:, 0:128]


def attention_back(ids, *refs):
    grad_blocks = refs[0:4]
    q_ref, k_ref, v_ref, probs_ref, w_qkv = refs[4:9]
    x_blocks = refs[9:13]
    outs = refs[13:17]
    keep, send = refs[17:19]
    xs, grads, grad_q, grad_k, grad_v, w_acc = refs[19:25]
    rows = x_blocks[0].shape[0]
    for s in range(SEQ):
        place = slice(s * rows, (s + 1) * rows)
        xs[place, :] = x_blocks[s][...]
        grads[place, :] = grad_blocks[s][0:rows, :]
    queries, keys, values = q_ref[...], k_ref[...], v_ref[...]
    width = keys.shape[1]
    heads = width // HEAD_DIM
    head_of = lax.broadcasted_iota(jnp.int32, (1, width), 1) // HEAD_DIM
    scale = 1.0 / math.sqrt(HEAD_DIM)
    for h in range(heads):
        mine = head_of == h
        head_keys = jnp.where(mine, keys, jnp.zeros_like(keys))
        for s in range(SEQ):
            place = slice(s * rows, (s + 1) * rows)
            grad_out = jnp.where(mine, grads[place, :], jnp.zeros((rows, width), BF16))
            query = jnp.where(mine, queries[place, :], jnp.zeros((rows, width), BF16))
            probs_low = probs_ref[h, place, :]
            probs = probs_low.astype(F32)
            grad_probs = dot_nt(grad_out, values)
            delta = jnp.sum(probs * grad_probs, axis=-1, keepdims=True)
            grad_scores = (probs * (grad_probs - delta)).astype(BF16)
            dq = dot(grad_scores, head_keys)
            dk = dot_tn(grad_scores, query)
            dv = dot_tn(probs_low, grad_out)
            if h == 0:
                grad_q[place, :] = dq
            else:
                grad_q[place, :] += dq
            if h == 0 and s == 0:
                grad_k[...] = dk
                grad_v[...] = dv
            else:
                grad_k[...] += dk
                grad_v[...] += dv
    low = (
        (grad_q[...] * scale).astype(BF16),
        (grad_k[...] * scale).astype(BF16),
        grad_v[...].astype(BF16),
    )
    grad_input = dot_nt(low[0], w_qkv[0]) + dot_nt(low[1], w_qkv[1]) + dot_nt(low[2], w_qkv[2])
    for s in range(SEQ):
        outs[s][...] = grad_input[s * rows : (s + 1) * rows, :].astype(outs[s].dtype)
    joint = xs[...]
    for part in range(3):
        w_acc[part] = dot_tn(joint, low[part])
    shard = keep.shape[2]
    for t in range(CHIPS):
        keep[t] = w_acc[:, at(ids[2 * t] * shard, shard, 32), :]
        send[t] = w_acc[:, at(ids[2 * t + 1] * shard, shard, 32), :].astype(BF16)


def input_final(*refs):
    grad_first, parts, stats_in, grad_blocks = refs[0], refs[1:5], refs[5], refs[6:9]
    out, means = refs[9:11]
    acc = grad_first[...] + parts[0][...]
    for s in range(1, SEQ):
        acc = acc + parts[s][...].astype(F32)
    out[...] = acc.astype(BF16)
    rows, model = out.shape
    stats = stats_in[...]
    for ref in grad_blocks:
        extra = ref[rows : rows + PAD, 0:128].astype(F32)
        stats = stats + (extra[0:8] + extra[8:16])
    means[...] = jnp.sqrt(stats * (1.0 / (SEQ * rows * model)))


def qkv_weight_final(ids, *refs):
    blocks, out, stage = refs[0:4], refs[4], refs[5]
    for s in range(SEQ):
        stage[ids[8 + s]] = blocks[s][...].astype(F32)
    width = blocks[0].shape[2]
    for part in range(3):
        for pos in range(SEQ):
            start = (part * SEQ + pos) * width
            out[:, start : start + width] = stage[pos, part]


def after(values, *deps):
    return lax.optimization_barrier((values, deps))[0]


def body(
    layer_input,
    w_qkv,
    w_out,
    ln1_gain,
    ln1_bias,
    w_gate_up,
    w_down,
    ln2_gain,
    ln2_bias,
    doc_starts,
    cotangent,
):
    dp = lax.axis_size("dp")
    stride = dp // INNER
    rows, model = layer_input.shape[1:]
    columns = tuple(tuple(range(g * stride, (g + 1) * stride)) for g in range(INNER))
    cores = tuple(
        tuple((2 * t + core) * stride + r for t in range(CHIPS))
        for core in range(2)
        for r in range(stride)
    )

    def gather_outer(value):
        if stride == 1:
            return value
        return lax.all_gather(value, "dp", axis=0, tiled=True, axis_index_groups=columns)

    def scatter_outer(value):
        if stride == 1:
            return value
        return lax.psum_scatter(
            value, "dp", scatter_dimension=0, tiled=True, axis_index_groups=columns
        )

    def swap(value, s):
        return lax.ppermute(value, "dp", [(i, i ^ (s * stride)) for i in range(dp)])

    def pass_seq(value, s):
        return lax.ppermute(value, "seq", [(i, i ^ s) for i in range(SEQ)])

    j = lax.axis_index("dp") // stride
    z = lax.axis_index("seq")
    chip = j // 2
    ids = jnp.concatenate(
        [
            jnp.bitwise_xor(j, jnp.arange(INNER, dtype=jnp.int32)),
            jnp.bitwise_xor(z, jnp.arange(SEQ, dtype=jnp.int32)),
        ]
    )
    slopes = jnp.asarray(SLOPES)

    w_qkv, w_out, w_gate_up, w_down = map(gather_outer, (w_qkv, w_out, w_gate_up, w_down))
    vectors = [gather_outer(v) for v in (ln1_gain, ln1_bias, ln2_gain, ln2_bias)]
    shard = w_out.shape[0]
    head_width = HEADS // SEQ * HEAD_DIM
    hidden_units = w_gate_up.shape[1] // 2
    slice_units = hidden_units // CHIPS

    x_own = layer_input[0]
    x_blocks = [x_own] + [pass_seq(x_own, s) for s in range(1, SEQ)]

    own_qkv = jnp.concatenate(
        [
            lax.dynamic_slice(w_qkv, (0, part * model + z * head_width), (shard, head_width))
            for part in range(3)
        ],
        axis=1,
    )
    qkv_even = [own_qkv] + [swap(own_qkv, s) for s in (2, 4, 6)]
    qkv_odd = [swap(block, 1) for block in qkv_even]
    qkv_pieces = [block for pair in zip(qkv_even, qkv_odd) for block in pair]

    params = jnp.pad(jnp.stack(vectors, axis=0), ((0, PAD - 4), (0, model - shard)))
    w_gate_up, w_out = after((w_gate_up, w_out), qkv_even, x_blocks[1])

    def quarter(s):
        target = jnp.bitwise_xor(chip, s // 2) * slice_units
        gate = lax.dynamic_slice(w_gate_up, (0, target), (shard, slice_units))
        up = lax.dynamic_slice(w_gate_up, (0, hidden_units + target), (shard, slice_units))
        return jnp.concatenate([gate, up, w_out, params], axis=0)

    feed_even = [quarter(0)] + [swap(quarter(s), s) for s in (2, 4, 6)]

    length = SEQ * rows
    attended = call(
        attention_forward,
        [((rows, head_width), BF16)] * SEQ
        + [((length, head_width), BF16)] * 3
        + [((HEADS // SEQ, length, length), BF16), ((3, model, head_width), BF16)],
        [ids, doc_starts, slopes],
        *x_blocks,
        *qkv_pieces,
        scratch=[((length, model), BF16), ((length, head_width), BF16)],
        mib=16,
        flops=2 * length * head_width * (3 * model + 2 * length),
    )
    attn_out, (queries, keys, values, probs, qkv_full) = attended[:SEQ], attended[SEQ:]
    attn_blocks = [attn_out[0]] + [pass_seq(attn_out[s], s) for s in range(1, SEQ)]

    feed_even, w_down = after((feed_even, w_down), attn_out[0])
    feed_odd = swap(jnp.concatenate(feed_even + [w_down], axis=0), 1)
    out_full, norm_vectors = call(
        gather_out,
        [((model, model), BF16), ((8, model), F32)],
        [ids],
        *feed_even,
        feed_odd,
        mib=12,
    )

    first_sum, normed, stats1 = call(
        project_forward,
        [((rows, model), F32), ((rows, model), BF16), ((8, 128), F32)],
        [ids],
        *attn_blocks,
        x_own,
        out_full,
        norm_vectors,
        mib=6,
        flops=2 * rows * model * model,
    )

    def plane(value):
        return [value] + [swap(value, s) for s in (2, 4, 6)]

    def far(value):
        return [pass_seq(value, s) for s in range(1, SEQ)]

    half = rows // 2

    def cross(owns, packs, *deps):
        first = jnp.concatenate([part[:half] for pair in zip(owns, packs) for part in pair])
        last = jnp.concatenate([part[half:] for pair in zip(owns, packs) for part in pair])
        first, last = after((first, last), *deps)
        return [swap(first, 4), swap(last, 2)]

    normed_blocks = plane(normed)
    normed_far = far(normed)
    gate_up_full, down_full = call(
        gather_feed,
        [((2, model, slice_units), BF16), ((slice_units, model), BF16)],
        [ids],
        *after(feed_even + [feed_odd, w_down], normed),
        mib=12,
    )
    shares = [((rows, model), F32)] + [((rows, model), BF16)] * 3
    *feed_parts, normed_pack = call(
        feed_forward,
        shares + [((rows, model), BF16)],
        [],
        *normed_blocks,
        gate_up_full,
        down_full,
        scratch=[((CHIPS * rows, model), BF16), ((CHIPS * rows, model), F32)],
        mib=14,
        flops=6 * CHIPS * rows * model * slice_units,
    )
    feed_parts = [feed_parts[0]] + [swap(feed_parts[t], 2 * t) for t in range(1, CHIPS)]
    normed_packs = far(normed_pack)

    output, grad_feed, grad_second, sums2, stats2 = call(
        final_norm,
        [
            ((rows, model), BF16),
            ((rows, model), BF16),
            ((rows, model), F32),
            ((8, model), F32),
            ((8, 128), F32),
        ],
        [],
        *feed_parts,
        after(normed, normed_far),
        cotangent[0],
        norm_vectors,
        stats1,
    )

    grad_blocks = plane(grad_feed)
    grad_far = far(grad_feed)
    back = call(
        feed_back,
        shares + [((CHIPS * rows, slice_units), BF16)] * 3 + [((rows, model), BF16)],
        [],
        *after(normed_blocks, normed_packs),
        *grad_blocks,
        gate_up_full,
        down_full,
        scratch=[((CHIPS * rows, model), BF16)] * 2 + [((CHIPS * rows, model), F32)],
        mib=20,
        flops=10 * CHIPS * rows * model * slice_units,
    )
    back_parts, saved, grad_pack = back[:CHIPS], back[CHIPS:-1], back[-1]
    grad_packs = far(grad_pack)
    back_parts = [back_parts[0]] + [swap(back_parts[t], 2 * t) for t in range(1, CHIPS)]
    units = slice_units // 2
    acc_shapes = [((units, model), F32), ((2, model, units), F32)] * 2
    token_scratch = [((CHIPS * rows, model), BF16)] * 2
    accs = call(
        weight_grads_near,
        acc_shapes,
        [],
        *saved,
        *normed_blocks,
        *grad_blocks,
        scratch=token_scratch,
        mib=20,
    )
    grad_second, accs = after((grad_second, accs))

    def add_far(normeds, grads, accs):
        return call(
            weight_grads_far,
            acc_shapes,
            [],
            *normeds,
            *grads,
            gate_up_full,
            down_full,
            *accs,
            scratch=[((3 * rows, model), BF16)] * 2,
            mib=28,
            aliases={8: 0, 9: 1, 10: 2, 11: 3},
        )


    projected = call(
        project_back,
        [((rows, model), F32)]
        + [((rows + PAD, head_width), BF16)] * SEQ
        + [((CHIPS, shard + PAD, model), F32), ((CHIPS, shard + PAD, model), BF16)],
        [ids],
        *back_parts,
        after(grad_second, grad_far),
        first_sum,
        norm_vectors,
        out_full,
        *attn_blocks,
        sums2,
        stats2,
        scratch=[((model, model), F32)],
        mib=14,
        flops=4 * rows * model * model,
    )
    grad_first, grad_attn, (out_keep, out_send) = projected[0], projected[1:5], projected[5:7]
    normed_cross = cross(normed_far, normed_packs, grad_attn[0])
    grad_cross = cross(grad_far, grad_packs, grad_attn[0])
    accs = add_far(normed_far, grad_far, after(accs, grad_attn[0]))
    grad_attn = [grad_attn[0]] + [pass_seq(grad_attn[s], s) for s in range(1, SEQ)]

    attended_back = call(
        attention_back,
        shares
        + [
            ((CHIPS, 3, shard, head_width), F32),
            ((CHIPS, 3, shard, head_width), BF16),
        ],
        [ids],
        *grad_attn,
        after(queries, accs[0]),
        keys,
        values,
        probs,
        qkv_full,
        *x_blocks,
        scratch=[((length, model), BF16), ((length, head_width), BF16)]
        + [((length, head_width), F32)] * 3
        + [((3, model, head_width), F32)],
        mib=18,
        flops=2 * length * head_width * (6 * model + 5 * length),
    )
    input_parts, (qkv_keep, qkv_send) = attended_back[:4], attended_back[4:6]
    input_parts = [input_parts[0]] + [pass_seq(input_parts[s], s) for s in range(1, SEQ)]

    def pair(keep, send):
        shape = keep.shape[1:]
        return call(pair_sum, [(shape, F32)] + [(shape, BF16)] * 3, [], keep, swap(send, 1))

    def reduce_plane(pieces):
        return [pieces[0]] + [swap(pieces[t], 2 * t) for t in range(1, CHIPS)]

    out_pieces = pair(out_keep, out_send)
    qkv_pieces = pair(qkv_keep, qkv_send)
    (out_share,) = call(plane_sum, [((shard + PAD, model), BF16)], [], *reduce_plane(out_pieces))
    grad_out_w, vector_grads = call(
        project_final,
        [((shard, model), F32), ((8, 128), F32)],
        [ids],
        out_share,
        *[pass_seq(out_share, s) for s in range(1, SEQ)],
    )

    (qkv_share,) = call(
        plane_sum, [((3, shard, head_width), BF16)], [], *reduce_plane(qkv_pieces)
    )
    (grad_qkv_w,) = call(
        qkv_weight_final,
        [((shard, 3 * model), F32)],
        [ids],
        qkv_share,
        *[pass_seq(qkv_share, s) for s in range(1, SEQ)],
        scratch=[((SEQ, 3, shard, head_width), F32)],
    )

    accs = add_far(normed_packs, grad_packs, after(accs, qkv_pieces[0]))

    def last_half(kernel, accs):
        return call(
            kernel,
            [
                ((units, model), F32),
                ((CHIPS, 2, shard, units), F32),
                ((CHIPS, 2, shard, units), BF16),
            ],
            [ids],
            *normed_cross,
            *grad_cross,
            gate_up_full,
            down_full,
            *accs,
            scratch=acc_shapes[:2],
            mib=28,
        )

    down_first, gate_keep, gate_send = last_half(weight_grads_first_half, accs[:2])
    first = reduce_plane(pair(gate_keep, gate_send))
    second_accs = after(accs[2:], gate_send)
    down_second, gate_keep, gate_send = last_half(weight_grads_second_half, second_accs)
    mine_first = j % 2 == 0
    down_send = jnp.where(mine_first, down_second, down_first).astype(BF16)
    down_keep = jnp.where(mine_first, down_first, down_second)
    second = reduce_plane(pair(gate_keep, gate_send))
    grad_gate_up_w, grad_down_w = call(
        feed_weight_final,
        [((shard, 2 * hidden_units), F32), ((units, model), F32)],
        [ids],
        *first,
        *second,
        down_keep,
        swap(down_send, 1),
    )

    input_grad, means = call(
        input_final,
        [((rows, model), BF16), ((8, 128), F32)],
        [],
        grad_first,
        *input_parts,
        stats2,
        *grad_attn[1:],
    )
    vector_grads = [scatter_outer(vector_grads[n, :shard]) for n in range(4)]
    return (
        output[None],
        input_grad[None],
        scatter_outer(grad_qkv_w),
        scatter_outer(grad_out_w),
        vector_grads[0],
        vector_grads[1],
        scatter_outer(grad_gate_up_w),
        scatter_outer(grad_down_w),
        vector_grads[2],
        vector_grads[3],
        means[0:1, 0:4],
    )


def solution(mesh):
    return jax.shard_map(
        body,
        mesh=mesh,
        in_specs=(
            P("dp", "seq", None),
            P("dp", None),
            P("dp", None),
            P("dp"),
            P("dp"),
            P("dp", None),
            P("dp", None),
            P("dp"),
            P("dp"),
            P("dp", None),
            P("dp", "seq", None),
        ),
        out_specs=(
            P("dp", "seq", None),
            P("dp", "seq", None),
            P("dp", None),
            P("dp", None),
            P("dp"),
            P("dp"),
            P("dp", None),
            P("dp", None),
            P("dp"),
            P("dp"),
            P("dp", None),
        ),
        check_vma=False,
    )
```

```python
import math

import jax
import jax.numpy as jnp
import numpy as np
from jax import lax
from jax.experimental import pallas as pl
from jax.experimental.pallas import tpu as pltpu
from jax.sharding import PartitionSpec as P

HEADS = 12
HEAD_DIM = 64
NORM_EPSILON = 1e-05
GELU_C = 0.7978845608028654
GELU_A = 0.044715
INNER = 8
CHIPS = 4
SEQ = 4
PAD = 16

F32 = jnp.float32
BF16 = jnp.bfloat16
SLOPES = (2.0 ** (-8.0 * (np.arange(HEADS) + 1.0) / HEADS)).astype(np.float32)


def dot(left, right):
    return jnp.dot(left, right, preferred_element_type=F32)


def dot_nt(left, right):
    return lax.dot_general(left, right, (((1,), (1,)), ((), ())), preferred_element_type=F32)


def dot_tn(left, right):
    return lax.dot_general(left, right, (((0,), (0,)), ((), ())), preferred_element_type=F32)


def gelu_parts(value):
    square = value * value
    tanh = jnp.tanh(GELU_C * (value + GELU_A * square * value))
    half = 0.5 * (1.0 + tanh)
    slope = half + 0.5 * value * (1.0 - tanh * tanh) * (GELU_C * (1.0 + 3.0 * GELU_A * square))
    return value * half, slope


def gelu(value):
    return 0.5 * value * (1.0 + jnp.tanh(GELU_C * (value + GELU_A * value * value * value)))


def norm_parts(summed):
    centered = summed - jnp.mean(summed, axis=-1, keepdims=True)
    variance = jnp.mean(centered * centered, axis=-1, keepdims=True)
    inv_std = lax.rsqrt(variance + NORM_EPSILON)
    return centered * inv_std, inv_std


def norm_back(grad_in, normalized, inv_std, gain):
    scaled = grad_in * gain
    return inv_std * (
        scaled
        - jnp.mean(scaled, axis=-1, keepdims=True)
        - normalized * jnp.mean(scaled * normalized, axis=-1, keepdims=True)
    )


def column_sum(value):
    return jnp.sum(value, axis=0, keepdims=True)


def total(value):
    return jnp.sum(jnp.sum(value, axis=1, keepdims=True), axis=0, keepdims=True)


def at(start, size, step):
    return pl.ds(pl.multiple_of(start, step), size)


def call(kernel, outs, smem, *vmem, scratch=(), flops=0, mib=8, aliases=None):
    specs = [pl.BlockSpec(memory_space=pltpu.SMEM) for _ in smem]
    specs += [pl.BlockSpec(memory_space=pltpu.VMEM) for _ in vmem]
    out_shape = [jax.ShapeDtypeStruct(shape, dtype) for shape, dtype in outs]
    moved = sum(math.prod(a.shape) * a.dtype.itemsize for a in list(vmem) + out_shape)
    return pl.pallas_call(
        kernel,
        out_shape=out_shape,
        in_specs=specs,
        out_specs=[pl.BlockSpec(memory_space=pltpu.VMEM) for _ in outs],
        scratch_shapes=[pltpu.VMEM(shape, dtype) for shape, dtype in scratch],
        input_output_aliases=aliases or {},
        cost_estimate=pl.CostEstimate(flops=flops, transcendentals=0, bytes_accessed=moved),
        name=kernel.__name__,
        compiler_params=pltpu.CompilerParams(vmem_limit_bytes=mib << 20),
    )(*smem, *vmem)


def select_units(ids, gate_up, down, w_out, params, piece):
    z = ids[8]
    rows = w_out.shape[0]
    window = down.shape[0]
    units = window // SEQ
    model = w_out.shape[1]
    hidden = gate_up.shape[1] // 2
    group = lax.broadcasted_iota(jnp.int32, (rows, window), 1) // units
    for g in range(2):
        for w in range(model // window):
            acc = jnp.zeros((rows, window), F32)
            for i in range(SEQ):
                start = g * hidden + (SEQ * w + i) * window
                shift = lax.rem(units * (i - z) + window, window)
                moved = pltpu.roll(gate_up[:, start : start + window].astype(F32), shift, 1)
                acc = jnp.where(group == i, moved, acc)
            piece[g * rows : (g + 1) * rows, w * window : (w + 1) * window] = acc.astype(BF16)
    piece[2 * rows : 3 * rows, :] = down[at(z * units, units, 32), :]
    piece[3 * rows : 4 * rows, :] = w_out[...]
    piece[4 * rows :, :] = params[...]


def gather_weights(ids, *refs):
    blocks, odd = refs[0:4], refs[4]
    gate_up, down, w_out, vectors = refs[5:9]
    model = w_out.shape[0]
    rows = model // INNER
    size = blocks[0].shape[0]
    gathered = jnp.zeros((8, model), F32)
    for t in range(CHIPS):
        for s in range(2):
            start = ids[2 * t + s] * rows
            place = at(start, rows, 32)
            block = blocks[t] if s == 0 else odd.at[t * size : (t + 1) * size]
            gate_up[0, place, :] = block[0:rows, :]
            gate_up[1, place, :] = block[rows : 2 * rows, :]
            down[place, :] = block[2 * rows : 3 * rows, :]
            w_out[place, :] = block[3 * rows : 4 * rows, :]
            piece = block[4 * rows : 4 * rows + PAD, :].astype(F32)
            gathered = gathered + pltpu.roll(piece, start, 1)[0:8]
    vectors[...] = gathered


def attention_forward(ids, starts, slopes, *refs):
    x_blocks, w_blocks, odd = refs[0:4], refs[4:8], refs[8]
    packed, q_out, k_out, v_out, probs_out, w_qkv = refs[9:15]
    xs, attended = refs[15:17]
    rows = x_blocks[0].shape[0]
    length = SEQ * rows
    model = w_qkv.shape[1]
    width = w_qkv.shape[2]
    shard = model // INNER
    for t in range(CHIPS):
        for s in range(2):
            place = at(ids[2 * t + s] * shard, shard, 32)
            block = w_blocks[t] if s == 0 else odd.at[t * shard : (t + 1) * shard]
            for part in range(3):
                w_qkv[part, place, :] = block[:, part * width : (part + 1) * width]
    for s in range(SEQ):
        xs[s * rows : (s + 1) * rows, :] = x_blocks[s][...]
    joint = xs[...]
    q_out[...] = dot(joint, w_qkv[0]).astype(BF16)
    k_out[...] = dot(joint, w_qkv[1]).astype(BF16)
    v_out[...] = dot(joint, w_qkv[2]).astype(BF16)
    keys = k_out[...]
    values = v_out[...]
    heads = width // HEAD_DIM
    z = ids[8]

    def doc_of(position):
        count = jnp.zeros(position.shape, jnp.int32)
        for n in range(starts.shape[1]):
            count = count + (starts[0, n] <= position).astype(jnp.int32)
        return count

    lane = lax.broadcasted_iota(jnp.int32, (1, length), 1)
    key_pos = (jnp.bitwise_xor(lane // rows, z)) * rows + lane % rows
    key_docs = doc_of(key_pos)
    head_of = lax.broadcasted_iota(jnp.int32, (1, width), 1) // HEAD_DIM
    head_values = [jnp.where(head_of == h, values, jnp.zeros_like(values)) for h in range(heads)]

    def one_block(s, carry):
        place = at(s * rows, rows, 128)
        query_pos = ids[8 + s] * rows + lax.broadcasted_iota(jnp.int32, (rows, 1), 0)
        distance = jnp.abs(query_pos - key_pos).astype(F32)
        same_doc = doc_of(query_pos) == key_docs
        block = q_out[place, :] * BF16(1.0 / math.sqrt(HEAD_DIM))
        total_out = jnp.zeros((rows, width), F32)
        for h in range(heads):
            query = jnp.where(head_of == h, block, jnp.zeros_like(block))
            scores = dot_nt(query, keys) - slopes[z * heads + h] * distance
            scores = jnp.where(same_doc, scores, -1e30)
            expon = jnp.exp(scores - jnp.max(scores, axis=-1, keepdims=True))
            probs = (expon / jnp.sum(expon, axis=-1, keepdims=True)).astype(BF16)
            probs_out[h, place, :] = probs
            total_out = total_out + dot(probs, head_values[h])
        attended[place, :] = total_out.astype(BF16)
        return carry

    lax.fori_loop(0, SEQ, one_block, 0)
    half = length // 2
    packed[0:length, :] = attended[:, 0:128]
    packed[length:, 0:64] = attended[0:half, 128:192]
    packed[length:, 64:128] = attended[half:, 128:192]


def middle_forward(ids, *refs):
    packs, x_blocks = refs[0:4], refs[4:8]
    w_out, vectors, gate_up, down = refs[8:12]
    outs = refs[12:16]
    first_ref, normed_ref, stats_ref, attn = refs[16:20]
    acc = refs[20]
    rows = x_blocks[0].shape[0]
    length = SEQ * rows
    width = attn.shape[2]
    for t in range(SEQ):
        for u in range(SEQ):
            place = slice(u * rows, (u + 1) * rows)
            b = t ^ u
            attn[t, place, 0:128] = packs[t][b * rows : (b + 1) * rows, :]
            start = length + (b % 2) * rows
            attn[t, place, 128:192] = packs[t][start : start + rows, (b // 2) * 64 : (b // 2) * 64 + 64]
    w_parts = [w_out[at(ids[8 + t] * width, width, 64), :] for t in range(SEQ)]
    for u in range(SEQ):
        place = slice(u * rows, (u + 1) * rows)
        branch = dot(attn[0, place, :], w_parts[0])
        for t in range(1, SEQ):
            branch = branch + dot(attn[t, place, :], w_parts[t])
        first_sum = x_blocks[u][...].astype(F32) + branch
        normalized, _ = norm_parts(first_sum)
        normed_ref[place, :] = (normalized * vectors[0:1, :] + vectors[1:2, :]).astype(BF16)
        if u == 0:
            first_ref[...] = first_sum
            lane = lax.broadcasted_iota(jnp.int32, stats_ref.shape, 1)
            stats_ref[...] = jnp.where(lane == 0, total(branch * branch), 0.0) + jnp.where(
                lane == 1, total(first_sum * first_sum), 0.0
            )
    normed = normed_ref[...]
    step = 256
    for start in range(0, down.shape[0], step):
        cols = slice(start, start + step)
        gate = dot(normed, gate_up[0, :, cols])
        up = dot(normed, gate_up[1, :, cols])
        hidden = (gelu(gate) * up).astype(BF16)
        part = dot(hidden, down[cols, :])
        if start == 0:
            acc[...] = part
        else:
            acc[...] += part
    for s in range(SEQ):
        outs[s][...] = acc[s * rows : (s + 1) * rows, :].astype(outs[s].dtype)


def final_norm(*refs):
    parts = refs[0:4]
    normed_ref, cot_ref, vectors, stats_in = refs[4:8]
    out_ref, grad_feed_ref, grad_second_ref, sums_ref, stats_ref = refs[8:13]
    feed_out = parts[0][...]
    for s in range(1, CHIPS):
        feed_out = feed_out + parts[s][...].astype(F32)
    second = normed_ref[0 : cot_ref.shape[0], :].astype(F32) + feed_out
    normalized, inv_std = norm_parts(second)
    gain = vectors[2:3, :]
    out_ref[...] = (normalized * gain + vectors[3:4, :]).astype(BF16)
    grad = cot_ref[...].astype(F32)
    grad_second = norm_back(grad, normalized, inv_std, gain)
    grad_second_ref[...] = grad_second
    grad_feed_ref[...] = grad_second.astype(BF16)
    sums_ref[0:1, :] = column_sum(grad * normalized)
    sums_ref[1:2, :] = column_sum(grad)
    sums_ref[2:8, :] = jnp.zeros((6, gain.shape[1]), F32)
    lane = lax.broadcasted_iota(jnp.int32, stats_ref.shape, 1)
    stats_ref[...] = (
        stats_in[...]
        + jnp.where(lane == 2, total(feed_out * feed_out), 0.0)
        + jnp.where(lane == 3, total(second * second), 0.0)
    )


def feed_back(*refs):
    normed_ref, grad_blocks = refs[0], refs[1:5]
    gate_up, down = refs[5:7]
    outs = refs[7:11]
    hidden_ref, dgate_ref, dup_ref, grads = refs[11:15]
    acc = refs[15]
    rows = grad_blocks[0].shape[0]
    for s in range(SEQ):
        grads[s * rows : (s + 1) * rows, :] = grad_blocks[s][...]
    normed = normed_ref[...]
    grad_feed = grads[...]
    step = 256
    for start in range(0, down.shape[0], step):
        cols = slice(start, start + step)
        gate = dot(normed, gate_up[0, :, cols])
        up = dot(normed, gate_up[1, :, cols])
        grad_hidden = dot_nt(grad_feed, down[cols, :])
        act, slope = gelu_parts(gate)
        hidden_ref[:, cols] = (act * up).astype(BF16)
        dgate = (grad_hidden * up * slope).astype(BF16)
        dup = (grad_hidden * act).astype(BF16)
        dgate_ref[:, cols] = dgate
        dup_ref[:, cols] = dup
        part = dot_nt(dgate, gate_up[0, :, cols]) + dot_nt(dup, gate_up[1, :, cols])
        if start == 0:
            acc[...] = part
        else:
            acc[...] += part
    for s in range(SEQ):
        outs[s][...] = acc[s * rows : (s + 1) * rows, :].astype(outs[s].dtype)


def split_rows(ids, acc, keep, send, where):
    shard = acc.shape[0] // INNER
    for t in range(CHIPS):
        keep[(t,) + where] = acc[at(ids[2 * t] * shard, shard, 32), :]
        send[(t,) + where] = acc[at(ids[2 * t + 1] * shard, shard, 32), :].astype(BF16)


def feed_weights(ids, *refs):
    normed, grads, hidden, dgate, dup = refs[0:5]
    keep, send = refs[5:7]
    acc = refs[7]
    for n, (left, right) in enumerate(((normed, dgate), (normed, dup), (hidden, grads))):
        acc[...] = dot_tn(left[...], right[...])
        split_rows(ids, acc, keep, send, (n,))


def pair_sum(*refs):
    keep, received = refs[0:2]
    for t in range(CHIPS):
        refs[2 + t][...] = (keep[t] + received[t].astype(F32)).astype(refs[2 + t].dtype)


def plane_sum(*refs):
    out = refs[-1]
    acc = refs[0][...].astype(F32)
    for ref in refs[1:-1]:
        acc = acc + ref[...].astype(F32)
    out[...] = acc.astype(out.dtype)


def feed_final(ids, *refs):
    blocks, out, down_out = refs[0:4], refs[4], refs[5]
    rows, model = blocks[0].shape[1:]
    hidden = out.shape[1] // 2
    window = hidden // INNER
    units = window // SEQ
    group = lax.broadcasted_iota(jnp.int32, (rows, window), 1) // units
    for g in range(2):
        for w in range(model // window):
            parts = [b[g, :, w * window : (w + 1) * window].astype(F32) for b in blocks]
            for i in range(SEQ):
                acc = jnp.zeros((rows, window), F32)
                for s in range(SEQ):
                    pos = ids[8 + s]
                    shift = lax.rem(units * (pos - i) + window, window)
                    acc = jnp.where(group == pos, pltpu.roll(parts[s], shift, 1), acc)
                start = g * hidden + (SEQ * w + i) * window
                out[:, start : start + window] = acc
    for s in range(SEQ):
        down_out[at(ids[8 + s] * units, units, 32), :] = blocks[s][2].astype(F32)


def project_back(ids, *refs):
    parts = refs[0:4]
    grad_second, first_ref, vectors, w_out = refs[4:8]
    sums_in, stats_ref = refs[8:10]
    grad_first_ref = refs[10]
    grad_outs, sums_ref = refs[11:15], refs[15]
    grad = grad_second[...] + parts[0][...]
    for s in range(1, SEQ):
        grad = grad + parts[s][...].astype(F32)
    normalized, inv_std = norm_parts(first_ref[...])
    grad_first = norm_back(grad, normalized, inv_std, vectors[0:1, :])
    grad_first_ref[...] = grad_first
    grad_branch = grad_first.astype(BF16)
    rows, model = grad_branch.shape
    width = grad_outs[0].shape[1] // 2
    high = stats_ref[...].astype(BF16)
    low = (stats_ref[...] - high.astype(F32)).astype(BF16)
    stats_rows = jnp.concatenate([high, low], axis=0)
    stats_rows = jnp.concatenate([stats_rows, jnp.zeros((PAD, 2 * width - 128), BF16)], axis=1)
    row = lax.broadcasted_iota(jnp.int32, (model, width), 0)
    column = lax.broadcasted_iota(jnp.int32, (model, width), 1)
    for s in range(SEQ):
        start = ids[8 + s] * width
        mine = w_out[at(start, width, 64), :]
        grad_outs[s][0:rows, 0:width] = dot_nt(grad_branch, mine).astype(BF16)
        grad_outs[s][rows : rows + PAD, :] = stats_rows
        chosen = (row == start + column).astype(F32).astype(BF16)
        grad_outs[s][0:rows, width:] = dot(grad_branch, chosen).astype(BF16)
    sums_ref[0:1, :] = column_sum(grad * normalized)
    sums_ref[1:2, :] = column_sum(grad)
    sums_ref[2:4, :] = sums_in[0:2, :]
    sums_ref[4:PAD, :] = jnp.zeros((PAD - 4, model), F32)


def attention_back(*refs):
    grad_blocks = refs[0:4]
    q_ref, k_ref, v_ref, probs_ref, w_qkv = refs[4:9]
    outs, grad_qkv = refs[9:13], refs[13]
    grads, grad_q, grad_k, grad_v = refs[14:18]
    rows = outs[0].shape[0]
    for s in range(SEQ):
        place = slice(s * rows, (s + 1) * rows)
        grads[place, :] = grad_blocks[s][0:rows, 0 : grads.shape[1]]
    queries, keys, values = q_ref[...], k_ref[...], v_ref[...]
    width = keys.shape[1]
    heads = width // HEAD_DIM
    head_of = lax.broadcasted_iota(jnp.int32, (1, width), 1) // HEAD_DIM
    scale = 1.0 / math.sqrt(HEAD_DIM)
    for h in range(heads):
        mine = head_of == h
        head_keys = jnp.where(mine, keys, jnp.zeros_like(keys))
        for s in range(SEQ):
            place = slice(s * rows, (s + 1) * rows)
            grad_out = jnp.where(mine, grads[place, :], jnp.zeros((rows, width), BF16))
            query = jnp.where(mine, queries[place, :], jnp.zeros((rows, width), BF16))
            probs_low = probs_ref[h, place, :]
            probs = probs_low.astype(F32)
            grad_probs = dot_nt(grad_out, values)
            delta = jnp.sum(probs * grad_probs, axis=-1, keepdims=True)
            grad_scores = (probs * (grad_probs - delta)).astype(BF16)
            dq = dot(grad_scores, head_keys)
            dk = dot_tn(grad_scores, query)
            dv = dot_tn(probs_low, grad_out)
            if h == 0:
                grad_q[place, :] = dq
            else:
                grad_q[place, :] += dq
            if h == 0 and s == 0:
                grad_k[...] = dk
                grad_v[...] = dv
            else:
                grad_k[...] += dk
                grad_v[...] += dv
    low = (
        (grad_q[...] * scale).astype(BF16),
        (grad_k[...] * scale).astype(BF16),
        grad_v[...].astype(BF16),
    )
    grad_input = dot_nt(low[0], w_qkv[0]) + dot_nt(low[1], w_qkv[1]) + dot_nt(low[2], w_qkv[2])
    for s in range(SEQ):
        outs[s][...] = grad_input[s * rows : (s + 1) * rows, :].astype(outs[s].dtype)
    for part in range(3):
        grad_qkv[:, part * width : (part + 1) * width] = low[part]


def attention_weights(ids, *refs):
    grad_qkv, x_blocks, attn, columns = refs[0], refs[1:5], refs[5], refs[6:10]
    sums = refs[10]
    keep, send = refs[11:13]
    xs, grads, out_acc, acc = refs[13:17]
    rows = x_blocks[0].shape[0]
    width = grads.shape[1]
    for s in range(SEQ):
        place = slice(s * rows, (s + 1) * rows)
        xs[place, :] = x_blocks[s][...]
        grads[place, :] = columns[s][0:rows, width:]
    for t in range(SEQ):
        out_acc[at(ids[8 + t] * width, width, 64), :] = dot_tn(attn[t], grads[...])
    acc[:, 0 : 3 * width] = dot_tn(xs[...], grad_qkv[...])
    acc[:, 3 * width : 4 * width] = out_acc[...]
    shard = acc.shape[0] // INNER
    split_rows(ids, acc, keep, send, (slice(0, shard),))
    for t in range(CHIPS):
        keep[t, shard : shard + PAD, :] = sums[...]
        send[t, shard : shard + PAD, :] = sums[...].astype(BF16)


def input_final(*refs):
    grad_first, parts, stats_in, grad_blocks = refs[0], refs[1:5], refs[5], refs[6:9]
    out, means = refs[9:11]
    acc = grad_first[...] + parts[0][...]
    for s in range(1, SEQ):
        acc = acc + parts[s][...].astype(F32)
    out[...] = acc.astype(BF16)
    rows, model = out.shape
    stats = stats_in[...]
    for ref in grad_blocks:
        extra = ref[rows : rows + PAD, 0:128].astype(F32)
        stats = stats + (extra[0:8] + extra[8:16])
    means[...] = jnp.sqrt(stats * (1.0 / (SEQ * rows * model)))


def attention_final(ids, *refs):
    blocks, qkv_out, out, vectors, stage = refs[0:4], refs[4], refs[5], refs[6], refs[7]
    for s in range(SEQ):
        stage[ids[8 + s]] = blocks[s][...].astype(F32)
    shard, model = out.shape
    width = model // SEQ
    for pos in range(SEQ):
        for part in range(3):
            start = (part * SEQ + pos) * width
            qkv_out[:, start : start + width] = stage[pos, 0:shard, part * width : (part + 1) * width]
        out[:, pos * width : (pos + 1) * width] = stage[pos, 0:shard, 3 * width : 4 * width]
    sums = stage[0, shard : shard + 8, :]
    for pos in range(1, SEQ):
        sums = sums + stage[pos, shard : shard + 8, :]
    shift = model - ids[0] * shard
    vectors[...] = pltpu.roll(sums, lax.rem(shift, model), 1)[:, 0:128]


def after(values, *deps):
    return lax.optimization_barrier((values, deps))[0]


def body(
    layer_input,
    w_qkv,
    w_out,
    ln1_gain,
    ln1_bias,
    w_gate_up,
    w_down,
    ln2_gain,
    ln2_bias,
    doc_starts,
    cotangent,
):
    dp = lax.axis_size("dp")
    stride = dp // INNER
    rows, model = layer_input.shape[1:]
    columns = tuple(tuple(range(g * stride, (g + 1) * stride)) for g in range(INNER))
    cores = tuple(
        tuple((2 * t + core) * stride + r for t in range(CHIPS))
        for core in range(2)
        for r in range(stride)
    )

    def gather_outer(value):
        if stride == 1:
            return value
        return lax.all_gather(value, "dp", axis=0, tiled=True, axis_index_groups=columns)

    def scatter_outer(value):
        if stride == 1:
            return value
        return lax.psum_scatter(
            value, "dp", scatter_dimension=0, tiled=True, axis_index_groups=columns
        )

    def swap(value, s):
        return lax.ppermute(value, "dp", [(i, i ^ (s * stride)) for i in range(dp)])

    def pass_seq(value, s):
        return lax.ppermute(value, "seq", [(i, i ^ s) for i in range(SEQ)])

    def gather_seq(value):
        far = pass_seq(value, 2)
        near = pass_seq(value, 1)
        return [value, near, far, pass_seq(far, 1)]

    def reduce_seq(pieces):
        return [pieces[0]] + [pass_seq(pieces[s], s) for s in range(1, SEQ)]

    j = lax.axis_index("dp") // stride
    z = lax.axis_index("seq")
    ids = jnp.concatenate(
        [
            jnp.bitwise_xor(j, jnp.arange(INNER, dtype=jnp.int32)),
            jnp.bitwise_xor(z, jnp.arange(SEQ, dtype=jnp.int32)),
        ]
    )
    slopes = jnp.asarray(SLOPES)

    w_qkv, w_out, w_gate_up, w_down = map(gather_outer, (w_qkv, w_out, w_gate_up, w_down))
    vectors = [gather_outer(v) for v in (ln1_gain, ln1_bias, ln2_gain, ln2_bias)]
    shard = w_out.shape[0]
    head_width = HEADS // SEQ * HEAD_DIM

    x_own = layer_input[0]
    x_blocks = gather_seq(x_own)

    own_qkv = jnp.concatenate(
        [
            lax.dynamic_slice(w_qkv, (0, part * model + z * head_width), (shard, head_width))
            for part in range(3)
        ],
        axis=1,
    )
    qkv_even = [own_qkv] + [swap(own_qkv, s) for s in (2, 4, 6)]
    qkv_odd = swap(jnp.concatenate(qkv_even, axis=0), 1)

    params = jnp.pad(jnp.stack(vectors, axis=0), ((0, PAD - 4), (0, model - shard)))
    (piece,) = call(
        select_units,
        [((4 * shard + PAD, model), BF16)],
        [ids],
        w_gate_up,
        w_down,
        w_out,
        params,
        mib=8,
    )
    piece = after(piece, qkv_even, x_blocks[1:3])
    feed_even = [piece] + [swap(piece, s) for s in (2, 4, 6)]

    length = SEQ * rows
    packed, queries, keys, values, probs, qkv_full = call(
        attention_forward,
        [((length * 3 // 2, 128), BF16)]
        + [((length, head_width), BF16)] * 3
        + [((HEADS // SEQ, length, length), BF16), ((3, model, head_width), BF16)],
        [ids, doc_starts, slopes],
        *x_blocks,
        *qkv_even,
        qkv_odd,
        scratch=[((length, model), BF16), ((length, head_width), BF16)],
        mib=16,
        flops=2 * length * head_width * (3 * model + 2 * length),
    )
    packs = gather_seq(packed)

    feed_even = after(feed_even, packs[1:3])
    feed_odd = swap(jnp.concatenate(feed_even, axis=0), 1)
    units = w_down.shape[0] // SEQ * INNER
    gate_up_full, down_full, out_full, norm_vectors = call(
        gather_weights,
        [
            ((2, model, units), BF16),
            ((units, model), BF16),
            ((model, model), BF16),
            ((8, model), F32),
        ],
        [ids],
        *feed_even,
        feed_odd,
        mib=16,
    )

    shares = [((rows, model), F32)] + [((rows, model), BF16)] * 3
    *feed_parts, first_sum, normed, stats1, attn = call(
        middle_forward,
        shares
        + [
            ((rows, model), F32),
            ((length, model), BF16),
            ((8, 128), F32),
            ((SEQ, length, head_width), BF16),
        ],
        [ids],
        *packs,
        *x_blocks,
        out_full,
        norm_vectors,
        gate_up_full,
        down_full,
        scratch=[((length, model), F32)],
        mib=16,
        flops=2 * length * model * (model + 3 * units),
    )

    output, grad_feed, grad_second, sums2, stats2 = call(
        final_norm,
        [
            ((rows, model), BF16),
            ((rows, model), BF16),
            ((rows, model), F32),
            ((8, model), F32),
            ((8, 128), F32),
        ],
        [],
        *reduce_seq(feed_parts),
        normed,
        cotangent[0],
        norm_vectors,
        stats1,
    )

    *back_parts, hidden, dgate, dup, grads = call(
        feed_back,
        shares + [((length, units), BF16)] * 3 + [((length, model), BF16)],
        [],
        normed,
        *gather_seq(grad_feed),
        gate_up_full,
        down_full,
        scratch=[((length, model), F32)],
        mib=18,
        flops=10 * length * model * units,
    )
    back_parts = reduce_seq(back_parts)

    feed_keep, feed_send = call(
        feed_weights,
        [((CHIPS, 3, shard, model), F32), ((CHIPS, 3, shard, model), BF16)],
        [ids],
        normed,
        grads,
        hidden,
        dgate,
        dup,
        scratch=[((model, model), F32)],
        mib=18,
        flops=6 * length * model * units,
    )

    def pair(keep, send):
        shape = keep.shape[1:]
        return call(pair_sum, [(shape, F32)] + [(shape, BF16)] * 3, [], keep, swap(send, 1))

    def reduce_plane(pieces):
        shape = pieces[0].shape
        pieces = [pieces[0]] + [swap(pieces[t], 2 * t) for t in range(1, CHIPS)]
        return call(plane_sum, [(shape, BF16)], [], *pieces)[0]

    feed_pieces = pair(feed_keep, feed_send)
    grad_second = after(grad_second, feed_pieces)
    feed_pieces = after(feed_pieces, back_parts)

    grad_first, *projected = call(
        project_back,
        [((rows, model), F32)]
        + [((rows + PAD, 2 * head_width), BF16)] * SEQ
        + [((PAD, model), F32)],
        [ids],
        *back_parts,
        grad_second,
        first_sum,
        norm_vectors,
        out_full,
        sums2,
        stats2,
        mib=10,
        flops=4 * rows * model * model,
    )
    grad_attn = reduce_seq(projected[0:4])
    sums = projected[4]
    feed_share = reduce_plane(feed_pieces)
    feed_blocks = gather_seq(after(feed_share, grad_attn))

    *input_parts, grad_qkv = call(
        attention_back,
        shares + [((length, 3 * head_width), BF16)],
        [],
        *grad_attn,
        queries,
        keys,
        values,
        probs,
        qkv_full,
        scratch=[((length, head_width), BF16)] + [((length, head_width), F32)] * 3,
        mib=16,
        flops=2 * length * head_width * (3 * model + 5 * length),
    )
    input_parts = reduce_seq(input_parts)

    sums = after(sums, feed_share)

    attn_keep, attn_send = call(
        attention_weights,
        [
            ((CHIPS, shard + PAD, model), F32),
            ((CHIPS, shard + PAD, model), BF16),
        ],
        [ids],
        grad_qkv,
        *x_blocks,
        attn,
        *grad_attn,
        sums,
        scratch=[
            ((length, model), BF16),
            ((length, head_width), BF16),
            ((model, head_width), F32),
            ((model, model), F32),
        ],
        mib=16,
        flops=2 * length * model * model,
    )

    grad_gate_up_w, grad_down_w = call(
        feed_final,
        [(w_gate_up.shape, F32), (w_down.shape, F32)],
        [ids],
        *feed_blocks,
        mib=10,
    )
    attn_pieces = after(pair(attn_keep, attn_send), input_parts)
    attn_share = after(reduce_plane(attn_pieces), feed_blocks[2])
    grad_qkv_w, grad_out_w, vector_grads = call(
        attention_final,
        [((shard, 3 * model), F32), ((shard, model), F32), ((8, 128), F32)],
        [ids],
        *gather_seq(attn_share),
        scratch=[((SEQ, shard + PAD, model), F32)],
    )

    input_grad, means = call(
        input_final,
        [((rows, model), BF16), ((8, 128), F32)],
        [],
        grad_first,
        *input_parts,
        stats2,
        *grad_attn[1:],
    )
    vector_grads = [scatter_outer(vector_grads[n, :shard]) for n in range(4)]
    return (
        output[None],
        input_grad[None],
        scatter_outer(grad_qkv_w),
        scatter_outer(grad_out_w),
        vector_grads[0],
        vector_grads[1],
        scatter_outer(grad_gate_up_w),
        scatter_outer(grad_down_w),
        vector_grads[2],
        vector_grads[3],
        means[0:1, 0:4],
    )


def solution(mesh):
    return jax.shard_map(
        body,
        mesh=mesh,
        in_specs=(
            P("dp", "seq", None),
            P("dp", None),
            P("dp", None),
            P("dp"),
            P("dp"),
            P("dp", None),
            P("dp", None),
            P("dp"),
            P("dp"),
            P("dp", None),
            P("dp", "seq", None),
        ),
        out_specs=(
            P("dp", "seq", None),
            P("dp", "seq", None),
            P("dp", None),
            P("dp", None),
            P("dp"),
            P("dp"),
            P("dp", None),
            P("dp", None),
            P("dp"),
            P("dp"),
            P("dp", None),
        ),
        check_vma=False,
    )
```

```python
import math

import jax
import jax.numpy as jnp
import numpy as np
from jax import lax
from jax.experimental import pallas as pl
from jax.experimental.pallas import tpu as pltpu
from jax.sharding import PartitionSpec as P

HEADS = 12
HEAD_DIM = 64
NORM_EPSILON = 1e-05
GELU_C = 0.7978845608028654
GELU_A = 0.044715
INNER = 8
CHIPS = 4
SEQ = 4
PAD = 16

F32 = jnp.float32
BF16 = jnp.bfloat16
SLOPES = (2.0 ** (-8.0 * (np.arange(HEADS) + 1.0) / HEADS)).astype(np.float32)


def dot(left, right):
    return jnp.dot(left, right, preferred_element_type=F32)


def dot_nt(left, right):
    return lax.dot_general(left, right, (((1,), (1,)), ((), ())), preferred_element_type=F32)


def dot_tn(left, right):
    return lax.dot_general(left, right, (((0,), (0,)), ((), ())), preferred_element_type=F32)


def gelu_parts(value):
    square = value * value
    tanh = jnp.tanh(GELU_C * (value + GELU_A * square * value))
    half = 0.5 * (1.0 + tanh)
    slope = half + 0.5 * value * (1.0 - tanh * tanh) * (GELU_C * (1.0 + 3.0 * GELU_A * square))
    return value * half, slope


def gelu(value):
    return 0.5 * value * (1.0 + jnp.tanh(GELU_C * (value + GELU_A * value * value * value)))


def norm_parts(summed):
    centered = summed - jnp.mean(summed, axis=-1, keepdims=True)
    variance = jnp.mean(centered * centered, axis=-1, keepdims=True)
    inv_std = lax.rsqrt(variance + NORM_EPSILON)
    return centered * inv_std, inv_std


def norm_back(grad_in, normalized, inv_std, gain):
    scaled = grad_in * gain
    return inv_std * (
        scaled
        - jnp.mean(scaled, axis=-1, keepdims=True)
        - normalized * jnp.mean(scaled * normalized, axis=-1, keepdims=True)
    )


def column_sum(value):
    return jnp.sum(value, axis=0, keepdims=True)


def total(value):
    return jnp.sum(jnp.sum(value, axis=1, keepdims=True), axis=0, keepdims=True)


def at(start, size, step):
    return pl.ds(pl.multiple_of(start, step), size)


def call(kernel, outs, smem, *vmem, scratch=(), flops=0, mib=8, aliases=None):
    specs = [pl.BlockSpec(memory_space=pltpu.SMEM) for _ in smem]
    specs += [pl.BlockSpec(memory_space=pltpu.VMEM) for _ in vmem]
    out_shape = [jax.ShapeDtypeStruct(shape, dtype) for shape, dtype in outs]
    moved = sum(math.prod(a.shape) * a.dtype.itemsize for a in list(vmem) + out_shape)
    return pl.pallas_call(
        kernel,
        out_shape=out_shape,
        in_specs=specs,
        out_specs=[pl.BlockSpec(memory_space=pltpu.VMEM) for _ in outs],
        scratch_shapes=[pltpu.VMEM(shape, dtype) for shape, dtype in scratch],
        input_output_aliases=aliases or {},
        cost_estimate=pl.CostEstimate(flops=flops, transcendentals=0, bytes_accessed=moved),
        name=kernel.__name__,
        compiler_params=pltpu.CompilerParams(vmem_limit_bytes=mib << 20),
    )(*smem, *vmem)


def select_units(ids, gate_up, down, w_out, params, piece):
    z = ids[8]
    rows = w_out.shape[0]
    window = down.shape[0]
    units = window // SEQ
    model = w_out.shape[1]
    hidden = gate_up.shape[1] // 2
    group = lax.broadcasted_iota(jnp.int32, (rows, window), 1) // units
    for g in range(2):
        for w in range(model // window):
            acc = jnp.zeros((rows, window), F32)
            for i in range(SEQ):
                start = g * hidden + (SEQ * w + i) * window
                shift = lax.rem(units * (i - z) + window, window)
                moved = pltpu.roll(gate_up[:, start : start + window].astype(F32), shift, 1)
                acc = jnp.where(group == i, moved, acc)
            piece[g * rows : (g + 1) * rows, w * window : (w + 1) * window] = acc.astype(BF16)
    piece[2 * rows : 3 * rows, :] = down[at(z * units, units, 32), :]
    piece[3 * rows : 4 * rows, :] = w_out[...]
    piece[4 * rows :, :] = params[...]


def gather_weights(ids, *refs):
    blocks, odd = refs[0:4], refs[4]
    gate_up, down, w_out, vectors = refs[5:9]
    model = w_out.shape[0]
    rows = model // INNER
    size = blocks[0].shape[0]
    gathered = jnp.zeros((8, model), F32)
    for t in range(CHIPS):
        for s in range(2):
            start = ids[2 * t + s] * rows
            place = at(start, rows, 32)
            block = blocks[t] if s == 0 else odd.at[t * size : (t + 1) * size]
            gate_up[0, place, :] = block[0:rows, :]
            gate_up[1, place, :] = block[rows : 2 * rows, :]
            down[place, :] = block[2 * rows : 3 * rows, :]
            w_out[place, :] = block[3 * rows : 4 * rows, :]
            piece = block[4 * rows : 4 * rows + PAD, :].astype(F32)
            gathered = gathered + pltpu.roll(piece, start, 1)[0:8]
    vectors[...] = gathered


def attention_forward(ids, starts, slopes, *refs):
    x_blocks, w_blocks, odd = refs[0:4], refs[4:8], refs[8]
    packed, q_out, k_out, v_out, probs_out, w_qkv = refs[9:15]
    xs, attended = refs[15:17]
    rows = x_blocks[0].shape[0]
    length = SEQ * rows
    model = w_qkv.shape[1]
    width = w_qkv.shape[2]
    shard = model // INNER
    for t in range(CHIPS):
        for s in range(2):
            place = at(ids[2 * t + s] * shard, shard, 32)
            block = w_blocks[t] if s == 0 else odd.at[t * shard : (t + 1) * shard]
            for part in range(3):
                w_qkv[part, place, :] = block[:, part * width : (part + 1) * width]
    for s in range(SEQ):
        xs[s * rows : (s + 1) * rows, :] = x_blocks[s][...]
    joint = xs[...]
    q_out[...] = dot(joint, w_qkv[0]).astype(BF16)
    k_out[...] = dot(joint, w_qkv[1]).astype(BF16)
    v_out[...] = dot(joint, w_qkv[2]).astype(BF16)
    keys = k_out[...]
    values = v_out[...]
    heads = width // HEAD_DIM
    z = ids[8]

    def doc_of(position):
        count = jnp.zeros(position.shape, jnp.int32)
        for n in range(starts.shape[1]):
            count = count + (starts[0, n] <= position).astype(jnp.int32)
        return count

    lane = lax.broadcasted_iota(jnp.int32, (1, length), 1)
    key_pos = (jnp.bitwise_xor(lane // rows, z)) * rows + lane % rows
    key_docs = doc_of(key_pos)
    head_of = lax.broadcasted_iota(jnp.int32, (1, width), 1) // HEAD_DIM
    head_values = [jnp.where(head_of == h, values, jnp.zeros_like(values)) for h in range(heads)]

    def one_block(s, carry):
        place = at(s * rows, rows, 128)
        query_pos = ids[8 + s] * rows + lax.broadcasted_iota(jnp.int32, (rows, 1), 0)
        distance = jnp.abs(query_pos - key_pos).astype(F32)
        same_doc = doc_of(query_pos) == key_docs
        block = q_out[place, :] * BF16(1.0 / math.sqrt(HEAD_DIM))
        total_out = jnp.zeros((rows, width), F32)
        for h in range(heads):
            query = jnp.where(head_of == h, block, jnp.zeros_like(block))
            scores = dot_nt(query, keys) - slopes[z * heads + h] * distance
            scores = jnp.where(same_doc, scores, -1e30)
            expon = jnp.exp(scores - jnp.max(scores, axis=-1, keepdims=True))
            probs = (expon / jnp.sum(expon, axis=-1, keepdims=True)).astype(BF16)
            probs_out[h, place, :] = probs
            total_out = total_out + dot(probs, head_values[h])
        attended[place, :] = total_out.astype(BF16)
        return carry

    lax.fori_loop(0, SEQ, one_block, 0)
    half = length // 2
    packed[0:length, :] = attended[:, 0:128]
    packed[length:, 0:64] = attended[0:half, 128:192]
    packed[length:, 64:128] = attended[half:, 128:192]


def middle_forward(ids, *refs):
    packs, x_blocks = refs[0:4], refs[4:8]
    w_out, vectors, gate_up, down = refs[8:12]
    outs = refs[12:16]
    first_ref, normed_ref, stats_ref, attn = refs[16:20]
    acc = refs[20]
    rows = x_blocks[0].shape[0]
    length = SEQ * rows
    width = attn.shape[2]
    for t in range(SEQ):
        for u in range(SEQ):
            place = slice(u * rows, (u + 1) * rows)
            b = t ^ u
            attn[t, place, 0:128] = packs[t][b * rows : (b + 1) * rows, :]
            start = length + (b % 2) * rows
            attn[t, place, 128:192] = packs[t][start : start + rows, (b // 2) * 64 : (b // 2) * 64 + 64]
    w_parts = [w_out[at(ids[8 + t] * width, width, 64), :] for t in range(SEQ)]
    for u in range(SEQ):
        place = slice(u * rows, (u + 1) * rows)
        branch = dot(attn[0, place, :], w_parts[0])
        for t in range(1, SEQ):
            branch = branch + dot(attn[t, place, :], w_parts[t])
        first_sum = x_blocks[u][...].astype(F32) + branch
        normalized, _ = norm_parts(first_sum)
        normed_ref[place, :] = (normalized * vectors[0:1, :] + vectors[1:2, :]).astype(BF16)
        if u == 0:
            first_ref[...] = first_sum
            lane = lax.broadcasted_iota(jnp.int32, stats_ref.shape, 1)
            stats_ref[...] = jnp.where(lane == 0, total(branch * branch), 0.0) + jnp.where(
                lane == 1, total(first_sum * first_sum), 0.0
            )
    normed = normed_ref[...]
    step = 256
    for start in range(0, down.shape[0], step):
        cols = slice(start, start + step)
        gate = dot(normed, gate_up[0, :, cols])
        up = dot(normed, gate_up[1, :, cols])
        hidden = (gelu(gate) * up).astype(BF16)
        part = dot(hidden, down[cols, :])
        if start == 0:
            acc[...] = part
        else:
            acc[...] += part
    for s in range(SEQ):
        outs[s][...] = acc[s * rows : (s + 1) * rows, :].astype(outs[s].dtype)


def final_norm(*refs):
    parts = refs[0:4]
    normed_ref, cot_ref, vectors, stats_in = refs[4:8]
    out_ref, grad_feed_ref, grad_second_ref, sums_ref, stats_ref = refs[8:13]
    feed_out = parts[0][...]
    for s in range(1, CHIPS):
        feed_out = feed_out + parts[s][...].astype(F32)
    second = normed_ref[0 : cot_ref.shape[0], :].astype(F32) + feed_out
    normalized, inv_std = norm_parts(second)
    gain = vectors[2:3, :]
    out_ref[...] = (normalized * gain + vectors[3:4, :]).astype(BF16)
    grad = cot_ref[...].astype(F32)
    grad_second = norm_back(grad, normalized, inv_std, gain)
    grad_second_ref[...] = grad_second
    grad_feed_ref[...] = grad_second.astype(BF16)
    sums_ref[0:1, :] = column_sum(grad * normalized)
    sums_ref[1:2, :] = column_sum(grad)
    sums_ref[2:8, :] = jnp.zeros((6, gain.shape[1]), F32)
    lane = lax.broadcasted_iota(jnp.int32, stats_ref.shape, 1)
    stats_ref[...] = (
        stats_in[...]
        + jnp.where(lane == 2, total(feed_out * feed_out), 0.0)
        + jnp.where(lane == 3, total(second * second), 0.0)
    )


def feed_back(*refs):
    normed_ref, grad_blocks = refs[0], refs[1:5]
    gate_up, down = refs[5:7]
    outs = refs[7:11]
    hidden_ref, dgate_ref, dup_ref, grads = refs[11:15]
    acc = refs[15]
    rows = grad_blocks[0].shape[0]
    for s in range(SEQ):
        grads[s * rows : (s + 1) * rows, :] = grad_blocks[s][...]
    normed = normed_ref[...]
    grad_feed = grads[...]
    step = 256
    for start in range(0, down.shape[0], step):
        cols = slice(start, start + step)
        gate = dot(normed, gate_up[0, :, cols])
        up = dot(normed, gate_up[1, :, cols])
        grad_hidden = dot_nt(grad_feed, down[cols, :])
        act, slope = gelu_parts(gate)
        hidden_ref[:, cols] = (act * up).astype(BF16)
        dgate = (grad_hidden * up * slope).astype(BF16)
        dup = (grad_hidden * act).astype(BF16)
        dgate_ref[:, cols] = dgate
        dup_ref[:, cols] = dup
        part = dot_nt(dgate, gate_up[0, :, cols]) + dot_nt(dup, gate_up[1, :, cols])
        if start == 0:
            acc[...] = part
        else:
            acc[...] += part
    for s in range(SEQ):
        outs[s][...] = acc[s * rows : (s + 1) * rows, :].astype(outs[s].dtype)


def split_rows(ids, acc, keep, send, where):
    shard = acc.shape[0] // INNER
    for t in range(CHIPS):
        keep[(t,) + where] = acc[at(ids[2 * t] * shard, shard, 32), :]
        send[(t,) + where] = acc[at(ids[2 * t + 1] * shard, shard, 32), :].astype(BF16)


def feed_weights(ids, *refs):
    normed, grads, hidden, dgate, dup = refs[0:5]
    keep, send = refs[5:7]
    acc = refs[7]
    for n, (left, right) in enumerate(((normed, dgate), (normed, dup), (hidden, grads))):
        acc[...] = dot_tn(left[...], right[...])
        split_rows(ids, acc, keep, send, (n,))


def pair_sum(*refs):
    keep, received = refs[0:2]
    for t in range(CHIPS):
        refs[2 + t][...] = (keep[t] + received[t].astype(F32)).astype(refs[2 + t].dtype)


def step_one(*refs):
    keep, received = refs[0:2]
    left, left_next, right, right_next, to_x, to_y = refs[2:8]
    half = left.shape[-1]

    def part(t, side):
        cols = slice(side * half, (side + 1) * half)
        return keep[t, :, :, cols] + received[t, :, :, cols].astype(F32)

    left[...] = part(0, 0)
    left_next[...] = part(2, 0)
    right[...] = part(0, 1)
    right_next[...] = part(1, 1)
    to_x[0] = part(1, 0).astype(BF16)
    to_x[1] = part(3, 0).astype(BF16)
    to_y[0] = part(2, 1).astype(BF16)
    to_y[1] = part(3, 1).astype(BF16)


def step_two(*refs):
    left, left_next, right, right_next, from_x, from_y = refs[0:6]
    left_out, right_out, to_y, to_x = refs[6:10]
    left_out[...] = left[...] + from_x[0].astype(F32)
    to_y[...] = (left_next[...] + from_x[1].astype(F32)).astype(BF16)
    right_out[...] = right[...] + from_y[0].astype(F32)
    to_x[...] = (right_next[...] + from_y[1].astype(F32)).astype(BF16)


def step_three(*refs):
    left, right, from_y, from_x, out = refs
    half = left.shape[-1]
    out[:, :, 0:half] = (left[...] + from_y[...].astype(F32)).astype(BF16)
    out[:, :, half:] = (right[...] + from_x[...].astype(F32)).astype(BF16)


def plane_sum(*refs):
    out = refs[-1]
    acc = refs[0][...].astype(F32)
    for ref in refs[1:-1]:
        acc = acc + ref[...].astype(F32)
    out[...] = acc.astype(out.dtype)


def feed_final(ids, *refs):
    blocks, out, down_out = refs[0:4], refs[4], refs[5]
    rows, model = blocks[0].shape[1:]
    hidden = out.shape[1] // 2
    window = hidden // INNER
    units = window // SEQ
    group = lax.broadcasted_iota(jnp.int32, (rows, window), 1) // units
    for g in range(2):
        for w in range(model // window):
            parts = [b[g, :, w * window : (w + 1) * window].astype(F32) for b in blocks]
            for i in range(SEQ):
                acc = jnp.zeros((rows, window), F32)
                for s in range(SEQ):
                    pos = ids[8 + s]
                    shift = lax.rem(units * (pos - i) + window, window)
                    acc = jnp.where(group == pos, pltpu.roll(parts[s], shift, 1), acc)
                start = g * hidden + (SEQ * w + i) * window
                out[:, start : start + window] = acc
    for s in range(SEQ):
        down_out[at(ids[8 + s] * units, units, 32), :] = blocks[s][2].astype(F32)


def project_back(ids, *refs):
    parts = refs[0:4]
    grad_second, first_ref, vectors, w_out = refs[4:8]
    sums_in, stats_ref = refs[8:10]
    grad_first_ref = refs[10]
    grad_outs, sums_ref = refs[11:15], refs[15]
    grad = grad_second[...] + parts[0][...]
    for s in range(1, SEQ):
        grad = grad + parts[s][...].astype(F32)
    normalized, inv_std = norm_parts(first_ref[...])
    grad_first = norm_back(grad, normalized, inv_std, vectors[0:1, :])
    grad_first_ref[...] = grad_first
    grad_branch = grad_first.astype(BF16)
    rows, model = grad_branch.shape
    width = grad_outs[0].shape[1] // 2
    high = stats_ref[...].astype(BF16)
    low = (stats_ref[...] - high.astype(F32)).astype(BF16)
    stats_rows = jnp.concatenate([high, low], axis=0)
    stats_rows = jnp.concatenate([stats_rows, jnp.zeros((PAD, 2 * width - 128), BF16)], axis=1)
    row = lax.broadcasted_iota(jnp.int32, (model, width), 0)
    column = lax.broadcasted_iota(jnp.int32, (model, width), 1)
    for s in range(SEQ):
        start = ids[8 + s] * width
        mine = w_out[at(start, width, 64), :]
        grad_outs[s][0:rows, 0:width] = dot_nt(grad_branch, mine).astype(BF16)
        grad_outs[s][rows : rows + PAD, :] = stats_rows
        chosen = (row == start + column).astype(F32).astype(BF16)
        grad_outs[s][0:rows, width:] = dot(grad_branch, chosen).astype(BF16)
    sums_ref[0:1, :] = column_sum(grad * normalized)
    sums_ref[1:2, :] = column_sum(grad)
    sums_ref[2:4, :] = sums_in[0:2, :]
    sums_ref[4:PAD, :] = jnp.zeros((PAD - 4, model), F32)


def attention_back(*refs):
    grad_blocks = refs[0:4]
    q_ref, k_ref, v_ref, probs_ref, w_qkv = refs[4:9]
    outs, grad_qkv = refs[9:13], refs[13]
    grads, grad_q, grad_k, grad_v = refs[14:18]
    rows = outs[0].shape[0]
    for s in range(SEQ):
        place = slice(s * rows, (s + 1) * rows)
        grads[place, :] = grad_blocks[s][0:rows, 0 : grads.shape[1]]
    queries, keys, values = q_ref[...], k_ref[...], v_ref[...]
    width = keys.shape[1]
    heads = width // HEAD_DIM
    head_of = lax.broadcasted_iota(jnp.int32, (1, width), 1) // HEAD_DIM
    scale = 1.0 / math.sqrt(HEAD_DIM)
    for h in range(heads):
        mine = head_of == h
        head_keys = jnp.where(mine, keys, jnp.zeros_like(keys))
        for s in range(SEQ):
            place = slice(s * rows, (s + 1) * rows)
            grad_out = jnp.where(mine, grads[place, :], jnp.zeros((rows, width), BF16))
            query = jnp.where(mine, queries[place, :], jnp.zeros((rows, width), BF16))
            probs_low = probs_ref[h, place, :]
            probs = probs_low.astype(F32)
            grad_probs = dot_nt(grad_out, values)
            delta = jnp.sum(probs * grad_probs, axis=-1, keepdims=True)
            grad_scores = (probs * (grad_probs - delta)).astype(BF16)
            dq = dot(grad_scores, head_keys)
            dk = dot_tn(grad_scores, query)
            dv = dot_tn(probs_low, grad_out)
            if h == 0:
                grad_q[place, :] = dq
            else:
                grad_q[place, :] += dq
            if h == 0 and s == 0:
                grad_k[...] = dk
                grad_v[...] = dv
            else:
                grad_k[...] += dk
                grad_v[...] += dv
    low = (
        (grad_q[...] * scale).astype(BF16),
        (grad_k[...] * scale).astype(BF16),
        grad_v[...].astype(BF16),
    )
    grad_input = dot_nt(low[0], w_qkv[0]) + dot_nt(low[1], w_qkv[1]) + dot_nt(low[2], w_qkv[2])
    for s in range(SEQ):
        outs[s][...] = grad_input[s * rows : (s + 1) * rows, :].astype(outs[s].dtype)
    for part in range(3):
        grad_qkv[:, part * width : (part + 1) * width] = low[part]


def attention_weights(ids, *refs):
    grad_qkv, x_blocks, attn, columns = refs[0], refs[1:5], refs[5], refs[6:10]
    sums = refs[10]
    keep, send = refs[11:13]
    xs, grads, out_acc, acc = refs[13:17]
    rows = x_blocks[0].shape[0]
    width = grads.shape[1]
    for s in range(SEQ):
        place = slice(s * rows, (s + 1) * rows)
        xs[place, :] = x_blocks[s][...]
        grads[place, :] = columns[s][0:rows, width:]
    for t in range(SEQ):
        out_acc[at(ids[8 + t] * width, width, 64), :] = dot_tn(attn[t], grads[...])
    acc[:, 0 : 3 * width] = dot_tn(xs[...], grad_qkv[...])
    acc[:, 3 * width : 4 * width] = out_acc[...]
    shard = acc.shape[0] // INNER
    split_rows(ids, acc, keep, send, (slice(0, shard),))
    for t in range(CHIPS):
        keep[t, shard : shard + PAD, :] = sums[...]
        send[t, shard : shard + PAD, :] = sums[...].astype(BF16)


def input_final(*refs):
    grad_first, parts, stats_in, grad_blocks = refs[0], refs[1:5], refs[5], refs[6:9]
    out, means = refs[9:11]
    acc = grad_first[...] + parts[0][...]
    for s in range(1, SEQ):
        acc = acc + parts[s][...].astype(F32)
    out[...] = acc.astype(BF16)
    rows, model = out.shape
    stats = stats_in[...]
    for ref in grad_blocks:
        extra = ref[rows : rows + PAD, 0:128].astype(F32)
        stats = stats + (extra[0:8] + extra[8:16])
    means[...] = jnp.sqrt(stats * (1.0 / (SEQ * rows * model)))


def attention_final(ids, *refs):
    blocks, qkv_out, out, vectors, stage = refs[0:4], refs[4], refs[5], refs[6], refs[7]
    for s in range(SEQ):
        stage[ids[8 + s]] = blocks[s][...].astype(F32)
    shard, model = out.shape
    width = model // SEQ
    for pos in range(SEQ):
        for part in range(3):
            start = (part * SEQ + pos) * width
            qkv_out[:, start : start + width] = stage[pos, 0:shard, part * width : (part + 1) * width]
        out[:, pos * width : (pos + 1) * width] = stage[pos, 0:shard, 3 * width : 4 * width]
    sums = stage[0, shard : shard + 8, :]
    for pos in range(1, SEQ):
        sums = sums + stage[pos, shard : shard + 8, :]
    shift = model - ids[0] * shard
    vectors[...] = pltpu.roll(sums, lax.rem(shift, model), 1)[:, 0:128]


def after(values, *deps):
    return lax.optimization_barrier((values, deps))[0]


def body(
    layer_input,
    w_qkv,
    w_out,
    ln1_gain,
    ln1_bias,
    w_gate_up,
    w_down,
    ln2_gain,
    ln2_bias,
    doc_starts,
    cotangent,
):
    dp = lax.axis_size("dp")
    stride = dp // INNER
    rows, model = layer_input.shape[1:]
    columns = tuple(tuple(range(g * stride, (g + 1) * stride)) for g in range(INNER))
    cores = tuple(
        tuple((2 * t + core) * stride + r for t in range(CHIPS))
        for core in range(2)
        for r in range(stride)
    )

    def gather_outer(value):
        if stride == 1:
            return value
        return lax.all_gather(value, "dp", axis=0, tiled=True, axis_index_groups=columns)

    def scatter_outer(value):
        if stride == 1:
            return value
        return lax.psum_scatter(
            value, "dp", scatter_dimension=0, tiled=True, axis_index_groups=columns
        )

    def swap(value, s):
        return lax.ppermute(value, "dp", [(i, i ^ (s * stride)) for i in range(dp)])

    def pass_seq(value, s):
        return lax.ppermute(value, "seq", [(i, i ^ s) for i in range(SEQ)])

    def gather_seq(value):
        far = pass_seq(value, 2)
        near = pass_seq(value, 1)
        return [value, near, far, pass_seq(far, 1)]

    def reduce_seq(pieces):
        return [pieces[0]] + [pass_seq(pieces[s], s) for s in range(1, SEQ)]

    j = lax.axis_index("dp") // stride
    z = lax.axis_index("seq")
    ids = jnp.concatenate(
        [
            jnp.bitwise_xor(j, jnp.arange(INNER, dtype=jnp.int32)),
            jnp.bitwise_xor(z, jnp.arange(SEQ, dtype=jnp.int32)),
        ]
    )
    slopes = jnp.asarray(SLOPES)

    w_qkv, w_out, w_gate_up, w_down = map(gather_outer, (w_qkv, w_out, w_gate_up, w_down))
    vectors = [gather_outer(v) for v in (ln1_gain, ln1_bias, ln2_gain, ln2_bias)]
    shard = w_out.shape[0]
    head_width = HEADS // SEQ * HEAD_DIM

    x_own = layer_input[0]
    x_blocks = gather_seq(x_own)

    own_qkv = jnp.concatenate(
        [
            lax.dynamic_slice(w_qkv, (0, part * model + z * head_width), (shard, head_width))
            for part in range(3)
        ],
        axis=1,
    )
    qkv_even = [own_qkv] + [swap(own_qkv, s) for s in (2, 4, 6)]
    qkv_odd = swap(jnp.concatenate(qkv_even, axis=0), 1)

    params = jnp.pad(jnp.stack(vectors, axis=0), ((0, PAD - 4), (0, model - shard)))
    (piece,) = call(
        select_units,
        [((4 * shard + PAD, model), BF16)],
        [ids],
        w_gate_up,
        w_down,
        w_out,
        params,
        mib=8,
    )
    piece = after(piece, qkv_even, x_blocks[1:3])
    feed_even = [piece] + [swap(piece, s) for s in (2, 4, 6)]

    length = SEQ * rows
    packed, queries, keys, values, probs, qkv_full = call(
        attention_forward,
        [((length * 3 // 2, 128), BF16)]
        + [((length, head_width), BF16)] * 3
        + [((HEADS // SEQ, length, length), BF16), ((3, model, head_width), BF16)],
        [ids, doc_starts, slopes],
        *x_blocks,
        *qkv_even,
        qkv_odd,
        scratch=[((length, model), BF16), ((length, head_width), BF16)],
        mib=16,
        flops=2 * length * head_width * (3 * model + 2 * length),
    )
    packs = gather_seq(packed)

    feed_even = after(feed_even, packs[1:3])
    feed_odd = swap(jnp.concatenate(feed_even, axis=0), 1)
    units = w_down.shape[0] // SEQ * INNER
    gate_up_full, down_full, out_full, norm_vectors = call(
        gather_weights,
        [
            ((2, model, units), BF16),
            ((units, model), BF16),
            ((model, model), BF16),
            ((8, model), F32),
        ],
        [ids],
        *feed_even,
        feed_odd,
        mib=16,
    )

    shares = [((rows, model), F32)] + [((rows, model), BF16)] * 3
    *feed_parts, first_sum, normed, stats1, attn = call(
        middle_forward,
        shares
        + [
            ((rows, model), F32),
            ((length, model), BF16),
            ((8, 128), F32),
            ((SEQ, length, head_width), BF16),
        ],
        [ids],
        *packs,
        *x_blocks,
        out_full,
        norm_vectors,
        gate_up_full,
        down_full,
        scratch=[((length, model), F32)],
        mib=16,
        flops=2 * length * model * (model + 3 * units),
    )

    output, grad_feed, grad_second, sums2, stats2 = call(
        final_norm,
        [
            ((rows, model), BF16),
            ((rows, model), BF16),
            ((rows, model), F32),
            ((8, model), F32),
            ((8, 128), F32),
        ],
        [],
        *reduce_seq(feed_parts),
        normed,
        cotangent[0],
        norm_vectors,
        stats1,
    )

    *back_parts, hidden, dgate, dup, grads = call(
        feed_back,
        shares + [((length, units), BF16)] * 3 + [((length, model), BF16)],
        [],
        normed,
        *gather_seq(grad_feed),
        gate_up_full,
        down_full,
        scratch=[((length, model), F32)],
        mib=18,
        flops=10 * length * model * units,
    )
    back_parts = reduce_seq(back_parts)

    feed_keep, feed_send = call(
        feed_weights,
        [((CHIPS, 3, shard, model), F32), ((CHIPS, 3, shard, model), BF16)],
        [ids],
        normed,
        grads,
        hidden,
        dgate,
        dup,
        scratch=[((model, model), F32)],
        mib=18,
        flops=6 * length * model * units,
    )

    def pair(keep, send):
        shape = keep.shape[1:]
        return call(pair_sum, [(shape, F32)] + [(shape, BF16)] * 3, [], keep, swap(send, 1))

    half_shape = (3, shard, model // 2)
    *feed_pieces, to_x, to_y = call(
        step_one,
        [(half_shape, F32)] * 4 + [((2,) + half_shape, BF16)] * 2,
        [],
        after(feed_keep, back_parts[1]),
        swap(feed_send, 1),
        mib=10,
    )
    left, right, to_y, to_x = call(
        step_two,
        [(half_shape, F32)] * 2 + [(half_shape, BF16)] * 2,
        [],
        *feed_pieces,
        swap(to_x, 2),
        swap(to_y, 4),
        mib=10,
    )
    grad_second = after(grad_second, to_y)

    grad_first, *projected = call(
        project_back,
        [((rows, model), F32)]
        + [((rows + PAD, 2 * head_width), BF16)] * SEQ
        + [((PAD, model), F32)],
        [ids],
        *back_parts,
        grad_second,
        first_sum,
        norm_vectors,
        out_full,
        sums2,
        stats2,
        mib=10,
        flops=4 * rows * model * model,
    )
    grad_attn = reduce_seq(projected[0:4])
    sums = projected[4]
    (feed_share,) = call(
        step_three, [((3, shard, model), BF16)], [], left, right, swap(to_y, 4), swap(to_x, 2)
    )
    queries = after(queries, feed_share)
    feed_blocks = gather_seq(after(feed_share, grad_attn))

    *input_parts, grad_qkv = call(
        attention_back,
        shares + [((length, 3 * head_width), BF16)],
        [],
        *grad_attn,
        queries,
        keys,
        values,
        probs,
        qkv_full,
        scratch=[((length, head_width), BF16)] + [((length, head_width), F32)] * 3,
        mib=16,
        flops=2 * length * head_width * (3 * model + 5 * length),
    )
    input_parts = reduce_seq(input_parts)


    attn_keep, attn_send = call(
        attention_weights,
        [
            ((CHIPS, shard + PAD, model), F32),
            ((CHIPS, shard + PAD, model), BF16),
        ],
        [ids],
        grad_qkv,
        *x_blocks,
        attn,
        *grad_attn,
        sums,
        scratch=[
            ((length, model), BF16),
            ((length, head_width), BF16),
            ((model, head_width), F32),
            ((model, model), F32),
        ],
        mib=16,
        flops=2 * length * model * model,
    )

    grad_gate_up_w, grad_down_w = call(
        feed_final,
        [(w_gate_up.shape, F32), (w_down.shape, F32)],
        [ids],
        *feed_blocks,
        mib=10,
    )
    attn_pieces = pair(attn_keep, attn_send)
    attn_pieces = [attn_pieces[0]] + [swap(attn_pieces[t], 2 * t) for t in range(1, CHIPS)]
    attn_pieces = after(attn_pieces, input_parts, feed_blocks[1:3])
    (attn_share,) = call(plane_sum, [((shard + PAD, model), BF16)], [], *attn_pieces)
    grad_qkv_w, grad_out_w, vector_grads = call(
        attention_final,
        [((shard, 3 * model), F32), ((shard, model), F32), ((8, 128), F32)],
        [ids],
        *gather_seq(attn_share),
        scratch=[((SEQ, shard + PAD, model), F32)],
    )

    input_grad, means = call(
        input_final,
        [((rows, model), BF16), ((8, 128), F32)],
        [],
        grad_first,
        *input_parts,
        stats2,
        *grad_attn[1:],
    )
    vector_grads = [scatter_outer(vector_grads[n, :shard]) for n in range(4)]
    return (
        output[None],
        input_grad[None],
        scatter_outer(grad_qkv_w),
        scatter_outer(grad_out_w),
        vector_grads[0],
        vector_grads[1],
        scatter_outer(grad_gate_up_w),
        scatter_outer(grad_down_w),
        vector_grads[2],
        vector_grads[3],
        means[0:1, 0:4],
    )


def solution(mesh):
    return jax.shard_map(
        body,
        mesh=mesh,
        in_specs=(
            P("dp", "seq", None),
            P("dp", None),
            P("dp", None),
            P("dp"),
            P("dp"),
            P("dp", None),
            P("dp", None),
            P("dp"),
            P("dp"),
            P("dp", None),
            P("dp", "seq", None),
        ),
        out_specs=(
            P("dp", "seq", None),
            P("dp", "seq", None),
            P("dp", None),
            P("dp", None),
            P("dp"),
            P("dp"),
            P("dp", None),
            P("dp", None),
            P("dp"),
            P("dp"),
            P("dp", None),
        ),
        check_vma=False,
    )
```

```python
import math

import jax
import jax.numpy as jnp
import numpy as np
from jax import lax
from jax.experimental import pallas as pl
from jax.experimental.pallas import tpu as pltpu
from jax.sharding import PartitionSpec as P

HEADS = 12
HEAD_DIM = 64
NORM_EPSILON = 1e-05
GELU_C = 0.7978845608028654
GELU_A = 0.044715
INNER = 8
CHIPS = 4
SEQ = 4
PAD = 16

F32 = jnp.float32
BF16 = jnp.bfloat16
SLOPES = (2.0 ** (-8.0 * (np.arange(HEADS) + 1.0) / HEADS)).astype(np.float32)


def dot(left, right):
    return jnp.dot(left, right, preferred_element_type=F32)


def dot_nt(left, right):
    return lax.dot_general(left, right, (((1,), (1,)), ((), ())), preferred_element_type=F32)


def dot_tn(left, right):
    return lax.dot_general(left, right, (((0,), (0,)), ((), ())), preferred_element_type=F32)


def gelu_parts(value):
    square = value * value
    tanh = jnp.tanh(GELU_C * (value + GELU_A * square * value))
    half = 0.5 * (1.0 + tanh)
    slope = half + 0.5 * value * (1.0 - tanh * tanh) * (GELU_C * (1.0 + 3.0 * GELU_A * square))
    return value * half, slope


def gelu(value):
    return 0.5 * value * (1.0 + jnp.tanh(GELU_C * (value + GELU_A * value * value * value)))


def norm_parts(summed):
    centered = summed - jnp.mean(summed, axis=-1, keepdims=True)
    variance = jnp.mean(centered * centered, axis=-1, keepdims=True)
    inv_std = lax.rsqrt(variance + NORM_EPSILON)
    return centered * inv_std, inv_std


def norm_back(grad_in, normalized, inv_std, gain):
    scaled = grad_in * gain
    return inv_std * (
        scaled
        - jnp.mean(scaled, axis=-1, keepdims=True)
        - normalized * jnp.mean(scaled * normalized, axis=-1, keepdims=True)
    )


def column_sum(value):
    return jnp.sum(value, axis=0, keepdims=True)


def total(value):
    return jnp.sum(jnp.sum(value, axis=1, keepdims=True), axis=0, keepdims=True)


def at(start, size, step):
    return pl.ds(pl.multiple_of(start, step), size)


def call(kernel, outs, smem, *vmem, scratch=(), flops=0, mib=8, aliases=None):
    specs = [pl.BlockSpec(memory_space=pltpu.SMEM) for _ in smem]
    specs += [pl.BlockSpec(memory_space=pltpu.VMEM) for _ in vmem]
    out_shape = [jax.ShapeDtypeStruct(shape, dtype) for shape, dtype in outs]
    moved = sum(math.prod(a.shape) * a.dtype.itemsize for a in list(vmem) + out_shape)
    return pl.pallas_call(
        kernel,
        out_shape=out_shape,
        in_specs=specs,
        out_specs=[pl.BlockSpec(memory_space=pltpu.VMEM) for _ in outs],
        scratch_shapes=[pltpu.VMEM(shape, dtype) for shape, dtype in scratch],
        input_output_aliases=aliases or {},
        cost_estimate=pl.CostEstimate(flops=flops, transcendentals=0, bytes_accessed=moved),
        name=kernel.__name__,
        compiler_params=pltpu.CompilerParams(vmem_limit_bytes=mib << 20),
    )(*smem, *vmem)


def select_units(ids, gate_up, down, w_out, params, piece):
    z = ids[8]
    rows = w_out.shape[0]
    window = down.shape[0]
    units = window // SEQ
    model = w_out.shape[1]
    hidden = gate_up.shape[1] // 2
    group = lax.broadcasted_iota(jnp.int32, (rows, window), 1) // units
    for g in range(2):
        for w in range(model // window):
            acc = jnp.zeros((rows, window), F32)
            for i in range(SEQ):
                start = g * hidden + (SEQ * w + i) * window
                shift = lax.rem(units * (i - z) + window, window)
                moved = pltpu.roll(gate_up[:, start : start + window].astype(F32), shift, 1)
                acc = jnp.where(group == i, moved, acc)
            piece[g * rows : (g + 1) * rows, w * window : (w + 1) * window] = acc.astype(BF16)
    piece[2 * rows : 3 * rows, :] = down[at(z * units, units, 32), :]
    piece[3 * rows : 4 * rows, :] = w_out[...]
    piece[4 * rows :, :] = params[...]


def gather_weights(ids, *refs):
    blocks, odd = refs[0:4], refs[4]
    gate_up, down, w_out, vectors = refs[5:9]
    model = w_out.shape[0]
    rows = model // INNER
    size = blocks[0].shape[0]
    gathered = jnp.zeros((8, model), F32)
    for t in range(CHIPS):
        for s in range(2):
            start = ids[2 * t + s] * rows
            place = at(start, rows, 32)
            block = blocks[t] if s == 0 else odd.at[t * size : (t + 1) * size]
            gate_up[0, place, :] = block[0:rows, :]
            gate_up[1, place, :] = block[rows : 2 * rows, :]
            down[place, :] = block[2 * rows : 3 * rows, :]
            w_out[place, :] = block[3 * rows : 4 * rows, :]
            piece = block[4 * rows : 4 * rows + PAD, :].astype(F32)
            gathered = gathered + pltpu.roll(piece, start, 1)[0:8]
    vectors[...] = gathered


def attention_forward(ids, starts, slopes, *refs):
    x_blocks, w_blocks, odd = refs[0:4], refs[4:8], refs[8]
    packed, q_out, k_out, v_out, probs_out, w_qkv = refs[9:15]
    xs, attended = refs[15:17]
    rows = x_blocks[0].shape[0]
    length = SEQ * rows
    model = w_qkv.shape[1]
    width = w_qkv.shape[2]
    shard = model // INNER
    for t in range(CHIPS):
        for s in range(2):
            place = at(ids[2 * t + s] * shard, shard, 32)
            block = w_blocks[t] if s == 0 else odd.at[t * shard : (t + 1) * shard]
            for part in range(3):
                w_qkv[part, place, :] = block[:, part * width : (part + 1) * width]
    for s in range(SEQ):
        xs[s * rows : (s + 1) * rows, :] = x_blocks[s][...]
    joint = xs[...]
    q_out[...] = dot(joint, w_qkv[0]).astype(BF16)
    k_out[...] = dot(joint, w_qkv[1]).astype(BF16)
    v_out[...] = dot(joint, w_qkv[2]).astype(BF16)
    keys = k_out[...]
    values = v_out[...]
    heads = width // HEAD_DIM
    z = ids[8]

    def doc_of(position):
        count = jnp.zeros(position.shape, jnp.int32)
        for n in range(starts.shape[1]):
            count = count + (starts[0, n] <= position).astype(jnp.int32)
        return count

    lane = lax.broadcasted_iota(jnp.int32, (1, length), 1)
    key_pos = (jnp.bitwise_xor(lane // rows, z)) * rows + lane % rows
    key_docs = doc_of(key_pos)
    head_of = lax.broadcasted_iota(jnp.int32, (1, width), 1) // HEAD_DIM
    head_values = [jnp.where(head_of == h, values, jnp.zeros_like(values)) for h in range(heads)]

    def one_block(s, carry):
        place = at(s * rows, rows, 128)
        query_pos = ids[8 + s] * rows + lax.broadcasted_iota(jnp.int32, (rows, 1), 0)
        distance = jnp.abs(query_pos - key_pos).astype(F32)
        same_doc = doc_of(query_pos) == key_docs
        block = q_out[place, :] * BF16(1.0 / math.sqrt(HEAD_DIM))
        total_out = jnp.zeros((rows, width), F32)
        for h in range(heads):
            query = jnp.where(head_of == h, block, jnp.zeros_like(block))
            scores = dot_nt(query, keys) - slopes[z * heads + h] * distance
            scores = jnp.where(same_doc, scores, -1e30)
            expon = jnp.exp(scores - jnp.max(scores, axis=-1, keepdims=True))
            probs = (expon / jnp.sum(expon, axis=-1, keepdims=True)).astype(BF16)
            probs_out[h, place, :] = probs
            total_out = total_out + dot(probs, head_values[h])
        attended[place, :] = total_out.astype(BF16)
        return carry

    lax.fori_loop(0, SEQ, one_block, 0)
    half = length // 2
    packed[0:length, :] = attended[:, 0:128]
    packed[length:, 0:64] = attended[0:half, 128:192]
    packed[length:, 64:128] = attended[half:, 128:192]


def middle_forward(ids, *refs):
    packs, x_blocks = refs[0:4], refs[4:8]
    w_out, vectors, gate_up, down = refs[8:12]
    outs = refs[12:16]
    first_ref, normed_ref, stats_ref, attn = refs[16:20]
    acc = refs[20]
    rows = x_blocks[0].shape[0]
    length = SEQ * rows
    width = attn.shape[2]
    for t in range(SEQ):
        for u in range(SEQ):
            place = slice(u * rows, (u + 1) * rows)
            b = t ^ u
            attn[t, place, 0:128] = packs[t][b * rows : (b + 1) * rows, :]
            start = length + (b % 2) * rows
            attn[t, place, 128:192] = packs[t][start : start + rows, (b // 2) * 64 : (b // 2) * 64 + 64]
    w_parts = [w_out[at(ids[8 + t] * width, width, 64), :] for t in range(SEQ)]
    for u in range(SEQ):
        place = slice(u * rows, (u + 1) * rows)
        branch = dot(attn[0, place, :], w_parts[0])
        for t in range(1, SEQ):
            branch = branch + dot(attn[t, place, :], w_parts[t])
        first_sum = x_blocks[u][...].astype(F32) + branch
        normalized, _ = norm_parts(first_sum)
        normed_ref[place, :] = (normalized * vectors[0:1, :] + vectors[1:2, :]).astype(BF16)
        if u == 0:
            first_ref[...] = first_sum
            lane = lax.broadcasted_iota(jnp.int32, stats_ref.shape, 1)
            stats_ref[...] = jnp.where(lane == 0, total(branch * branch), 0.0) + jnp.where(
                lane == 1, total(first_sum * first_sum), 0.0
            )
    normed = normed_ref[...]
    step = 256
    for start in range(0, down.shape[0], step):
        cols = slice(start, start + step)
        gate = dot(normed, gate_up[0, :, cols])
        up = dot(normed, gate_up[1, :, cols])
        hidden = (gelu(gate) * up).astype(BF16)
        part = dot(hidden, down[cols, :])
        if start == 0:
            acc[...] = part
        else:
            acc[...] += part
    for s in range(SEQ):
        outs[s][...] = acc[s * rows : (s + 1) * rows, :].astype(outs[s].dtype)


def final_norm(*refs):
    parts = refs[0:4]
    normed_ref, cot_ref, vectors, stats_in = refs[4:8]
    out_ref, grad_feed_ref, grad_second_ref, sums_ref, stats_ref = refs[8:13]
    feed_out = parts[0][...]
    for s in range(1, CHIPS):
        feed_out = feed_out + parts[s][...].astype(F32)
    second = normed_ref[0 : cot_ref.shape[0], :].astype(F32) + feed_out
    normalized, inv_std = norm_parts(second)
    gain = vectors[2:3, :]
    out_ref[...] = (normalized * gain + vectors[3:4, :]).astype(BF16)
    grad = cot_ref[...].astype(F32)
    grad_second = norm_back(grad, normalized, inv_std, gain)
    grad_second_ref[...] = grad_second
    grad_feed_ref[...] = grad_second.astype(BF16)
    sums_ref[0:1, :] = column_sum(grad * normalized)
    sums_ref[1:2, :] = column_sum(grad)
    sums_ref[2:8, :] = jnp.zeros((6, gain.shape[1]), F32)
    lane = lax.broadcasted_iota(jnp.int32, stats_ref.shape, 1)
    stats_ref[...] = (
        stats_in[...]
        + jnp.where(lane == 2, total(feed_out * feed_out), 0.0)
        + jnp.where(lane == 3, total(second * second), 0.0)
    )


def feed_back(*refs):
    normed_ref, grad_blocks = refs[0], refs[1:5]
    gate_up, down = refs[5:7]
    outs = refs[7:11]
    hidden_ref, dgate_ref, dup_ref, grads = refs[11:15]
    acc = refs[15]
    rows = grad_blocks[0].shape[0]
    for s in range(SEQ):
        grads[s * rows : (s + 1) * rows, :] = grad_blocks[s][...]
    normed = normed_ref[...]
    grad_feed = grads[...]
    step = 256
    for start in range(0, down.shape[0], step):
        cols = slice(start, start + step)
        gate = dot(normed, gate_up[0, :, cols])
        up = dot(normed, gate_up[1, :, cols])
        grad_hidden = dot_nt(grad_feed, down[cols, :])
        act, slope = gelu_parts(gate)
        hidden_ref[:, cols] = (act * up).astype(BF16)
        dgate = (grad_hidden * up * slope).astype(BF16)
        dup = (grad_hidden * act).astype(BF16)
        dgate_ref[:, cols] = dgate
        dup_ref[:, cols] = dup
        part = dot_nt(dgate, gate_up[0, :, cols]) + dot_nt(dup, gate_up[1, :, cols])
        if start == 0:
            acc[...] = part
        else:
            acc[...] += part
    for s in range(SEQ):
        outs[s][...] = acc[s * rows : (s + 1) * rows, :].astype(outs[s].dtype)


def split_rows(ids, acc, keep, send, where):
    shard = acc.shape[0] // INNER
    for t in range(CHIPS):
        keep[(t,) + where] = acc[at(ids[2 * t] * shard, shard, 32), :]
        send[(t,) + where] = acc[at(ids[2 * t + 1] * shard, shard, 32), :].astype(BF16)


def feed_weights(ids, *refs):
    normed, grads, hidden, dgate, dup = refs[0:5]
    keep, send = refs[5:7]
    acc = refs[7]
    for n, (left, right) in enumerate(((normed, dgate), (normed, dup), (hidden, grads))):
        acc[...] = dot_tn(left[...], right[...])
        split_rows(ids, acc, keep, send, (n,))


def pair_sum(*refs):
    keep, received = refs[0:2]
    for t in range(CHIPS):
        refs[2 + t][...] = (keep[t] + received[t].astype(F32)).astype(refs[2 + t].dtype)


def step_one(*refs):
    keep, received = refs[0:2]
    left, left_next, right, right_next, to_x, to_y = refs[2:8]
    half = left.shape[-1]

    def part(t, side):
        cols = slice(side * half, (side + 1) * half)
        return keep[t, :, :, cols] + received[t, :, :, cols].astype(F32)

    left[...] = part(0, 0)
    left_next[...] = part(2, 0)
    right[...] = part(0, 1)
    right_next[...] = part(1, 1)
    to_x[0] = part(1, 0).astype(BF16)
    to_x[1] = part(3, 0).astype(BF16)
    to_y[0] = part(2, 1).astype(BF16)
    to_y[1] = part(3, 1).astype(BF16)


def step_two(*refs):
    left, left_next, right, right_next, from_x, from_y = refs[0:6]
    left_out, right_out, to_y, to_x = refs[6:10]
    left_out[...] = left[...] + from_x[0].astype(F32)
    to_y[...] = (left_next[...] + from_x[1].astype(F32)).astype(BF16)
    right_out[...] = right[...] + from_y[0].astype(F32)
    to_x[...] = (right_next[...] + from_y[1].astype(F32)).astype(BF16)


def step_three(*refs):
    left, right, from_y, from_x, out = refs
    half = left.shape[-1]
    out[:, :, 0:half] = (left[...] + from_y[...].astype(F32)).astype(BF16)
    out[:, :, half:] = (right[...] + from_x[...].astype(F32)).astype(BF16)


def plane_sum(*refs):
    out = refs[-1]
    acc = refs[0][...].astype(F32)
    for ref in refs[1:-1]:
        acc = acc + ref[...].astype(F32)
    out[...] = acc.astype(out.dtype)


def feed_final(ids, *refs):
    blocks, out, down_out = refs[0:4], refs[4], refs[5]
    rows, model = blocks[0].shape[1:]
    hidden = out.shape[1] // 2
    window = hidden // INNER
    units = window // SEQ
    group = lax.broadcasted_iota(jnp.int32, (rows, window), 1) // units
    for g in range(2):
        for w in range(model // window):
            parts = [b[g, :, w * window : (w + 1) * window].astype(F32) for b in blocks]
            for i in range(SEQ):
                acc = jnp.zeros((rows, window), F32)
                for s in range(SEQ):
                    pos = ids[8 + s]
                    shift = lax.rem(units * (pos - i) + window, window)
                    acc = jnp.where(group == pos, pltpu.roll(parts[s], shift, 1), acc)
                start = g * hidden + (SEQ * w + i) * window
                out[:, start : start + window] = acc
    for s in range(SEQ):
        down_out[at(ids[8 + s] * units, units, 32), :] = blocks[s][2].astype(F32)


def project_back(ids, *refs):
    parts = refs[0:4]
    grad_second, first_ref, vectors, w_out = refs[4:8]
    sums_in, stats_ref = refs[8:10]
    grad_first_ref = refs[10]
    grad_outs, sums_ref = refs[11:15], refs[15]
    grad = grad_second[...] + parts[0][...]
    for s in range(1, SEQ):
        grad = grad + parts[s][...].astype(F32)
    normalized, inv_std = norm_parts(first_ref[...])
    grad_first = norm_back(grad, normalized, inv_std, vectors[0:1, :])
    grad_first_ref[...] = grad_first
    grad_branch = grad_first.astype(BF16)
    rows, model = grad_branch.shape
    width = grad_outs[0].shape[1] // 2
    high = stats_ref[...].astype(BF16)
    low = (stats_ref[...] - high.astype(F32)).astype(BF16)
    stats_rows = jnp.concatenate([high, low], axis=0)
    stats_rows = jnp.concatenate([stats_rows, jnp.zeros((PAD, 2 * width - 128), BF16)], axis=1)
    row = lax.broadcasted_iota(jnp.int32, (model, width), 0)
    column = lax.broadcasted_iota(jnp.int32, (model, width), 1)
    for s in range(SEQ):
        start = ids[8 + s] * width
        mine = w_out[at(start, width, 64), :]
        grad_outs[s][0:rows, 0:width] = dot_nt(grad_branch, mine).astype(BF16)
        grad_outs[s][rows : rows + PAD, :] = stats_rows
        chosen = (row == start + column).astype(F32).astype(BF16)
        grad_outs[s][0:rows, width:] = dot(grad_branch, chosen).astype(BF16)
    sums_ref[0:1, :] = column_sum(grad * normalized)
    sums_ref[1:2, :] = column_sum(grad)
    sums_ref[2:4, :] = sums_in[0:2, :]
    sums_ref[4:PAD, :] = jnp.zeros((PAD - 4, model), F32)


def attention_back(*refs):
    grad_blocks = refs[0:4]
    q_ref, k_ref, v_ref, probs_ref, w_qkv = refs[4:9]
    outs, grad_qkv = refs[9:13], refs[13]
    grads, grad_q, grad_k, grad_v = refs[14:18]
    rows = outs[0].shape[0]
    for s in range(SEQ):
        place = slice(s * rows, (s + 1) * rows)
        grads[place, :] = grad_blocks[s][0:rows, 0 : grads.shape[1]]
    queries, keys, values = q_ref[...], k_ref[...], v_ref[...]
    width = keys.shape[1]
    heads = width // HEAD_DIM
    head_of = lax.broadcasted_iota(jnp.int32, (1, width), 1) // HEAD_DIM
    scale = 1.0 / math.sqrt(HEAD_DIM)
    for h in range(heads):
        mine = head_of == h
        head_keys = jnp.where(mine, keys, jnp.zeros_like(keys))
        for s in range(SEQ):
            place = slice(s * rows, (s + 1) * rows)
            grad_out = jnp.where(mine, grads[place, :], jnp.zeros((rows, width), BF16))
            query = jnp.where(mine, queries[place, :], jnp.zeros((rows, width), BF16))
            probs_low = probs_ref[h, place, :]
            probs = probs_low.astype(F32)
            grad_probs = dot_nt(grad_out, values)
            delta = jnp.sum(probs * grad_probs, axis=-1, keepdims=True)
            grad_scores = (probs * (grad_probs - delta)).astype(BF16)
            dq = dot(grad_scores, head_keys)
            dk = dot_tn(grad_scores, query)
            dv = dot_tn(probs_low, grad_out)
            if h == 0:
                grad_q[place, :] = dq
            else:
                grad_q[place, :] += dq
            if h == 0 and s == 0:
                grad_k[...] = dk
                grad_v[...] = dv
            else:
                grad_k[...] += dk
                grad_v[...] += dv
    low = (
        (grad_q[...] * scale).astype(BF16),
        (grad_k[...] * scale).astype(BF16),
        grad_v[...].astype(BF16),
    )
    grad_input = dot_nt(low[0], w_qkv[0]) + dot_nt(low[1], w_qkv[1]) + dot_nt(low[2], w_qkv[2])
    for s in range(SEQ):
        outs[s][...] = grad_input[s * rows : (s + 1) * rows, :].astype(outs[s].dtype)
    for part in range(3):
        grad_qkv[:, part * width : (part + 1) * width] = low[part]


def attention_weights(ids, *refs):
    grad_qkv, x_blocks, attn, columns = refs[0], refs[1:5], refs[5], refs[6:10]
    sums = refs[10]
    keep, send = refs[11:13]
    xs, grads, out_acc, acc = refs[13:17]
    rows = x_blocks[0].shape[0]
    width = grads.shape[1]
    for s in range(SEQ):
        place = slice(s * rows, (s + 1) * rows)
        xs[place, :] = x_blocks[s][...]
        grads[place, :] = columns[s][0:rows, width:]
    for t in range(SEQ):
        out_acc[at(ids[8 + t] * width, width, 64), :] = dot_tn(attn[t], grads[...])
    acc[:, 0 : 3 * width] = dot_tn(xs[...], grad_qkv[...])
    acc[:, 3 * width : 4 * width] = out_acc[...]
    shard = acc.shape[0] // INNER
    split_rows(ids, acc, keep, send, (slice(0, shard),))
    for t in range(CHIPS):
        keep[t, shard : shard + PAD, :] = sums[...]
        send[t, shard : shard + PAD, :] = sums[...].astype(BF16)


def input_final(*refs):
    grad_first, parts, stats_in, grad_blocks = refs[0], refs[1:5], refs[5], refs[6:9]
    out, means = refs[9:11]
    acc = grad_first[...] + parts[0][...]
    for s in range(1, SEQ):
        acc = acc + parts[s][...].astype(F32)
    out[...] = acc.astype(BF16)
    rows, model = out.shape
    stats = stats_in[...]
    for ref in grad_blocks:
        extra = ref[rows : rows + PAD, 0:128].astype(F32)
        stats = stats + (extra[0:8] + extra[8:16])
    means[...] = jnp.sqrt(stats * (1.0 / (SEQ * rows * model)))


def attention_final(ids, *refs):
    blocks, qkv_out, out, vectors, stage = refs[0:4], refs[4], refs[5], refs[6], refs[7]
    for s in range(SEQ):
        stage[ids[8 + s]] = blocks[s][...].astype(F32)
    shard, model = out.shape
    width = model // SEQ
    for pos in range(SEQ):
        for part in range(3):
            start = (part * SEQ + pos) * width
            qkv_out[:, start : start + width] = stage[pos, 0:shard, part * width : (part + 1) * width]
        out[:, pos * width : (pos + 1) * width] = stage[pos, 0:shard, 3 * width : 4 * width]
    sums = stage[0, shard : shard + 8, :]
    for pos in range(1, SEQ):
        sums = sums + stage[pos, shard : shard + 8, :]
    shift = model - ids[0] * shard
    vectors[...] = pltpu.roll(sums, lax.rem(shift, model), 1)[:, 0:128]


def after(values, *deps):
    return lax.optimization_barrier((values, deps))[0]


def body(
    layer_input,
    w_qkv,
    w_out,
    ln1_gain,
    ln1_bias,
    w_gate_up,
    w_down,
    ln2_gain,
    ln2_bias,
    doc_starts,
    cotangent,
):
    dp = lax.axis_size("dp")
    stride = dp // INNER
    rows, model = layer_input.shape[1:]
    columns = tuple(tuple(range(g * stride, (g + 1) * stride)) for g in range(INNER))
    cores = tuple(
        tuple((2 * t + core) * stride + r for t in range(CHIPS))
        for core in range(2)
        for r in range(stride)
    )

    def gather_outer(value):
        if stride == 1:
            return value
        return lax.all_gather(value, "dp", axis=0, tiled=True, axis_index_groups=columns)

    def scatter_outer(value):
        if stride == 1:
            return value
        return lax.psum_scatter(
            value, "dp", scatter_dimension=0, tiled=True, axis_index_groups=columns
        )

    def swap(value, s):
        return lax.ppermute(value, "dp", [(i, i ^ (s * stride)) for i in range(dp)])

    def pass_seq(value, s):
        return lax.ppermute(value, "seq", [(i, i ^ s) for i in range(SEQ)])

    def gather_seq(value):
        far = pass_seq(value, 2)
        near = pass_seq(value, 1)
        return [value, near, far, pass_seq(far, 1)]

    def reduce_seq(pieces):
        return [pieces[0]] + [pass_seq(pieces[s], s) for s in range(1, SEQ)]

    j = lax.axis_index("dp") // stride
    z = lax.axis_index("seq")
    ids = jnp.concatenate(
        [
            jnp.bitwise_xor(j, jnp.arange(INNER, dtype=jnp.int32)),
            jnp.bitwise_xor(z, jnp.arange(SEQ, dtype=jnp.int32)),
        ]
    )
    slopes = jnp.asarray(SLOPES)

    w_qkv, w_out, w_gate_up, w_down = map(gather_outer, (w_qkv, w_out, w_gate_up, w_down))
    vectors = [gather_outer(v) for v in (ln1_gain, ln1_bias, ln2_gain, ln2_bias)]
    shard = w_out.shape[0]
    head_width = HEADS // SEQ * HEAD_DIM

    x_own = layer_input[0]
    x_blocks = gather_seq(x_own)

    own_qkv = jnp.concatenate(
        [
            lax.dynamic_slice(w_qkv, (0, part * model + z * head_width), (shard, head_width))
            for part in range(3)
        ],
        axis=1,
    )
    qkv_even = [own_qkv] + [swap(own_qkv, s) for s in (2, 4, 6)]
    qkv_odd = swap(jnp.concatenate(qkv_even, axis=0), 1)

    params = jnp.pad(jnp.stack(vectors, axis=0), ((0, PAD - 4), (0, model - shard)))
    (piece,) = call(
        select_units,
        [((4 * shard + PAD, model), BF16)],
        [ids],
        w_gate_up,
        w_down,
        w_out,
        params,
        mib=8,
    )
    piece = after(piece, qkv_even, x_blocks[1:3])
    feed_even = [piece] + [swap(piece, s) for s in (2, 4, 6)]

    length = SEQ * rows
    packed, queries, keys, values, probs, qkv_full = call(
        attention_forward,
        [((length * 3 // 2, 128), BF16)]
        + [((length, head_width), BF16)] * 3
        + [((HEADS // SEQ, length, length), BF16), ((3, model, head_width), BF16)],
        [ids, doc_starts, slopes],
        *x_blocks,
        *qkv_even,
        qkv_odd,
        scratch=[((length, model), BF16), ((length, head_width), BF16)],
        mib=16,
        flops=2 * length * head_width * (3 * model + 2 * length),
    )
    packs = gather_seq(packed)

    feed_even = after(feed_even, packs[1:3])
    feed_odd = swap(jnp.concatenate(feed_even, axis=0), 1)
    units = w_down.shape[0] // SEQ * INNER
    gate_up_full, down_full, out_full, norm_vectors = call(
        gather_weights,
        [
            ((2, model, units), BF16),
            ((units, model), BF16),
            ((model, model), BF16),
            ((8, model), F32),
        ],
        [ids],
        *feed_even,
        feed_odd,
        mib=16,
    )

    shares = [((rows, model), F32)] + [((rows, model), BF16)] * 3
    *feed_parts, first_sum, normed, stats1, attn = call(
        middle_forward,
        shares
        + [
            ((rows, model), F32),
            ((length, model), BF16),
            ((8, 128), F32),
            ((SEQ, length, head_width), BF16),
        ],
        [ids],
        *packs,
        *x_blocks,
        out_full,
        norm_vectors,
        gate_up_full,
        down_full,
        scratch=[((length, model), F32)],
        mib=16,
        flops=2 * length * model * (model + 3 * units),
    )

    output, grad_feed, grad_second, sums2, stats2 = call(
        final_norm,
        [
            ((rows, model), BF16),
            ((rows, model), BF16),
            ((rows, model), F32),
            ((8, model), F32),
            ((8, 128), F32),
        ],
        [],
        *reduce_seq(feed_parts),
        normed,
        cotangent[0],
        norm_vectors,
        stats1,
    )

    *back_parts, hidden, dgate, dup, grads = call(
        feed_back,
        shares + [((length, units), BF16)] * 3 + [((length, model), BF16)],
        [],
        normed,
        *gather_seq(grad_feed),
        gate_up_full,
        down_full,
        scratch=[((length, model), F32)],
        mib=18,
        flops=10 * length * model * units,
    )
    back_parts = reduce_seq(back_parts)

    feed_keep, feed_send = call(
        feed_weights,
        [((CHIPS, 3, shard, model), F32), ((CHIPS, 3, shard, model), BF16)],
        [ids],
        normed,
        grads,
        hidden,
        dgate,
        dup,
        scratch=[((model, model), F32)],
        mib=18,
        flops=6 * length * model * units,
    )

    def pair(keep, send):
        shape = keep.shape[1:]
        return call(pair_sum, [(shape, F32)] + [(shape, BF16)] * 3, [], keep, swap(send, 1))

    half_shape = (3, shard, model // 2)
    grad_first, *projected = call(
        project_back,
        [((rows, model), F32)]
        + [((rows + PAD, 2 * head_width), BF16)] * SEQ
        + [((PAD, model), F32)],
        [ids],
        *back_parts,
        grad_second,
        first_sum,
        norm_vectors,
        out_full,
        sums2,
        stats2,
        mib=10,
        flops=4 * rows * model * model,
    )
    grad_attn = reduce_seq(projected[0:4])
    *feed_pieces, to_x, to_y = call(
        step_one,
        [(half_shape, F32)] * 4 + [((2,) + half_shape, BF16)] * 2,
        [],
        after(feed_keep, grad_first),
        swap(feed_send, 1),
        mib=10,
    )
    left, right, to_y, to_x = call(
        step_two,
        [(half_shape, F32)] * 2 + [(half_shape, BF16)] * 2,
        [],
        *after(feed_pieces, grad_attn),
        swap(to_x, 2),
        swap(to_y, 4),
        mib=10,
    )

    sums = projected[4]
    (feed_share,) = call(
        step_three, [((3, shard, model), BF16)], [], left, right, swap(to_y, 4), swap(to_x, 2)
    )
    sums = after(sums, feed_share)
    feed_blocks = gather_seq(after(feed_share, grad_attn))

    *input_parts, grad_qkv = call(
        attention_back,
        shares + [((length, 3 * head_width), BF16)],
        [],
        *grad_attn,
        queries,
        keys,
        values,
        probs,
        qkv_full,
        scratch=[((length, head_width), BF16)] + [((length, head_width), F32)] * 3,
        mib=16,
        flops=2 * length * head_width * (3 * model + 5 * length),
    )
    input_parts = reduce_seq(input_parts)


    attn_keep, attn_send = call(
        attention_weights,
        [
            ((CHIPS, shard + PAD, model), F32),
            ((CHIPS, shard + PAD, model), BF16),
        ],
        [ids],
        grad_qkv,
        *x_blocks,
        attn,
        *grad_attn,
        sums,
        scratch=[
            ((length, model), BF16),
            ((length, head_width), BF16),
            ((model, head_width), F32),
            ((model, model), F32),
        ],
        mib=16,
        flops=2 * length * model * model,
    )

    grad_gate_up_w, grad_down_w = call(
        feed_final,
        [(w_gate_up.shape, F32), (w_down.shape, F32)],
        [ids],
        *feed_blocks,
        mib=10,
    )
    attn_pieces = pair(attn_keep, attn_send)
    attn_pieces = [attn_pieces[0]] + [swap(attn_pieces[t], 2 * t) for t in range(1, CHIPS)]
    attn_pieces = after(attn_pieces, input_parts, feed_blocks[1:3])
    (attn_share,) = call(plane_sum, [((shard + PAD, model), BF16)], [], *attn_pieces)
    input_grad, means = call(
        input_final,
        [((rows, model), BF16), ((8, 128), F32)],
        [],
        grad_first,
        *input_parts,
        stats2,
        *grad_attn[1:],
    )
    attn_near = pass_seq(attn_share, 1)
    attn_far = after(pass_seq(attn_share, 2), grad_gate_up_w, input_grad)
    grad_qkv_w, grad_out_w, vector_grads = call(
        attention_final,
        [((shard, 3 * model), F32), ((shard, model), F32), ((8, 128), F32)],
        [ids],
        attn_share,
        attn_near,
        attn_far,
        pass_seq(attn_far, 1),
        scratch=[((SEQ, shard + PAD, model), F32)],
    )

    vector_grads = [scatter_outer(vector_grads[n, :shard]) for n in range(4)]
    return (
        output[None],
        input_grad[None],
        scatter_outer(grad_qkv_w),
        scatter_outer(grad_out_w),
        vector_grads[0],
        vector_grads[1],
        scatter_outer(grad_gate_up_w),
        scatter_outer(grad_down_w),
        vector_grads[2],
        vector_grads[3],
        means[0:1, 0:4],
    )


def solution(mesh):
    return jax.shard_map(
        body,
        mesh=mesh,
        in_specs=(
            P("dp", "seq", None),
            P("dp", None),
            P("dp", None),
            P("dp"),
            P("dp"),
            P("dp", None),
            P("dp", None),
            P("dp"),
            P("dp"),
            P("dp", None),
            P("dp", "seq", None),
        ),
        out_specs=(
            P("dp", "seq", None),
            P("dp", "seq", None),
            P("dp", None),
            P("dp", None),
            P("dp"),
            P("dp"),
            P("dp", None),
            P("dp", None),
            P("dp"),
            P("dp"),
            P("dp", None),
        ),
        check_vma=False,
    )
```

```python
import math

import jax
import jax.numpy as jnp
import numpy as np
from jax import lax
from jax.experimental import pallas as pl
from jax.experimental.pallas import tpu as pltpu
from jax.sharding import PartitionSpec as P

HEADS = 12
HEAD_DIM = 64
NORM_EPSILON = 1e-05
GELU_C = 0.7978845608028654
GELU_A = 0.044715
INNER = 8
CHIPS = 4
SEQ = 4
PAD = 16

F32 = jnp.float32
BF16 = jnp.bfloat16
SLOPES = (2.0 ** (-8.0 * (np.arange(HEADS) + 1.0) / HEADS)).astype(np.float32)


def dot(left, right):
    return jnp.dot(left, right, preferred_element_type=F32)


def dot_nt(left, right):
    return lax.dot_general(left, right, (((1,), (1,)), ((), ())), preferred_element_type=F32)


def dot_tn(left, right):
    return lax.dot_general(left, right, (((0,), (0,)), ((), ())), preferred_element_type=F32)


def gelu_parts(value):
    square = value * value
    tanh = jnp.tanh(GELU_C * (value + GELU_A * square * value))
    half = 0.5 * (1.0 + tanh)
    slope = half + 0.5 * value * (1.0 - tanh * tanh) * (GELU_C * (1.0 + 3.0 * GELU_A * square))
    return value * half, slope


def gelu(value):
    return 0.5 * value * (1.0 + jnp.tanh(GELU_C * (value + GELU_A * value * value * value)))


def norm_parts(summed):
    centered = summed - jnp.mean(summed, axis=-1, keepdims=True)
    variance = jnp.mean(centered * centered, axis=-1, keepdims=True)
    inv_std = lax.rsqrt(variance + NORM_EPSILON)
    return centered * inv_std, inv_std


def norm_back(grad_in, normalized, inv_std, gain):
    scaled = grad_in * gain
    return inv_std * (
        scaled
        - jnp.mean(scaled, axis=-1, keepdims=True)
        - normalized * jnp.mean(scaled * normalized, axis=-1, keepdims=True)
    )


def column_sum(value):
    return jnp.sum(value, axis=0, keepdims=True)


def total(value):
    return jnp.sum(jnp.sum(value, axis=1, keepdims=True), axis=0, keepdims=True)


def at(start, size, step):
    return pl.ds(pl.multiple_of(start, step), size)


def call(kernel, outs, smem, *vmem, scratch=(), flops=0, mib=8, aliases=None):
    specs = [pl.BlockSpec(memory_space=pltpu.SMEM) for _ in smem]
    specs += [pl.BlockSpec(memory_space=pltpu.VMEM) for _ in vmem]
    out_shape = [jax.ShapeDtypeStruct(shape, dtype) for shape, dtype in outs]
    moved = sum(math.prod(a.shape) * a.dtype.itemsize for a in list(vmem) + out_shape)
    return pl.pallas_call(
        kernel,
        out_shape=out_shape,
        in_specs=specs,
        out_specs=[pl.BlockSpec(memory_space=pltpu.VMEM) for _ in outs],
        scratch_shapes=[pltpu.VMEM(shape, dtype) for shape, dtype in scratch],
        input_output_aliases=aliases or {},
        cost_estimate=pl.CostEstimate(flops=flops, transcendentals=0, bytes_accessed=moved),
        name=kernel.__name__,
        compiler_params=pltpu.CompilerParams(vmem_limit_bytes=mib << 20),
    )(*smem, *vmem)


def select_units(ids, gate_up, down, w_out, params, piece):
    z = ids[8]
    rows = w_out.shape[0]
    window = down.shape[0]
    units = window // SEQ
    model = w_out.shape[1]
    hidden = gate_up.shape[1] // 2
    group = lax.broadcasted_iota(jnp.int32, (rows, window), 1) // units
    for g in range(2):
        for w in range(model // window):
            acc = jnp.zeros((rows, window), F32)
            for i in range(SEQ):
                start = g * hidden + (SEQ * w + i) * window
                shift = lax.rem(units * (i - z) + window, window)
                moved = pltpu.roll(gate_up[:, start : start + window].astype(F32), shift, 1)
                acc = jnp.where(group == i, moved, acc)
            piece[g * rows : (g + 1) * rows, w * window : (w + 1) * window] = acc.astype(BF16)
    piece[2 * rows : 3 * rows, :] = down[at(z * units, units, 32), :]
    piece[3 * rows : 4 * rows, :] = w_out[...]
    piece[4 * rows :, :] = params[...]


def gather_weights(ids, *refs):
    blocks, odd = refs[0:4], refs[4]
    gate_up, down, w_out, vectors = refs[5:9]
    model = w_out.shape[0]
    rows = model // INNER
    size = blocks[0].shape[0]
    gathered = jnp.zeros((8, model), F32)
    for t in range(CHIPS):
        for s in range(2):
            start = ids[2 * t + s] * rows
            place = at(start, rows, 32)
            block = blocks[t] if s == 0 else odd.at[t * size : (t + 1) * size]
            gate_up[0, place, :] = block[0:rows, :]
            gate_up[1, place, :] = block[rows : 2 * rows, :]
            down[place, :] = block[2 * rows : 3 * rows, :]
            w_out[place, :] = block[3 * rows : 4 * rows, :]
            piece = block[4 * rows : 4 * rows + PAD, :].astype(F32)
            gathered = gathered + pltpu.roll(piece, start, 1)[0:8]
    vectors[...] = gathered


def attention_forward(ids, starts, slopes, *refs):
    x_blocks, w_blocks, odd = refs[0:4], refs[4:8], refs[8]
    packed, q_out, k_out, v_out, probs_out, w_qkv = refs[9:15]
    xs, attended = refs[15:17]
    rows = x_blocks[0].shape[0]
    length = SEQ * rows
    model = w_qkv.shape[1]
    width = w_qkv.shape[2]
    shard = model // INNER
    for t in range(CHIPS):
        for s in range(2):
            place = at(ids[2 * t + s] * shard, shard, 32)
            block = w_blocks[t] if s == 0 else odd.at[t * shard : (t + 1) * shard]
            for part in range(3):
                w_qkv[part, place, :] = block[:, part * width : (part + 1) * width]
    for s in range(SEQ):
        xs[s * rows : (s + 1) * rows, :] = x_blocks[s][...]
    joint = xs[...]
    q_out[...] = dot(joint, w_qkv[0]).astype(BF16)
    k_out[...] = dot(joint, w_qkv[1]).astype(BF16)
    v_out[...] = dot(joint, w_qkv[2]).astype(BF16)
    keys = k_out[...]
    values = v_out[...]
    heads = width // HEAD_DIM
    z = ids[8]

    def doc_of(position):
        count = jnp.zeros(position.shape, jnp.int32)
        for n in range(starts.shape[1]):
            count = count + (starts[0, n] <= position).astype(jnp.int32)
        return count

    lane = lax.broadcasted_iota(jnp.int32, (1, length), 1)
    key_pos = (jnp.bitwise_xor(lane // rows, z)) * rows + lane % rows
    key_docs = doc_of(key_pos)
    head_of = lax.broadcasted_iota(jnp.int32, (1, width), 1) // HEAD_DIM
    head_values = [jnp.where(head_of == h, values, jnp.zeros_like(values)) for h in range(heads)]

    def one_block(s, carry):
        place = at(s * rows, rows, 128)
        query_pos = ids[8 + s] * rows + lax.broadcasted_iota(jnp.int32, (rows, 1), 0)
        distance = jnp.abs(query_pos - key_pos).astype(F32)
        same_doc = doc_of(query_pos) == key_docs
        block = q_out[place, :] * BF16(1.0 / math.sqrt(HEAD_DIM))
        total_out = jnp.zeros((rows, width), F32)
        for h in range(heads):
            query = jnp.where(head_of == h, block, jnp.zeros_like(block))
            scores = dot_nt(query, keys) - slopes[z * heads + h] * distance
            scores = jnp.where(same_doc, scores, -1e30)
            expon = jnp.exp(scores - jnp.max(scores, axis=-1, keepdims=True))
            probs = (expon / jnp.sum(expon, axis=-1, keepdims=True)).astype(BF16)
            probs_out[h, place, :] = probs
            total_out = total_out + dot(probs, head_values[h])
        attended[place, :] = total_out.astype(BF16)
        return carry

    lax.fori_loop(0, SEQ, one_block, 0)
    half = length // 2
    packed[0:length, :] = attended[:, 0:128]
    packed[length:, 0:64] = attended[0:half, 128:192]
    packed[length:, 64:128] = attended[half:, 128:192]


def middle_forward(ids, *refs):
    packs, x_blocks = refs[0:4], refs[4:8]
    w_out, vectors, gate_up, down = refs[8:12]
    outs = refs[12:16]
    first_ref, normed_ref, stats_ref, attn = refs[16:20]
    acc = refs[20]
    rows = x_blocks[0].shape[0]
    length = SEQ * rows
    width = attn.shape[2]
    for t in range(SEQ):
        for u in range(SEQ):
            place = slice(u * rows, (u + 1) * rows)
            b = t ^ u
            attn[t, place, 0:128] = packs[t][b * rows : (b + 1) * rows, :]
            start = length + (b % 2) * rows
            attn[t, place, 128:192] = packs[t][start : start + rows, (b // 2) * 64 : (b // 2) * 64 + 64]
    w_parts = [w_out[at(ids[8 + t] * width, width, 64), :] for t in range(SEQ)]
    for u in range(SEQ):
        place = slice(u * rows, (u + 1) * rows)
        branch = dot(attn[0, place, :], w_parts[0])
        for t in range(1, SEQ):
            branch = branch + dot(attn[t, place, :], w_parts[t])
        first_sum = x_blocks[u][...].astype(F32) + branch
        normalized, _ = norm_parts(first_sum)
        normed_ref[place, :] = (normalized * vectors[0:1, :] + vectors[1:2, :]).astype(BF16)
        if u == 0:
            first_ref[...] = first_sum
            lane = lax.broadcasted_iota(jnp.int32, stats_ref.shape, 1)
            stats_ref[...] = jnp.where(lane == 0, total(branch * branch), 0.0) + jnp.where(
                lane == 1, total(first_sum * first_sum), 0.0
            )
    normed = normed_ref[...]
    step = 256
    for start in range(0, down.shape[0], step):
        cols = slice(start, start + step)
        gate = dot(normed, gate_up[0, :, cols])
        up = dot(normed, gate_up[1, :, cols])
        hidden = (gelu(gate) * up).astype(BF16)
        part = dot(hidden, down[cols, :])
        if start == 0:
            acc[...] = part
        else:
            acc[...] += part
    for s in range(SEQ):
        outs[s][...] = acc[s * rows : (s + 1) * rows, :].astype(outs[s].dtype)


def final_norm(*refs):
    parts = refs[0:4]
    normed_ref, cot_ref, vectors, stats_in = refs[4:8]
    out_ref, grad_feed_ref, grad_second_ref, sums_ref, stats_ref = refs[8:13]
    feed_out = parts[0][...]
    for s in range(1, CHIPS):
        feed_out = feed_out + parts[s][...].astype(F32)
    second = normed_ref[0 : cot_ref.shape[0], :].astype(F32) + feed_out
    normalized, inv_std = norm_parts(second)
    gain = vectors[2:3, :]
    out_ref[...] = (normalized * gain + vectors[3:4, :]).astype(BF16)
    grad = cot_ref[...].astype(F32)
    grad_second = norm_back(grad, normalized, inv_std, gain)
    grad_second_ref[...] = grad_second
    grad_feed_ref[...] = grad_second.astype(BF16)
    sums_ref[0:1, :] = column_sum(grad * normalized)
    sums_ref[1:2, :] = column_sum(grad)
    sums_ref[2:8, :] = jnp.zeros((6, gain.shape[1]), F32)
    lane = lax.broadcasted_iota(jnp.int32, stats_ref.shape, 1)
    stats_ref[...] = (
        stats_in[...]
        + jnp.where(lane == 2, total(feed_out * feed_out), 0.0)
        + jnp.where(lane == 3, total(second * second), 0.0)
    )


def feed_back(*refs):
    normed_ref, grad_blocks = refs[0], refs[1:5]
    gate_up, down = refs[5:7]
    outs = refs[7:11]
    hidden_ref, dgate_ref, dup_ref, grads = refs[11:15]
    acc = refs[15]
    rows = grad_blocks[0].shape[0]
    for s in range(SEQ):
        grads[s * rows : (s + 1) * rows, :] = grad_blocks[s][...]
    normed = normed_ref[...]
    grad_feed = grads[...]
    step = 256
    for start in range(0, down.shape[0], step):
        cols = slice(start, start + step)
        gate = dot(normed, gate_up[0, :, cols])
        up = dot(normed, gate_up[1, :, cols])
        grad_hidden = dot_nt(grad_feed, down[cols, :])
        act, slope = gelu_parts(gate)
        hidden_ref[:, cols] = (act * up).astype(BF16)
        dgate = (grad_hidden * up * slope).astype(BF16)
        dup = (grad_hidden * act).astype(BF16)
        dgate_ref[:, cols] = dgate
        dup_ref[:, cols] = dup
        part = dot_nt(dgate, gate_up[0, :, cols]) + dot_nt(dup, gate_up[1, :, cols])
        if start == 0:
            acc[...] = part
        else:
            acc[...] += part
    for s in range(SEQ):
        outs[s][...] = acc[s * rows : (s + 1) * rows, :].astype(outs[s].dtype)


def split_rows(ids, acc, keep, send, where):
    shard = acc.shape[0] // INNER
    for t in range(CHIPS):
        keep[(t,) + where] = acc[at(ids[2 * t] * shard, shard, 32), :]
        send[(t,) + where] = acc[at(ids[2 * t + 1] * shard, shard, 32), :].astype(BF16)


def feed_weights(ids, *refs):
    normed, grads, hidden, dgate, dup = refs[0:5]
    keep, send = refs[5:7]
    acc = refs[7]
    for n, (left, right) in enumerate(((normed, dgate), (normed, dup), (hidden, grads))):
        acc[...] = dot_tn(left[...], right[...])
        split_rows(ids, acc, keep, send, (n,))


def pair_sum(*refs):
    keep, received = refs[0:2]
    for t in range(CHIPS):
        refs[2 + t][...] = (keep[t] + received[t].astype(F32)).astype(refs[2 + t].dtype)


def step_one(*refs):
    keep, received = refs[0:2]
    left, left_next, right, right_next, to_x, to_y = refs[2:8]
    half = left.shape[-1]

    def part(t, side):
        cols = slice(side * half, (side + 1) * half)
        return keep[t, :, :, cols] + received[t, :, :, cols].astype(F32)

    left[...] = part(0, 0)
    left_next[...] = part(2, 0)
    right[...] = part(0, 1)
    right_next[...] = part(1, 1)
    to_x[0] = part(1, 0).astype(BF16)
    to_x[1] = part(3, 0).astype(BF16)
    to_y[0] = part(2, 1).astype(BF16)
    to_y[1] = part(3, 1).astype(BF16)


def step_two(*refs):
    left, left_next, right, right_next, from_x, from_y = refs[0:6]
    left_out, right_out, to_y, to_x = refs[6:10]
    left_out[...] = left[...] + from_x[0].astype(F32)
    to_y[...] = (left_next[...] + from_x[1].astype(F32)).astype(BF16)
    right_out[...] = right[...] + from_y[0].astype(F32)
    to_x[...] = (right_next[...] + from_y[1].astype(F32)).astype(BF16)


def step_three(*refs):
    left, right, from_y, from_x, out = refs
    half = left.shape[-1]
    out[:, :, 0:half] = (left[...] + from_y[...].astype(F32)).astype(BF16)
    out[:, :, half:] = (right[...] + from_x[...].astype(F32)).astype(BF16)


def plane_sum(*refs):
    out = refs[-1]
    acc = refs[0][...].astype(F32)
    for ref in refs[1:-1]:
        acc = acc + ref[...].astype(F32)
    out[...] = acc.astype(out.dtype)


def feed_final(ids, *refs):
    blocks, out, down_out = refs[0:4], refs[4], refs[5]
    rows, model = blocks[0].shape[1:]
    hidden = out.shape[1] // 2
    window = hidden // INNER
    units = window // SEQ
    group = lax.broadcasted_iota(jnp.int32, (rows, window), 1) // units
    for g in range(2):
        for w in range(model // window):
            parts = [b[g, :, w * window : (w + 1) * window].astype(F32) for b in blocks]
            for i in range(SEQ):
                acc = jnp.zeros((rows, window), F32)
                for s in range(SEQ):
                    pos = ids[8 + s]
                    shift = lax.rem(units * (pos - i) + window, window)
                    acc = jnp.where(group == pos, pltpu.roll(parts[s], shift, 1), acc)
                start = g * hidden + (SEQ * w + i) * window
                out[:, start : start + window] = acc
    for s in range(SEQ):
        down_out[at(ids[8 + s] * units, units, 32), :] = blocks[s][2].astype(F32)


def project_back(ids, *refs):
    parts = refs[0:4]
    grad_second, first_ref, vectors, w_out = refs[4:8]
    sums_in, stats_ref = refs[8:10]
    grad_first_ref = refs[10]
    grad_outs, sums_ref = refs[11:15], refs[15]
    grad = grad_second[...] + parts[0][...]
    for s in range(1, SEQ):
        grad = grad + parts[s][...].astype(F32)
    normalized, inv_std = norm_parts(first_ref[...])
    grad_first = norm_back(grad, normalized, inv_std, vectors[0:1, :])
    grad_first_ref[...] = grad_first
    grad_branch = grad_first.astype(BF16)
    rows, model = grad_branch.shape
    width = grad_outs[0].shape[1] // 2
    high = stats_ref[...].astype(BF16)
    low = (stats_ref[...] - high.astype(F32)).astype(BF16)
    stats_rows = jnp.concatenate([high, low], axis=0)
    stats_rows = jnp.concatenate([stats_rows, jnp.zeros((PAD, 2 * width - 128), BF16)], axis=1)
    row = lax.broadcasted_iota(jnp.int32, (model, width), 0)
    column = lax.broadcasted_iota(jnp.int32, (model, width), 1)
    for s in range(SEQ):
        start = ids[8 + s] * width
        mine = w_out[at(start, width, 64), :]
        grad_outs[s][0:rows, 0:width] = dot_nt(grad_branch, mine).astype(BF16)
        grad_outs[s][rows : rows + PAD, :] = stats_rows
        chosen = (row == start + column).astype(F32).astype(BF16)
        grad_outs[s][0:rows, width:] = dot(grad_branch, chosen).astype(BF16)
    sums_ref[0:1, :] = column_sum(grad * normalized)
    sums_ref[1:2, :] = column_sum(grad)
    sums_ref[2:4, :] = sums_in[0:2, :]
    sums_ref[4:PAD, :] = jnp.zeros((PAD - 4, model), F32)


def attention_back(*refs):
    grad_blocks = refs[0:4]
    q_ref, k_ref, v_ref, probs_ref, w_qkv = refs[4:9]
    outs, grad_qkv = refs[9:13], refs[13]
    grads, grad_q, grad_k, grad_v = refs[14:18]
    rows = outs[0].shape[0]
    for s in range(SEQ):
        place = slice(s * rows, (s + 1) * rows)
        grads[place, :] = grad_blocks[s][0:rows, 0 : grads.shape[1]]
    queries, keys, values = q_ref[...], k_ref[...], v_ref[...]
    width = keys.shape[1]
    heads = width // HEAD_DIM
    head_of = lax.broadcasted_iota(jnp.int32, (1, width), 1) // HEAD_DIM
    scale = 1.0 / math.sqrt(HEAD_DIM)
    for h in range(heads):
        mine = head_of == h
        head_keys = jnp.where(mine, keys, jnp.zeros_like(keys))
        for s in range(SEQ):
            place = slice(s * rows, (s + 1) * rows)
            grad_out = jnp.where(mine, grads[place, :], jnp.zeros((rows, width), BF16))
            query = jnp.where(mine, queries[place, :], jnp.zeros((rows, width), BF16))
            probs_low = probs_ref[h, place, :]
            probs = probs_low.astype(F32)
            grad_probs = dot_nt(grad_out, values)
            delta = jnp.sum(probs * grad_probs, axis=-1, keepdims=True)
            grad_scores = (probs * (grad_probs - delta)).astype(BF16)
            dq = dot(grad_scores, head_keys)
            dk = dot_tn(grad_scores, query)
            dv = dot_tn(probs_low, grad_out)
            if h == 0:
                grad_q[place, :] = dq
            else:
                grad_q[place, :] += dq
            if h == 0 and s == 0:
                grad_k[...] = dk
                grad_v[...] = dv
            else:
                grad_k[...] += dk
                grad_v[...] += dv
    low = (
        (grad_q[...] * scale).astype(BF16),
        (grad_k[...] * scale).astype(BF16),
        grad_v[...].astype(BF16),
    )
    grad_input = dot_nt(low[0], w_qkv[0]) + dot_nt(low[1], w_qkv[1]) + dot_nt(low[2], w_qkv[2])
    for s in range(SEQ):
        outs[s][...] = grad_input[s * rows : (s + 1) * rows, :].astype(outs[s].dtype)
    for part in range(3):
        grad_qkv[:, part * width : (part + 1) * width] = low[part]


def attention_weights(ids, *refs):
    grad_qkv, x_blocks, attn, columns = refs[0], refs[1:5], refs[5], refs[6:10]
    sums = refs[10]
    keep, send = refs[11:13]
    xs, grads, out_acc, acc = refs[13:17]
    rows = x_blocks[0].shape[0]
    width = grads.shape[1]
    for s in range(SEQ):
        place = slice(s * rows, (s + 1) * rows)
        xs[place, :] = x_blocks[s][...]
        grads[place, :] = columns[s][0:rows, width:]
    for t in range(SEQ):
        out_acc[at(ids[8 + t] * width, width, 64), :] = dot_tn(attn[t], grads[...])
    acc[:, 0 : 3 * width] = dot_tn(xs[...], grad_qkv[...])
    acc[:, 3 * width : 4 * width] = out_acc[...]
    shard = acc.shape[0] // INNER
    split_rows(ids, acc, keep, send, (slice(0, shard),))
    for t in range(CHIPS):
        keep[t, shard : shard + PAD, :] = sums[...]
        send[t, shard : shard + PAD, :] = sums[...].astype(BF16)


def input_final(*refs):
    grad_first, parts, stats_in, grad_blocks = refs[0], refs[1:5], refs[5], refs[6:9]
    out, means = refs[9:11]
    acc = grad_first[...] + parts[0][...]
    for s in range(1, SEQ):
        acc = acc + parts[s][...].astype(F32)
    out[...] = acc.astype(BF16)
    rows, model = out.shape
    stats = stats_in[...]
    for ref in grad_blocks:
        extra = ref[rows : rows + PAD, 0:128].astype(F32)
        stats = stats + (extra[0:8] + extra[8:16])
    means[...] = jnp.sqrt(stats * (1.0 / (SEQ * rows * model)))


def attention_final(ids, *refs):
    blocks, qkv_out, out, vectors, stage = refs[0:4], refs[4], refs[5], refs[6], refs[7]
    for s in range(SEQ):
        stage[ids[8 + s]] = blocks[s][...].astype(F32)
    shard, model = out.shape
    width = model // SEQ
    for pos in range(SEQ):
        for part in range(3):
            start = (part * SEQ + pos) * width
            qkv_out[:, start : start + width] = stage[pos, 0:shard, part * width : (part + 1) * width]
        out[:, pos * width : (pos + 1) * width] = stage[pos, 0:shard, 3 * width : 4 * width]
    sums = stage[0, shard : shard + 8, :]
    for pos in range(1, SEQ):
        sums = sums + stage[pos, shard : shard + 8, :]
    shift = model - ids[0] * shard
    vectors[...] = pltpu.roll(sums, lax.rem(shift, model), 1)[:, 0:128]


def after(values, *deps):
    return lax.optimization_barrier((values, deps))[0]


def body(
    layer_input,
    w_qkv,
    w_out,
    ln1_gain,
    ln1_bias,
    w_gate_up,
    w_down,
    ln2_gain,
    ln2_bias,
    doc_starts,
    cotangent,
):
    dp = lax.axis_size("dp")
    stride = dp // INNER
    rows, model = layer_input.shape[1:]
    columns = tuple(tuple(range(g * stride, (g + 1) * stride)) for g in range(INNER))
    cores = tuple(
        tuple((2 * t + core) * stride + r for t in range(CHIPS))
        for core in range(2)
        for r in range(stride)
    )

    def gather_outer(value):
        if stride == 1:
            return value
        return lax.all_gather(value, "dp", axis=0, tiled=True, axis_index_groups=columns)

    def scatter_outer(value):
        if stride == 1:
            return value
        return lax.psum_scatter(
            value, "dp", scatter_dimension=0, tiled=True, axis_index_groups=columns
        )

    def swap(value, s):
        return lax.ppermute(value, "dp", [(i, i ^ (s * stride)) for i in range(dp)])

    def pass_seq(value, s):
        return lax.ppermute(value, "seq", [(i, i ^ s) for i in range(SEQ)])

    def gather_seq(value):
        far = pass_seq(value, 2)
        near = pass_seq(value, 1)
        return [value, near, far, pass_seq(far, 1)]

    def reduce_seq(pieces):
        return [pieces[0]] + [pass_seq(pieces[s], s) for s in range(1, SEQ)]

    j = lax.axis_index("dp") // stride
    z = lax.axis_index("seq")
    ids = jnp.concatenate(
        [
            jnp.bitwise_xor(j, jnp.arange(INNER, dtype=jnp.int32)),
            jnp.bitwise_xor(z, jnp.arange(SEQ, dtype=jnp.int32)),
        ]
    )
    slopes = jnp.asarray(SLOPES)

    w_qkv, w_out, w_gate_up, w_down = map(gather_outer, (w_qkv, w_out, w_gate_up, w_down))
    vectors = [gather_outer(v) for v in (ln1_gain, ln1_bias, ln2_gain, ln2_bias)]
    shard = w_out.shape[0]
    head_width = HEADS // SEQ * HEAD_DIM

    x_own = layer_input[0]
    x_blocks = gather_seq(x_own)

    own_qkv = jnp.concatenate(
        [
            lax.dynamic_slice(w_qkv, (0, part * model + z * head_width), (shard, head_width))
            for part in range(3)
        ],
        axis=1,
    )
    qkv_even = [own_qkv] + [swap(own_qkv, s) for s in (2, 4, 6)]
    qkv_odd = swap(jnp.concatenate(qkv_even, axis=0), 1)

    params = jnp.pad(jnp.stack(vectors, axis=0), ((0, PAD - 4), (0, model - shard)))
    (piece,) = call(
        select_units,
        [((4 * shard + PAD, model), BF16)],
        [ids],
        w_gate_up,
        w_down,
        w_out,
        params,
        mib=8,
    )
    piece = after(piece, qkv_even, x_blocks[1:3])
    even_x, even_y = swap(piece, 2), swap(piece, 4)

    length = SEQ * rows
    packed, queries, keys, values, probs, qkv_full = call(
        attention_forward,
        [((length * 3 // 2, 128), BF16)]
        + [((length, head_width), BF16)] * 3
        + [((HEADS // SEQ, length, length), BF16), ((3, model, head_width), BF16)],
        [ids, doc_starts, slopes],
        *x_blocks,
        *qkv_even,
        qkv_odd,
        scratch=[((length, model), BF16), ((length, head_width), BF16)],
        mib=16,
        flops=2 * length * head_width * (3 * model + 2 * length),
    )
    packs = gather_seq(packed)
    even_x, even_y = after((even_x, even_y), packed)
    half = model // 2
    diagonal = [swap(even_x[:, :half], 4), swap(even_y[:, half:], 2)]
    feed_even = [piece, even_x, even_y, jnp.concatenate(diagonal, axis=1)]


    feed_even = after(feed_even, packs[1:3])
    feed_odd = swap(jnp.concatenate(feed_even, axis=0), 1)
    units = w_down.shape[0] // SEQ * INNER
    gate_up_full, down_full, out_full, norm_vectors = call(
        gather_weights,
        [
            ((2, model, units), BF16),
            ((units, model), BF16),
            ((model, model), BF16),
            ((8, model), F32),
        ],
        [ids],
        *feed_even,
        feed_odd,
        mib=16,
    )

    shares = [((rows, model), F32)] + [((rows, model), BF16)] * 3
    *feed_parts, first_sum, normed, stats1, attn = call(
        middle_forward,
        shares
        + [
            ((rows, model), F32),
            ((length, model), BF16),
            ((8, 128), F32),
            ((SEQ, length, head_width), BF16),
        ],
        [ids],
        *packs,
        *x_blocks,
        out_full,
        norm_vectors,
        gate_up_full,
        down_full,
        scratch=[((length, model), F32)],
        mib=16,
        flops=2 * length * model * (model + 3 * units),
    )

    output, grad_feed, grad_second, sums2, stats2 = call(
        final_norm,
        [
            ((rows, model), BF16),
            ((rows, model), BF16),
            ((rows, model), F32),
            ((8, model), F32),
            ((8, 128), F32),
        ],
        [],
        *reduce_seq(feed_parts),
        normed,
        cotangent[0],
        norm_vectors,
        stats1,
    )

    *back_parts, hidden, dgate, dup, grads = call(
        feed_back,
        shares + [((length, units), BF16)] * 3 + [((length, model), BF16)],
        [],
        normed,
        *gather_seq(grad_feed),
        gate_up_full,
        down_full,
        scratch=[((length, model), F32)],
        mib=18,
        flops=10 * length * model * units,
    )
    back_parts = reduce_seq(back_parts)

    feed_keep, feed_send = call(
        feed_weights,
        [((CHIPS, 3, shard, model), F32), ((CHIPS, 3, shard, model), BF16)],
        [ids],
        normed,
        grads,
        hidden,
        dgate,
        dup,
        scratch=[((model, model), F32)],
        mib=18,
        flops=6 * length * model * units,
    )

    def pair(keep, send):
        shape = keep.shape[1:]
        return call(pair_sum, [(shape, F32)] + [(shape, BF16)] * 3, [], keep, swap(send, 1))

    half_shape = (3, shard, model // 2)
    grad_first, *projected = call(
        project_back,
        [((rows, model), F32)]
        + [((rows + PAD, 2 * head_width), BF16)] * SEQ
        + [((PAD, model), F32)],
        [ids],
        *back_parts,
        grad_second,
        first_sum,
        norm_vectors,
        out_full,
        sums2,
        stats2,
        mib=10,
        flops=4 * rows * model * model,
    )
    grad_attn = reduce_seq(projected[0:4])
    *feed_pieces, to_x, to_y = call(
        step_one,
        [(half_shape, F32)] * 4 + [((2,) + half_shape, BF16)] * 2,
        [],
        after(feed_keep, grad_first),
        swap(feed_send, 1),
        mib=10,
    )
    left, right, to_y, to_x = call(
        step_two,
        [(half_shape, F32)] * 2 + [(half_shape, BF16)] * 2,
        [],
        *after(feed_pieces, grad_attn),
        swap(to_x, 2),
        swap(to_y, 4),
        mib=10,
    )

    sums = projected[4]
    (feed_share,) = call(
        step_three, [((3, shard, model), BF16)], [], left, right, swap(to_y, 4), swap(to_x, 2)
    )
    sums = after(sums, feed_share)
    feed_blocks = gather_seq(after(feed_share, grad_attn))

    *input_parts, grad_qkv = call(
        attention_back,
        shares + [((length, 3 * head_width), BF16)],
        [],
        *grad_attn,
        queries,
        keys,
        values,
        probs,
        qkv_full,
        scratch=[((length, head_width), BF16)] + [((length, head_width), F32)] * 3,
        mib=16,
        flops=2 * length * head_width * (3 * model + 5 * length),
    )
    input_parts = reduce_seq(input_parts)


    attn_keep, attn_send = call(
        attention_weights,
        [
            ((CHIPS, shard + PAD, model), F32),
            ((CHIPS, shard + PAD, model), BF16),
        ],
        [ids],
        grad_qkv,
        *x_blocks,
        attn,
        *grad_attn,
        sums,
        scratch=[
            ((length, model), BF16),
            ((length, head_width), BF16),
            ((model, head_width), F32),
            ((model, model), F32),
        ],
        mib=16,
        flops=2 * length * model * model,
    )

    grad_gate_up_w, grad_down_w = call(
        feed_final,
        [(w_gate_up.shape, F32), (w_down.shape, F32)],
        [ids],
        *feed_blocks,
        mib=10,
    )
    attn_pieces = pair(attn_keep, attn_send)
    attn_pieces = [attn_pieces[0]] + [swap(attn_pieces[t], 2 * t) for t in range(1, CHIPS)]
    attn_pieces = after(attn_pieces, input_parts, feed_blocks[1:3])
    (attn_share,) = call(plane_sum, [((shard + PAD, model), BF16)], [], *attn_pieces)
    input_grad, means = call(
        input_final,
        [((rows, model), BF16), ((8, 128), F32)],
        [],
        grad_first,
        *input_parts,
        stats2,
        *grad_attn[1:],
    )
    attn_near = pass_seq(attn_share, 1)
    attn_far = after(pass_seq(attn_share, 2), grad_gate_up_w, input_grad)
    grad_qkv_w, grad_out_w, vector_grads = call(
        attention_final,
        [((shard, 3 * model), F32), ((shard, model), F32), ((8, 128), F32)],
        [ids],
        attn_share,
        attn_near,
        attn_far,
        pass_seq(attn_far, 1),
        scratch=[((SEQ, shard + PAD, model), F32)],
    )

    vector_grads = [scatter_outer(vector_grads[n, :shard]) for n in range(4)]
    return (
        output[None],
        input_grad[None],
        scatter_outer(grad_qkv_w),
        scatter_outer(grad_out_w),
        vector_grads[0],
        vector_grads[1],
        scatter_outer(grad_gate_up_w),
        scatter_outer(grad_down_w),
        vector_grads[2],
        vector_grads[3],
        means[0:1, 0:4],
    )


def solution(mesh):
    return jax.shard_map(
        body,
        mesh=mesh,
        in_specs=(
            P("dp", "seq", None),
            P("dp", None),
            P("dp", None),
            P("dp"),
            P("dp"),
            P("dp", None),
            P("dp", None),
            P("dp"),
            P("dp"),
            P("dp", None),
            P("dp", "seq", None),
        ),
        out_specs=(
            P("dp", "seq", None),
            P("dp", "seq", None),
            P("dp", None),
            P("dp", None),
            P("dp"),
            P("dp"),
            P("dp", None),
            P("dp", None),
            P("dp"),
            P("dp"),
            P("dp", None),
        ),
        check_vma=False,
    )
```

```python
import math

import jax
import jax.numpy as jnp
import numpy as np
from jax import lax
from jax.experimental import pallas as pl
from jax.experimental.pallas import tpu as pltpu
from jax.sharding import PartitionSpec as P

HEADS = 12
HEAD_DIM = 64
NORM_EPSILON = 1e-05
GELU_C = 0.7978845608028654
GELU_A = 0.044715
INNER = 8
CHIPS = 4
SEQ = 4
PAD = 16

F32 = jnp.float32
BF16 = jnp.bfloat16
SLOPES = (2.0 ** (-8.0 * (np.arange(HEADS) + 1.0) / HEADS)).astype(np.float32)


def dot(left, right):
    return jnp.dot(left, right, preferred_element_type=F32)


def dot_nt(left, right):
    return lax.dot_general(left, right, (((1,), (1,)), ((), ())), preferred_element_type=F32)


def dot_tn(left, right):
    return lax.dot_general(left, right, (((0,), (0,)), ((), ())), preferred_element_type=F32)


def gelu_parts(value):
    square = value * value
    tanh = jnp.tanh(GELU_C * (value + GELU_A * square * value))
    half = 0.5 * (1.0 + tanh)
    slope = half + 0.5 * value * (1.0 - tanh * tanh) * (GELU_C * (1.0 + 3.0 * GELU_A * square))
    return value * half, slope


def gelu(value):
    return 0.5 * value * (1.0 + jnp.tanh(GELU_C * (value + GELU_A * value * value * value)))


def norm_parts(summed):
    centered = summed - jnp.mean(summed, axis=-1, keepdims=True)
    variance = jnp.mean(centered * centered, axis=-1, keepdims=True)
    inv_std = lax.rsqrt(variance + NORM_EPSILON)
    return centered * inv_std, inv_std


def norm_back(grad_in, normalized, inv_std, gain):
    scaled = grad_in * gain
    return inv_std * (
        scaled
        - jnp.mean(scaled, axis=-1, keepdims=True)
        - normalized * jnp.mean(scaled * normalized, axis=-1, keepdims=True)
    )


def column_sum(value):
    return jnp.sum(value, axis=0, keepdims=True)


def total(value):
    return jnp.sum(jnp.sum(value, axis=1, keepdims=True), axis=0, keepdims=True)


def at(start, size, step):
    return pl.ds(pl.multiple_of(start, step), size)


def call(kernel, outs, smem, *vmem, scratch=(), flops=0, mib=8, aliases=None):
    specs = [pl.BlockSpec(memory_space=pltpu.SMEM) for _ in smem]
    specs += [pl.BlockSpec(memory_space=pltpu.VMEM) for _ in vmem]
    out_shape = [jax.ShapeDtypeStruct(shape, dtype) for shape, dtype in outs]
    moved = sum(math.prod(a.shape) * a.dtype.itemsize for a in list(vmem) + out_shape)
    return pl.pallas_call(
        kernel,
        out_shape=out_shape,
        in_specs=specs,
        out_specs=[pl.BlockSpec(memory_space=pltpu.VMEM) for _ in outs],
        scratch_shapes=[pltpu.VMEM(shape, dtype) for shape, dtype in scratch],
        input_output_aliases=aliases or {},
        cost_estimate=pl.CostEstimate(flops=flops, transcendentals=0, bytes_accessed=moved),
        name=kernel.__name__,
        compiler_params=pltpu.CompilerParams(vmem_limit_bytes=mib << 20),
    )(*smem, *vmem)


def select_units(ids, gate_up, down, w_out, params, piece):
    z = ids[8]
    rows = w_out.shape[0]
    window = down.shape[0]
    units = window // SEQ
    model = w_out.shape[1]
    hidden = gate_up.shape[1] // 2
    group = lax.broadcasted_iota(jnp.int32, (rows, window), 1) // units
    for g in range(2):
        for w in range(model // window):
            acc = jnp.zeros((rows, window), F32)
            for i in range(SEQ):
                start = g * hidden + (SEQ * w + i) * window
                shift = lax.rem(units * (i - z) + window, window)
                moved = pltpu.roll(gate_up[:, start : start + window].astype(F32), shift, 1)
                acc = jnp.where(group == i, moved, acc)
            piece[g * rows : (g + 1) * rows, w * window : (w + 1) * window] = acc.astype(BF16)
    piece[2 * rows : 3 * rows, :] = down[at(z * units, units, 32), :]
    piece[3 * rows : 4 * rows, :] = w_out[...]
    piece[4 * rows :, :] = params[...]


def gather_weights(ids, *refs):
    blocks, odd = refs[0:4], refs[4]
    gate_up, down, w_out, vectors = refs[5:9]
    model = w_out.shape[0]
    rows = model // INNER
    size = blocks[0].shape[0]
    gathered = jnp.zeros((8, model), F32)
    for t in range(CHIPS):
        for s in range(2):
            start = ids[2 * t + s] * rows
            place = at(start, rows, 32)
            block = blocks[t] if s == 0 else odd.at[t * size : (t + 1) * size]
            gate_up[0, place, :] = block[0:rows, :]
            gate_up[1, place, :] = block[rows : 2 * rows, :]
            down[place, :] = block[2 * rows : 3 * rows, :]
            w_out[place, :] = block[3 * rows : 4 * rows, :]
            piece = block[4 * rows : 4 * rows + PAD, :].astype(F32)
            gathered = gathered + pltpu.roll(piece, start, 1)[0:8]
    vectors[...] = gathered


def attention_forward(ids, starts, slopes, *refs):
    x_blocks, w_blocks, odd = refs[0:4], refs[4:8], refs[8]
    packed, q_out, k_out, v_out, probs_out, w_qkv = refs[9:15]
    xs, attended = refs[15:17]
    rows = x_blocks[0].shape[0]
    length = SEQ * rows
    model = w_qkv.shape[1]
    width = w_qkv.shape[2]
    shard = model // INNER
    for t in range(CHIPS):
        for s in range(2):
            place = at(ids[2 * t + s] * shard, shard, 32)
            block = w_blocks[t] if s == 0 else odd.at[t * shard : (t + 1) * shard]
            for part in range(3):
                w_qkv[part, place, :] = block[:, part * width : (part + 1) * width]
    for s in range(SEQ):
        xs[s * rows : (s + 1) * rows, :] = x_blocks[s][...]
    joint = xs[...]
    q_out[...] = dot(joint, w_qkv[0]).astype(BF16)
    k_out[...] = dot(joint, w_qkv[1]).astype(BF16)
    v_out[...] = dot(joint, w_qkv[2]).astype(BF16)
    keys = k_out[...]
    values = v_out[...]
    heads = width // HEAD_DIM
    z = ids[8]

    def doc_of(position):
        count = jnp.zeros(position.shape, jnp.int32)
        for n in range(starts.shape[1]):
            count = count + (starts[0, n] <= position).astype(jnp.int32)
        return count

    lane = lax.broadcasted_iota(jnp.int32, (1, length), 1)
    key_pos = (jnp.bitwise_xor(lane // rows, z)) * rows + lane % rows
    key_docs = doc_of(key_pos)
    head_of = lax.broadcasted_iota(jnp.int32, (1, width), 1) // HEAD_DIM
    head_values = [jnp.where(head_of == h, values, jnp.zeros_like(values)) for h in range(heads)]

    def one_block(s, carry):
        place = at(s * rows, rows, 128)
        query_pos = ids[8 + s] * rows + lax.broadcasted_iota(jnp.int32, (rows, 1), 0)
        distance = jnp.abs(query_pos - key_pos).astype(F32)
        same_doc = doc_of(query_pos) == key_docs
        block = q_out[place, :] * BF16(1.0 / math.sqrt(HEAD_DIM))
        total_out = jnp.zeros((rows, width), F32)
        for h in range(heads):
            query = jnp.where(head_of == h, block, jnp.zeros_like(block))
            scores = dot_nt(query, keys) - slopes[z * heads + h] * distance
            scores = jnp.where(same_doc, scores, -1e30)
            expon = jnp.exp(scores - jnp.max(scores, axis=-1, keepdims=True))
            probs = (expon / jnp.sum(expon, axis=-1, keepdims=True)).astype(BF16)
            probs_out[h, place, :] = probs
            total_out = total_out + dot(probs, head_values[h])
        attended[place, :] = total_out.astype(BF16)
        return carry

    lax.fori_loop(0, SEQ, one_block, 0)
    half = length // 2
    packed[0:length, :] = attended[:, 0:128]
    packed[length:, 0:64] = attended[0:half, 128:192]
    packed[length:, 64:128] = attended[half:, 128:192]


def middle_forward(ids, *refs):
    packs, x_blocks = refs[0:4], refs[4:8]
    w_out, vectors, gate_up, down = refs[8:12]
    outs = refs[12:16]
    first_ref, normed_ref, stats_ref, attn = refs[16:20]
    acc = refs[20]
    rows = x_blocks[0].shape[0]
    length = SEQ * rows
    width = attn.shape[2]
    for t in range(SEQ):
        for u in range(SEQ):
            place = slice(u * rows, (u + 1) * rows)
            b = t ^ u
            attn[t, place, 0:128] = packs[t][b * rows : (b + 1) * rows, :]
            start = length + (b % 2) * rows
            attn[t, place, 128:192] = packs[t][start : start + rows, (b // 2) * 64 : (b // 2) * 64 + 64]
    w_parts = [w_out[at(ids[8 + t] * width, width, 64), :] for t in range(SEQ)]
    for u in range(SEQ):
        place = slice(u * rows, (u + 1) * rows)
        branch = dot(attn[0, place, :], w_parts[0])
        for t in range(1, SEQ):
            branch = branch + dot(attn[t, place, :], w_parts[t])
        first_sum = x_blocks[u][...].astype(F32) + branch
        normalized, _ = norm_parts(first_sum)
        normed_ref[place, :] = (normalized * vectors[0:1, :] + vectors[1:2, :]).astype(BF16)
        if u == 0:
            first_ref[...] = first_sum
            lane = lax.broadcasted_iota(jnp.int32, stats_ref.shape, 1)
            stats_ref[...] = jnp.where(lane == 0, total(branch * branch), 0.0) + jnp.where(
                lane == 1, total(first_sum * first_sum), 0.0
            )
    normed = normed_ref[...]
    step = 256
    for start in range(0, down.shape[0], step):
        cols = slice(start, start + step)
        gate = dot(normed, gate_up[0, :, cols])
        up = dot(normed, gate_up[1, :, cols])
        hidden = (gelu(gate) * up).astype(BF16)
        part = dot(hidden, down[cols, :])
        if start == 0:
            acc[...] = part
        else:
            acc[...] += part
    for s in range(SEQ):
        outs[s][...] = acc[s * rows : (s + 1) * rows, :].astype(outs[s].dtype)


def final_norm(*refs):
    parts = refs[0:4]
    normed_ref, cot_ref, vectors, stats_in = refs[4:8]
    out_ref, grad_feed_ref, grad_second_ref, sums_ref, stats_ref = refs[8:13]
    feed_out = parts[0][...]
    for s in range(1, CHIPS):
        feed_out = feed_out + parts[s][...].astype(F32)
    second = normed_ref[0 : cot_ref.shape[0], :].astype(F32) + feed_out
    normalized, inv_std = norm_parts(second)
    gain = vectors[2:3, :]
    out_ref[...] = (normalized * gain + vectors[3:4, :]).astype(BF16)
    grad = cot_ref[...].astype(F32)
    grad_second = norm_back(grad, normalized, inv_std, gain)
    grad_second_ref[...] = grad_second
    grad_feed_ref[...] = grad_second.astype(BF16)
    sums_ref[0:1, :] = column_sum(grad * normalized)
    sums_ref[1:2, :] = column_sum(grad)
    sums_ref[2:8, :] = jnp.zeros((6, gain.shape[1]), F32)
    lane = lax.broadcasted_iota(jnp.int32, stats_ref.shape, 1)
    stats_ref[...] = (
        stats_in[...]
        + jnp.where(lane == 2, total(feed_out * feed_out), 0.0)
        + jnp.where(lane == 3, total(second * second), 0.0)
    )


def feed_back(*refs):
    normed_ref, grad_blocks = refs[0], refs[1:5]
    gate_up, down = refs[5:7]
    outs = refs[7:11]
    hidden_ref, dgate_ref, dup_ref, grads = refs[11:15]
    acc = refs[15]
    rows = grad_blocks[0].shape[0]
    for s in range(SEQ):
        grads[s * rows : (s + 1) * rows, :] = grad_blocks[s][...]
    normed = normed_ref[...]
    grad_feed = grads[...]
    step = 256
    for start in range(0, down.shape[0], step):
        cols = slice(start, start + step)
        gate = dot(normed, gate_up[0, :, cols])
        up = dot(normed, gate_up[1, :, cols])
        grad_hidden = dot_nt(grad_feed, down[cols, :])
        act, slope = gelu_parts(gate)
        hidden_ref[:, cols] = (act * up).astype(BF16)
        dgate = (grad_hidden * up * slope).astype(BF16)
        dup = (grad_hidden * act).astype(BF16)
        dgate_ref[:, cols] = dgate
        dup_ref[:, cols] = dup
        part = dot_nt(dgate, gate_up[0, :, cols]) + dot_nt(dup, gate_up[1, :, cols])
        if start == 0:
            acc[...] = part
        else:
            acc[...] += part
    for s in range(SEQ):
        outs[s][...] = acc[s * rows : (s + 1) * rows, :].astype(outs[s].dtype)


def split_rows(ids, acc, keep, send, where):
    shard = acc.shape[0] // INNER
    for t in range(CHIPS):
        keep[(t,) + where] = acc[at(ids[2 * t] * shard, shard, 32), :]
        send[(t,) + where] = acc[at(ids[2 * t + 1] * shard, shard, 32), :].astype(BF16)


def feed_weights(ids, *refs):
    normed, grads, hidden, dgate, dup = refs[0:5]
    keep, send = refs[5:7]
    acc = refs[7]
    for n, (left, right) in enumerate(((normed, dgate), (normed, dup), (hidden, grads))):
        acc[...] = dot_tn(left[...], right[...])
        split_rows(ids, acc, keep, send, (n,))


def pair_sum(*refs):
    keep, received = refs[0:2]
    for t in range(CHIPS):
        refs[2 + t][...] = (keep[t] + received[t].astype(F32)).astype(refs[2 + t].dtype)


def step_one(*refs):
    keep, received = refs[0:2]
    left, left_next, right, right_next, to_x, to_y = refs[2:8]
    half = left.shape[-1]

    def part(t, side):
        cols = slice(side * half, (side + 1) * half)
        return keep[t, :, :, cols] + received[t, :, :, cols].astype(F32)

    left[...] = part(0, 0)
    left_next[...] = part(2, 0)
    right[...] = part(0, 1)
    right_next[...] = part(1, 1)
    to_x[0] = part(1, 0).astype(BF16)
    to_x[1] = part(3, 0).astype(BF16)
    to_y[0] = part(2, 1).astype(BF16)
    to_y[1] = part(3, 1).astype(BF16)


def step_two(*refs):
    left, left_next, right, right_next, from_x, from_y = refs[0:6]
    left_out, right_out, to_y, to_x = refs[6:10]
    left_out[...] = left[...] + from_x[0].astype(F32)
    to_y[...] = (left_next[...] + from_x[1].astype(F32)).astype(BF16)
    right_out[...] = right[...] + from_y[0].astype(F32)
    to_x[...] = (right_next[...] + from_y[1].astype(F32)).astype(BF16)


def step_three(*refs):
    left, right, from_y, from_x, out = refs
    half = left.shape[-1]
    out[:, :, 0:half] = (left[...] + from_y[...].astype(F32)).astype(BF16)
    out[:, :, half:] = (right[...] + from_x[...].astype(F32)).astype(BF16)


def plane_sum(*refs):
    out = refs[-1]
    acc = refs[0][...].astype(F32)
    for ref in refs[1:-1]:
        acc = acc + ref[...].astype(F32)
    out[...] = acc.astype(out.dtype)


def feed_final(ids, *refs):
    blocks, out, down_out = refs[0:4], refs[4], refs[5]
    rows, model = blocks[0].shape[1:]
    hidden = out.shape[1] // 2
    window = hidden // INNER
    units = window // SEQ
    group = lax.broadcasted_iota(jnp.int32, (rows, window), 1) // units
    for g in range(2):
        for w in range(model // window):
            parts = [b[g, :, w * window : (w + 1) * window].astype(F32) for b in blocks]
            for i in range(SEQ):
                acc = jnp.zeros((rows, window), F32)
                for s in range(SEQ):
                    pos = ids[8 + s]
                    shift = lax.rem(units * (pos - i) + window, window)
                    acc = jnp.where(group == pos, pltpu.roll(parts[s], shift, 1), acc)
                start = g * hidden + (SEQ * w + i) * window
                out[:, start : start + window] = acc
    for s in range(SEQ):
        down_out[at(ids[8 + s] * units, units, 32), :] = blocks[s][2].astype(F32)


def project_back(ids, *refs):
    parts = refs[0:4]
    grad_second, first_ref, vectors, w_out = refs[4:8]
    sums_in, stats_ref = refs[8:10]
    grad_first_ref = refs[10]
    grad_outs, sums_ref = refs[11:15], refs[15]
    grad = grad_second[...] + parts[0][...]
    for s in range(1, SEQ):
        grad = grad + parts[s][...].astype(F32)
    normalized, inv_std = norm_parts(first_ref[...])
    grad_first = norm_back(grad, normalized, inv_std, vectors[0:1, :])
    grad_first_ref[...] = grad_first
    grad_branch = grad_first.astype(BF16)
    rows, model = grad_branch.shape
    width = grad_outs[0].shape[1] // 2
    high = stats_ref[...].astype(BF16)
    low = (stats_ref[...] - high.astype(F32)).astype(BF16)
    stats_rows = jnp.concatenate([high, low], axis=0)
    stats_rows = jnp.concatenate([stats_rows, jnp.zeros((PAD, 2 * width - 128), BF16)], axis=1)
    row = lax.broadcasted_iota(jnp.int32, (model, width), 0)
    column = lax.broadcasted_iota(jnp.int32, (model, width), 1)
    for s in range(SEQ):
        start = ids[8 + s] * width
        mine = w_out[at(start, width, 64), :]
        grad_outs[s][0:rows, 0:width] = dot_nt(grad_branch, mine).astype(BF16)
        grad_outs[s][rows : rows + PAD, :] = stats_rows
        chosen = (row == start + column).astype(F32).astype(BF16)
        grad_outs[s][0:rows, width:] = dot(grad_branch, chosen).astype(BF16)
    sums_ref[0:1, :] = column_sum(grad * normalized)
    sums_ref[1:2, :] = column_sum(grad)
    sums_ref[2:4, :] = sums_in[0:2, :]
    sums_ref[4:PAD, :] = jnp.zeros((PAD - 4, model), F32)


def attention_back(*refs):
    grad_blocks = refs[0:4]
    q_ref, k_ref, v_ref, probs_ref, w_qkv = refs[4:9]
    outs, grad_qkv = refs[9:13], refs[13]
    grads, grad_q, grad_k, grad_v = refs[14:18]
    rows = outs[0].shape[0]
    for s in range(SEQ):
        place = slice(s * rows, (s + 1) * rows)
        grads[place, :] = grad_blocks[s][0:rows, 0 : grads.shape[1]]
    queries, keys, values = q_ref[...], k_ref[...], v_ref[...]
    width = keys.shape[1]
    heads = width // HEAD_DIM
    head_of = lax.broadcasted_iota(jnp.int32, (1, width), 1) // HEAD_DIM
    scale = 1.0 / math.sqrt(HEAD_DIM)
    for h in range(heads):
        mine = head_of == h
        head_keys = jnp.where(mine, keys, jnp.zeros_like(keys))
        for s in range(SEQ):
            place = slice(s * rows, (s + 1) * rows)
            grad_out = jnp.where(mine, grads[place, :], jnp.zeros((rows, width), BF16))
            query = jnp.where(mine, queries[place, :], jnp.zeros((rows, width), BF16))
            probs_low = probs_ref[h, place, :]
            probs = probs_low.astype(F32)
            grad_probs = dot_nt(grad_out, values)
            delta = jnp.sum(probs * grad_probs, axis=-1, keepdims=True)
            grad_scores = (probs * (grad_probs - delta)).astype(BF16)
            dq = dot(grad_scores, head_keys)
            dk = dot_tn(grad_scores, query)
            dv = dot_tn(probs_low, grad_out)
            if h == 0:
                grad_q[place, :] = dq
            else:
                grad_q[place, :] += dq
            if h == 0 and s == 0:
                grad_k[...] = dk
                grad_v[...] = dv
            else:
                grad_k[...] += dk
                grad_v[...] += dv
    low = (
        (grad_q[...] * scale).astype(BF16),
        (grad_k[...] * scale).astype(BF16),
        grad_v[...].astype(BF16),
    )
    grad_input = dot_nt(low[0], w_qkv[0]) + dot_nt(low[1], w_qkv[1]) + dot_nt(low[2], w_qkv[2])
    for s in range(SEQ):
        outs[s][...] = grad_input[s * rows : (s + 1) * rows, :].astype(outs[s].dtype)
    for part in range(3):
        grad_qkv[:, part * width : (part + 1) * width] = low[part]


def attention_weights(ids, *refs):
    grad_qkv, x_blocks, attn, columns = refs[0], refs[1:5], refs[5], refs[6:10]
    sums = refs[10]
    keep, send = refs[11:13]
    xs, grads, out_acc, acc = refs[13:17]
    rows = x_blocks[0].shape[0]
    width = grads.shape[1]
    for s in range(SEQ):
        place = slice(s * rows, (s + 1) * rows)
        xs[place, :] = x_blocks[s][...]
        grads[place, :] = columns[s][0:rows, width:]
    for t in range(SEQ):
        out_acc[at(ids[8 + t] * width, width, 64), :] = dot_tn(attn[t], grads[...])
    acc[:, 0 : 3 * width] = dot_tn(xs[...], grad_qkv[...])
    acc[:, 3 * width : 4 * width] = out_acc[...]
    shard = acc.shape[0] // INNER
    split_rows(ids, acc, keep, send, (slice(0, shard),))
    for t in range(CHIPS):
        keep[t, shard : shard + PAD, :] = sums[...]
        send[t, shard : shard + PAD, :] = sums[...].astype(BF16)


def input_final(*refs):
    grad_first, parts, stats_in, grad_blocks = refs[0], refs[1:5], refs[5], refs[6:9]
    out, means = refs[9:11]
    acc = grad_first[...] + parts[0][...]
    for s in range(1, SEQ):
        acc = acc + parts[s][...].astype(F32)
    out[...] = acc.astype(BF16)
    rows, model = out.shape
    stats = stats_in[...]
    for ref in grad_blocks:
        extra = ref[rows : rows + PAD, 0:128].astype(F32)
        stats = stats + (extra[0:8] + extra[8:16])
    means[...] = jnp.sqrt(stats * (1.0 / (SEQ * rows * model)))


def attention_final(ids, *refs):
    blocks, qkv_out, out, vectors, stage = refs[0:4], refs[4], refs[5], refs[6:10], refs[10]
    for s in range(SEQ):
        stage[ids[8 + s]] = blocks[s][...].astype(F32)
    shard, model = out.shape
    width = model // SEQ
    for pos in range(SEQ):
        for part in range(3):
            start = (part * SEQ + pos) * width
            qkv_out[:, start : start + width] = stage[pos, 0:shard, part * width : (part + 1) * width]
        out[:, pos * width : (pos + 1) * width] = stage[pos, 0:shard, 3 * width : 4 * width]
    sums = stage[0, shard : shard + 8, :]
    for pos in range(1, SEQ):
        sums = sums + stage[pos, shard : shard + 8, :]
    shift = model - ids[0] * shard
    moved = pltpu.roll(sums, lax.rem(shift, model), 1)
    for n in range(4):
        vectors[n][...] = moved[n : n + 1, 0:shard]


def after(values, *deps):
    return lax.optimization_barrier((values, deps))[0]


def body(
    layer_input,
    w_qkv,
    w_out,
    ln1_gain,
    ln1_bias,
    w_gate_up,
    w_down,
    ln2_gain,
    ln2_bias,
    doc_starts,
    cotangent,
):
    dp = lax.axis_size("dp")
    stride = dp // INNER
    rows, model = layer_input.shape[1:]
    columns = tuple(tuple(range(g * stride, (g + 1) * stride)) for g in range(INNER))
    cores = tuple(
        tuple((2 * t + core) * stride + r for t in range(CHIPS))
        for core in range(2)
        for r in range(stride)
    )

    def gather_outer(value):
        if stride == 1:
            return value
        return lax.all_gather(value, "dp", axis=0, tiled=True, axis_index_groups=columns)

    def scatter_outer(value):
        if stride == 1:
            return value
        return lax.psum_scatter(
            value, "dp", scatter_dimension=0, tiled=True, axis_index_groups=columns
        )

    def swap(value, s):
        return lax.ppermute(value, "dp", [(i, i ^ (s * stride)) for i in range(dp)])

    def pass_seq(value, s):
        return lax.ppermute(value, "seq", [(i, i ^ s) for i in range(SEQ)])

    def gather_seq(value):
        far = pass_seq(value, 2)
        near = pass_seq(value, 1)
        return [value, near, far, pass_seq(far, 1)]

    def reduce_seq(pieces):
        return [pieces[0]] + [pass_seq(pieces[s], s) for s in range(1, SEQ)]

    j = lax.axis_index("dp") // stride
    z = lax.axis_index("seq")
    ids = jnp.concatenate(
        [
            jnp.bitwise_xor(j, jnp.arange(INNER, dtype=jnp.int32)),
            jnp.bitwise_xor(z, jnp.arange(SEQ, dtype=jnp.int32)),
        ]
    )
    slopes = jnp.asarray(SLOPES)

    w_qkv, w_out, w_gate_up, w_down = map(gather_outer, (w_qkv, w_out, w_gate_up, w_down))
    vectors = [gather_outer(v) for v in (ln1_gain, ln1_bias, ln2_gain, ln2_bias)]
    shard = w_out.shape[0]
    head_width = HEADS // SEQ * HEAD_DIM

    x_own = layer_input[0]
    x_blocks = gather_seq(x_own)

    own_qkv = jnp.concatenate(
        [
            lax.dynamic_slice(w_qkv, (0, part * model + z * head_width), (shard, head_width))
            for part in range(3)
        ],
        axis=1,
    )
    qkv_even = [own_qkv] + [swap(own_qkv, s) for s in (2, 4, 6)]
    qkv_odd = swap(jnp.concatenate(qkv_even, axis=0), 1)

    params = jnp.pad(jnp.stack(vectors, axis=0), ((0, PAD - 4), (0, model - shard)))
    (piece,) = call(
        select_units,
        [((4 * shard + PAD, model), BF16)],
        [ids],
        w_gate_up,
        w_down,
        w_out,
        params,
        mib=8,
    )
    piece = after(piece, qkv_even, x_blocks[1:3])
    even_x, even_y = swap(piece, 2), swap(piece, 4)

    length = SEQ * rows
    packed, queries, keys, values, probs, qkv_full = call(
        attention_forward,
        [((length * 3 // 2, 128), BF16)]
        + [((length, head_width), BF16)] * 3
        + [((HEADS // SEQ, length, length), BF16), ((3, model, head_width), BF16)],
        [ids, doc_starts, slopes],
        *x_blocks,
        *qkv_even,
        qkv_odd,
        scratch=[((length, model), BF16), ((length, head_width), BF16)],
        mib=16,
        flops=2 * length * head_width * (3 * model + 2 * length),
    )
    packs = gather_seq(packed)
    even_x, even_y = after((even_x, even_y), packed)
    half = model // 2
    diagonal = [swap(even_x[:, :half], 4), swap(even_y[:, half:], 2)]
    feed_even = [piece, even_x, even_y, jnp.concatenate(diagonal, axis=1)]


    feed_even = after(feed_even, packs[1:3])
    feed_odd = swap(jnp.concatenate(feed_even, axis=0), 1)
    units = w_down.shape[0] // SEQ * INNER
    gate_up_full, down_full, out_full, norm_vectors = call(
        gather_weights,
        [
            ((2, model, units), BF16),
            ((units, model), BF16),
            ((model, model), BF16),
            ((8, model), F32),
        ],
        [ids],
        *feed_even,
        feed_odd,
        mib=16,
    )

    shares = [((rows, model), F32)] + [((rows, model), BF16)] * 3
    *feed_parts, first_sum, normed, stats1, attn = call(
        middle_forward,
        shares
        + [
            ((rows, model), F32),
            ((length, model), BF16),
            ((8, 128), F32),
            ((SEQ, length, head_width), BF16),
        ],
        [ids],
        *packs,
        *x_blocks,
        out_full,
        norm_vectors,
        gate_up_full,
        down_full,
        scratch=[((length, model), F32)],
        mib=16,
        flops=2 * length * model * (model + 3 * units),
    )

    output, grad_feed, grad_second, sums2, stats2 = call(
        final_norm,
        [
            ((rows, model), BF16),
            ((rows, model), BF16),
            ((rows, model), F32),
            ((8, model), F32),
            ((8, 128), F32),
        ],
        [],
        *reduce_seq(feed_parts),
        normed,
        cotangent[0],
        norm_vectors,
        stats1,
    )

    *back_parts, hidden, dgate, dup, grads = call(
        feed_back,
        shares + [((length, units), BF16)] * 3 + [((length, model), BF16)],
        [],
        normed,
        *gather_seq(grad_feed),
        gate_up_full,
        down_full,
        scratch=[((length, model), F32)],
        mib=18,
        flops=10 * length * model * units,
    )
    back_parts = reduce_seq(back_parts)

    feed_keep, feed_send = call(
        feed_weights,
        [((CHIPS, 3, shard, model), F32), ((CHIPS, 3, shard, model), BF16)],
        [ids],
        normed,
        grads,
        hidden,
        dgate,
        dup,
        scratch=[((model, model), F32)],
        mib=18,
        flops=6 * length * model * units,
    )

    def pair(keep, send):
        shape = keep.shape[1:]
        return call(pair_sum, [(shape, F32)] + [(shape, BF16)] * 3, [], keep, swap(send, 1))

    half_shape = (3, shard, model // 2)
    grad_first, *projected = call(
        project_back,
        [((rows, model), F32)]
        + [((rows + PAD, 2 * head_width), BF16)] * SEQ
        + [((PAD, model), F32)],
        [ids],
        *back_parts,
        grad_second,
        first_sum,
        norm_vectors,
        out_full,
        sums2,
        stats2,
        mib=10,
        flops=4 * rows * model * model,
    )
    grad_attn = reduce_seq(projected[0:4])
    *feed_pieces, to_x, to_y = call(
        step_one,
        [(half_shape, F32)] * 4 + [((2,) + half_shape, BF16)] * 2,
        [],
        after(feed_keep, grad_first),
        swap(feed_send, 1),
        mib=10,
    )
    left, right, to_y, to_x = call(
        step_two,
        [(half_shape, F32)] * 2 + [(half_shape, BF16)] * 2,
        [],
        *after(feed_pieces, grad_attn),
        swap(to_x, 2),
        swap(to_y, 4),
        mib=10,
    )

    sums = projected[4]
    (feed_share,) = call(
        step_three, [((3, shard, model), BF16)], [], left, right, swap(to_y, 4), swap(to_x, 2)
    )
    sums = after(sums, feed_share)
    feed_blocks = gather_seq(after(feed_share, grad_attn))

    *input_parts, grad_qkv = call(
        attention_back,
        shares + [((length, 3 * head_width), BF16)],
        [],
        *grad_attn,
        queries,
        keys,
        values,
        probs,
        qkv_full,
        scratch=[((length, head_width), BF16)] + [((length, head_width), F32)] * 3,
        mib=16,
        flops=2 * length * head_width * (3 * model + 5 * length),
    )
    input_parts = reduce_seq(input_parts)


    attn_keep, attn_send = call(
        attention_weights,
        [
            ((CHIPS, shard + PAD, model), F32),
            ((CHIPS, shard + PAD, model), BF16),
        ],
        [ids],
        grad_qkv,
        *x_blocks,
        attn,
        *grad_attn,
        sums,
        scratch=[
            ((length, model), BF16),
            ((length, head_width), BF16),
            ((model, head_width), F32),
            ((model, model), F32),
        ],
        mib=16,
        flops=2 * length * model * model,
    )

    grad_gate_up_w, grad_down_w = call(
        feed_final,
        [(w_gate_up.shape, F32), (w_down.shape, F32)],
        [ids],
        *feed_blocks,
        mib=10,
    )
    attn_pieces = pair(attn_keep, attn_send)
    attn_pieces = [attn_pieces[0]] + [swap(attn_pieces[t], 2 * t) for t in range(1, CHIPS)]
    attn_pieces = after(attn_pieces, input_parts, feed_blocks[1:3])
    (attn_share,) = call(plane_sum, [((shard + PAD, model), BF16)], [], *attn_pieces)
    input_grad, means = call(
        input_final,
        [((rows, model), BF16), ((8, 128), F32)],
        [],
        grad_first,
        *input_parts,
        stats2,
        *grad_attn[1:],
    )
    attn_near = pass_seq(attn_share, 1)
    attn_far = after(pass_seq(attn_share, 2), grad_gate_up_w, input_grad)
    grad_qkv_w, grad_out_w, *vector_grads = call(
        attention_final,
        [((shard, 3 * model), F32), ((shard, model), F32)] + [((1, shard), F32)] * 4,
        [ids],
        attn_share,
        attn_near,
        attn_far,
        pass_seq(attn_far, 1),
        scratch=[((SEQ, shard + PAD, model), F32)],
    )

    vector_grads = [scatter_outer(vector_grads[n].reshape(shard)) for n in range(4)]
    return (
        output[None],
        input_grad[None],
        scatter_outer(grad_qkv_w),
        scatter_outer(grad_out_w),
        vector_grads[0],
        vector_grads[1],
        scatter_outer(grad_gate_up_w),
        scatter_outer(grad_down_w),
        vector_grads[2],
        vector_grads[3],
        means[0:1, 0:4],
    )


def solution(mesh):
    return jax.shard_map(
        body,
        mesh=mesh,
        in_specs=(
            P("dp", "seq", None),
            P("dp", None),
            P("dp", None),
            P("dp"),
            P("dp"),
            P("dp", None),
            P("dp", None),
            P("dp"),
            P("dp"),
            P("dp", None),
            P("dp", "seq", None),
        ),
        out_specs=(
            P("dp", "seq", None),
            P("dp", "seq", None),
            P("dp", None),
            P("dp", None),
            P("dp"),
            P("dp"),
            P("dp", None),
            P("dp", None),
            P("dp"),
            P("dp"),
            P("dp", None),
        ),
        check_vma=False,
    )
```
